32 devices in a mesh: rep: 8 (over y, x, core), shard: 4 (over z).
Axes of the slice: x: 2, y: 2, z: 4, core: 2. Of those that a mesh axis runs over, the one named last changes fastest.
Arguments:
- inputs: bfloat16 [2, 1024, 4, 1024], P(None, 'rep', 'shard'), may hold values from -6 to 6
- early_gain: bfloat16 [1024], P('shard'), may hold values from 0.5 to 1.5
- early_shift: bfloat16 [1024], P('shard'), may hold values from -2 to 2
- early_widen: bfloat16 [1024, 4096], P('shard'), may hold values from -0.1875 to 0.1875
- early_offset: bfloat16 [4096], P('shard'), may hold values from -2 to 2
- early_narrow: bfloat16 [4096, 1024], P('shard'), may hold values from -0.1875 to 0.1875
- early_bias: bfloat16 [1024], P('shard'), may hold values from -2 to 2
- attend_gain: bfloat16 [1024], P('shard'), may hold values from 0.5 to 1.5
- attend_shift: bfloat16 [1024], P('shard'), may hold values from -2 to 2
- query_weight: bfloat16 [1024, 1024], P('shard'), may hold values from -0.25 to 0.25
- query_bias: bfloat16 [1024], P('shard'), may hold values from -2 to 2
- key_weight: bfloat16 [1024, 1024], P('shard'), may hold values from -0.25 to 0.25
- value_weight: bfloat16 [1024, 1024], P('shard'), may hold values from -0.1875 to 0.1875
- value_bias: bfloat16 [1024], P('shard'), may hold values from -2 to 2
- mixer_weight: bfloat16 [1024, 1024], P('shard'), may hold values from -0.75 to 0.75
- mixer_bias: bfloat16 [1024], P('shard'), may hold values from -2 to 2
- distance_table: bfloat16 [73, 64], P(None, 'shard'), may hold values from -3 to 3
- conv_gain: bfloat16 [1024], P('shard'), may hold values from 0.5 to 1.5
- conv_shift: bfloat16 [1024], P('shard'), may hold values from -2 to 2
- gated_weight: bfloat16 [1024, 2048], P('shard'), may hold values from -0.1875 to 0.1875
- depth_kernel: bfloat16 [31, 1024], P(None, 'shard'), may hold values from -1 to 1
- depth_gain: bfloat16 [1024], P('shard'), may hold values from 0.5 to 1.5
- depth_shift: bfloat16 [1024], P('shard'), may hold values from -2 to 2
- pointwise_weight: bfloat16 [1024, 1024], P('shard'), may hold values from -0.1875 to 0.1875
- later_gain: bfloat16 [1024], P('shard'), may hold values from 0.5 to 1.5
- later_shift: bfloat16 [1024], P('shard'), may hold values from -2 to 2
- later_widen: bfloat16 [1024, 4096], P('shard'), may hold values from -0.1875 to 0.1875
- later_offset: bfloat16 [4096], P('shard'), may hold values from -2 to 2
- later_narrow: bfloat16 [4096, 1024], P('shard'), may hold values from -0.1875 to 0.1875
- later_bias: bfloat16 [1024], P('shard'), may hold values from -2 to 2
- final_gain: bfloat16 [1024], P('shard'), may hold values from 0.5 to 1.5
- final_shift: bfloat16 [1024], P('shard'), may hold values from -2 to 2
- cotangent: bfloat16 [2, 1024, 4, 1024], P(None, 'rep', 'shard'), may hold values from -6 to 6
Outputs:
- output: bfloat16 [2, 1024, 4, 1024], P(None, 'rep', 'shard')
- input_grad: float32 [2, 1024, 4, 1024], P(None, 'rep', 'shard')
- grad_early_gain: float32 [1024], P('shard')
- grad_early_shift: float32 [1024], P('shard')
- grad_early_widen: float32 [1024, 4096], P('shard')
- grad_early_offset: float32 [4096], P('shard')
- grad_early_narrow: float32 [4096, 1024], P('shard')
- grad_early_bias: float32 [1024], P('shard')
- grad_attend_gain: float32 [1024], P('shard')
- grad_attend_shift: float32 [1024], P('shard')
- grad_query_weight: float32 [1024, 1024], P('shard')
- grad_query_bias: float32 [1024], P('shard')
- grad_key_weight: float32 [1024, 1024], P('shard')
- grad_value_weight: float32 [1024, 1024], P('shard')
- grad_value_bias: float32 [1024], P('shard')
- grad_mixer_weight: float32 [1024, 1024], P('shard')
- grad_mixer_bias: float32 [1024], P('shard')
- grad_distance_table: float32 [73, 64], P(None, 'shard')
- grad_conv_gain: float32 [1024], P('shard')
- grad_conv_shift: float32 [1024], P('shard')
- grad_gated_weight: float32 [1024, 2048], P('shard')
- grad_depth_kernel: float32 [31, 1024], P(None, 'shard')
- grad_depth_gain: float32 [1024], P('shard')
- grad_depth_shift: float32 [1024], P('shard')
- grad_pointwise_weight: float32 [1024, 1024], P('shard')
- grad_later_gain: float32 [1024], P('shard')
- grad_later_shift: float32 [1024], P('shard')
- grad_later_widen: float32 [1024, 4096], P('shard')
- grad_later_offset: float32 [4096], P('shard')
- grad_later_narrow: float32 [4096, 1024], P('shard')
- grad_later_bias: float32 [1024], P('shard')
- grad_final_gain: float32 [1024], P('shard')
- grad_final_shift: float32 [1024], P('shard')
The draws below stay inside these ranges and needn't reach their ends.
All inputs are finite; a program needn't handle non-finite values.
Results may differ from the reference program's by a relative error of at most 0.025.
Values may be sent and summed in bfloat16 or wider, within the bound.
A program may use at most 320 MiB of HBM per device.

```python
import jax
import jax.numpy as jnp
from jax import lax

D = 1024
H = 16
HD = 64
FF = 4096
KERNEL = 31
LEFT = 64
RIGHT = 8
TABLE = 73
MB = 2
SEQS = 4
LENGTH = 1024


def shard_levels(key, dims, split, low, top_value):
    def one(axis_at, shards_of):
        steps = jax.random.uniform(jax.random.fold_in(jax.random.fold_in(key, 6), axis_at), (shards_of,), jnp.float32, low / len(split), top_value / len(split))
        return jnp.repeat(jnp.exp(steps), dims[axis_at] // shards_of).reshape((-1,) + (1,) * (len(dims) - axis_at - 1))

    loudness = one(*split[0])
    for cut in split[1:]:
        loudness = loudness * one(*cut)
    return loudness


def gaussian(rng, shape, scale, reach, pieces=(), kind=jnp.bfloat16):
    level = shard_levels(rng, shape, pieces, -0.22, 0.18) if pieces else 1.0
    drawn = jax.random.normal(rng, shape, jnp.float32) * scale * level
    return jnp.minimum(jnp.maximum(drawn, -reach), reach).astype(kind)


def setup_inputs(seed: int = 0) -> dict:
    seeds = jax.random.split(jax.random.key(seed), 34)
    inputs = gaussian(seeds[0], (MB, LENGTH, SEQS, D), 1.0, 6.0, ((1, 8), (2, 4)))
    early_gain = jnp.clip(1.0 + 0.1 * jax.random.normal(seeds[1], (D,), jnp.float32), 0.5, 1.5).astype(jnp.bfloat16)
    early_shift = gaussian(seeds[2], (D,), 0.3, 2.0, ((0, 4),))
    early_widen = gaussian(seeds[3], (D, FF), D ** -0.5, 0.1875, ((0, 4),))
    early_offset = gaussian(seeds[4], (FF,), 0.3, 2.0, ((0, 4),))
    early_narrow = gaussian(seeds[5], (FF, D), (FF // 4) ** -0.5, 0.1875, ((0, 4),))
    early_bias = gaussian(seeds[6], (D,), 0.3, 2.0, ((0, 4),))
    attend_gain = jnp.clip(1.0 + 0.1 * jax.random.normal(seeds[7], (D,), jnp.float32), 0.5, 1.5).astype(jnp.bfloat16)
    attend_shift = gaussian(seeds[8], (D,), 0.3, 2.0, ((0, 4),))
    query_weight = gaussian(seeds[9], (D, D), (D // 2) ** -0.5, 0.25, ((0, 4),))
    query_bias = gaussian(seeds[10], (D,), 0.3, 2.0, ((0, 4),))
    key_weight = gaussian(seeds[11], (D, D), (D // 2) ** -0.5, 0.25, ((0, 4),))
    value_weight = gaussian(seeds[12], (D, D), D ** -0.5, 0.1875, ((0, 4),))
    value_bias = gaussian(seeds[13], (D,), 0.3, 2.0, ((0, 4),))
    mixer_weight = gaussian(seeds[14], (D, D), HD ** -0.5, 0.75, ((0, 4),))
    mixer_bias = gaussian(seeds[15], (D,), 0.3, 2.0, ((0, 4),))
    distance_table = gaussian(seeds[16], (TABLE, HD), 0.5, 3.0, ((1, 4),))
    conv_gain = jnp.clip(1.0 + 0.1 * jax.random.normal(seeds[17], (D,), jnp.float32), 0.5, 1.5).astype(jnp.bfloat16)
    conv_shift = gaussian(seeds[18], (D,), 0.3, 2.0, ((0, 4),))
    gated_weight = gaussian(seeds[19], (D, 2 * D), D ** -0.5, 0.1875, ((0, 4),))
    depth_kernel = gaussian(seeds[20], (KERNEL, D), KERNEL ** -0.5, 1.0, ((1, 4),))
    depth_gain = jnp.clip(1.0 + 0.1 * jax.random.normal(seeds[21], (D,), jnp.float32), 0.5, 1.5).astype(jnp.bfloat16)
    depth_shift = gaussian(seeds[22], (D,), 0.3, 2.0, ((0, 4),))
    pointwise_weight = gaussian(seeds[23], (D, D), D ** -0.5, 0.1875, ((0, 4),))
    later_gain = jnp.clip(1.0 + 0.1 * jax.random.normal(seeds[24], (D,), jnp.float32), 0.5, 1.5).astype(jnp.bfloat16)
    later_shift = gaussian(seeds[25], (D,), 0.3, 2.0, ((0, 4),))
    later_widen = gaussian(seeds[26], (D, FF), D ** -0.5, 0.1875, ((0, 4),))
    later_offset = gaussian(seeds[27], (FF,), 0.3, 2.0, ((0, 4),))
    later_narrow = gaussian(seeds[28], (FF, D), (FF // 4) ** -0.5, 0.1875, ((0, 4),))
    later_bias = gaussian(seeds[29], (D,), 0.3, 2.0, ((0, 4),))
    final_gain = jnp.clip(1.0 + 0.1 * jax.random.normal(seeds[30], (D,), jnp.float32), 0.5, 1.5).astype(jnp.bfloat16)
    final_shift = gaussian(seeds[31], (D,), 0.3, 2.0, ((0, 4),))
    cotangent = gaussian(seeds[32], (MB, LENGTH, SEQS, D), 1.0, 6.0, ((1, 8), (2, 4)))
    return dict(inputs=inputs, early_gain=early_gain, early_shift=early_shift, early_widen=early_widen, early_offset=early_offset, early_narrow=early_narrow, early_bias=early_bias, attend_gain=attend_gain, attend_shift=attend_shift, query_weight=query_weight, query_bias=query_bias, key_weight=key_weight, value_weight=value_weight, value_bias=value_bias, mixer_weight=mixer_weight, mixer_bias=mixer_bias, distance_table=distance_table, conv_gain=conv_gain, conv_shift=conv_shift, gated_weight=gated_weight, depth_kernel=depth_kernel, depth_gain=depth_gain, depth_shift=depth_shift, pointwise_weight=pointwise_weight, later_gain=later_gain, later_shift=later_shift, later_widen=later_widen, later_offset=later_offset, later_narrow=later_narrow, later_bias=later_bias, final_gain=final_gain, final_shift=final_shift, cotangent=cotangent)


@jax.custom_vjp
def low(v):
    return lax.optimization_barrier(v.astype(jnp.bfloat16)).astype(jnp.float32)

@jax.custom_vjp
def low_back(v):
    return v

def low_keep(v):
    return (low(v), None)

def low_pass(kept, grad):
    return (grad,)

def back_keep(v):
    return (v, None)

def back_low(kept, grad):
    return (low(grad),)
low.defvjp(low_keep, low_pass)
low_back.defvjp(back_keep, back_low)

def norm_rows(values, scale_row, offset_row):
    centre = lax.optimization_barrier(jnp.mean(values, axis=-1, keepdims=True))
    centred = values - centre
    spread = lax.optimization_barrier(jnp.mean(centred * centred, axis=-1, keepdims=True))
    return centred * lax.rsqrt(spread + 1e-05) * scale_row + offset_row

def matmul_high(left_side, right_side):
    return jnp.dot(left_side, right_side, precision=lax.Precision.HIGHEST)

def swish_value(values):
    return values * jax.nn.sigmoid(values)

def feed_forward(weights, entering):
    normed = low(norm_rows(entering, weights[0], weights[1]))
    inner_act = low_back(matmul_high(normed, weights[2]) + weights[3])
    return low_back(matmul_high(low(swish_value(inner_act)), weights[4]) + weights[5])

def self_attention(weights, entering):
    length = entering.shape[0]
    normed = low(norm_rows(entering, weights[0], weights[1]))
    query_rows = low(low_back(matmul_high(normed, weights[2]) + weights[3])).reshape(length, H, HD)
    key_rows = low(low_back(matmul_high(normed, weights[4]))).reshape(length, H, HD)
    values = low(low_back(matmul_high(normed, weights[5]) + weights[6])).reshape(length, H, HD)
    offsets = low(low_back(jnp.einsum('lhd,rd->lhr', query_rows, weights[9], precision=lax.Precision.HIGHEST)))
    block_rows = min(512, length)
    blocks = length // block_rows
    query_blocks = query_rows.reshape(blocks, block_rows, H, HD)
    offset_blocks = offsets.reshape(blocks, block_rows, H, TABLE)
    starts = jnp.arange(blocks, dtype=jnp.int32) * block_rows
    key_places = jnp.arange(length, dtype=jnp.int32)

    def one_block(members):
        query_part, offset_part, block_first = members
        query_places = block_first + jnp.arange(block_rows, dtype=jnp.int32)
        lookup = jnp.clip(key_places[None, :] - query_places[:, None], -LEFT, RIGHT) + LEFT
        lookup = jnp.broadcast_to(lookup[None], (H, block_rows, length)).astype(jnp.int32)
        placed = jnp.take_along_axis(jnp.transpose(offset_part, (1, 0, 2)), lookup, axis=2)
        raw_scores = jnp.einsum('qhd,khd->hqk', query_part, key_rows, precision=lax.Precision.HIGHEST)
        scores = low_back((raw_scores + placed) * 0.125)
        probability = low(jnp.exp(scores - jax.nn.logsumexp(scores, axis=-1, keepdims=True)))
        return jnp.einsum('hqk,khd->qhd', probability, values, precision=lax.Precision.HIGHEST)
    mixed_heads = lax.map(jax.checkpoint(one_block), (query_blocks, offset_blocks, starts))
    mixed_heads = low(low_back(mixed_heads.reshape(length, D)))
    return low_back(matmul_high(mixed_heads, weights[7]) + weights[8])

def convolution(weights, entering):
    length = entering.shape[0]
    normed = low(norm_rows(entering, weights[0], weights[1]))
    doubled = low_back(matmul_high(normed, weights[2]))
    gated_rows = doubled[:, :D] * jax.nn.sigmoid(doubled[:, D:])
    padded = jnp.concatenate([jnp.zeros((KERNEL - 1, D), jnp.float32), gated_rows], axis=0)
    depth_rows = padded[0:length] * weights[3][0]
    for tap_index in range(1, KERNEL):
        depth_rows = depth_rows + padded[tap_index:tap_index + length] * weights[3][tap_index]
    acted_rows = swish_value(norm_rows(depth_rows, weights[4], weights[5]))
    return low_back(matmul_high(low(acted_rows), weights[6]))

def layer_whole(weights, entering):
    level_one = entering + 0.5 * feed_forward(weights[0:6], entering)
    level_two = level_one + self_attention(weights[6:16], level_one)
    level_three = level_two + convolution(weights[16:23], level_two)
    level_four = level_three + 0.5 * feed_forward(weights[23:29], level_three)
    return norm_rows(level_four, weights[29], weights[30])

def reference(inputs, early_gain, early_shift, early_widen, early_offset, early_narrow, early_bias, attend_gain, attend_shift, query_weight, query_bias, key_weight, value_weight, value_bias, mixer_weight, mixer_bias, distance_table, conv_gain, conv_shift, gated_weight, depth_kernel, depth_gain, depth_shift, pointwise_weight, later_gain, later_shift, later_widen, later_offset, later_narrow, later_bias, final_gain, final_shift, cotangent):
    weights = [member.astype(jnp.float32) for member in (early_gain, early_shift, early_widen, early_offset, early_narrow, early_bias, attend_gain, attend_shift, query_weight, query_bias, key_weight, value_weight, value_bias, mixer_weight, mixer_bias, distance_table, conv_gain, conv_shift, gated_weight, depth_kernel, depth_gain, depth_shift, pointwise_weight, later_gain, later_shift, later_widen, later_offset, later_narrow, later_bias, final_gain, final_shift)]
    sequences = jnp.transpose(inputs.astype(jnp.float32), (0, 2, 1, 3)).reshape(MB * SEQS, LENGTH, D)
    cotangents = jnp.transpose(cotangent.astype(jnp.float32), (0, 2, 1, 3)).reshape(MB * SEQS, LENGTH, D)

    def one_sequence(totals, members):
        sequence, incoming = members
        result, pull = jax.vjp(layer_whole, weights, sequence)
        grads, sequence_grad = pull(incoming)
        return (jax.tree.map(jnp.add, totals, grads), (result, sequence_grad))
    zeroed = [jnp.zeros_like(member) for member in weights]
    totals, (results, sequence_grads) = lax.scan(one_sequence, zeroed, (sequences, cotangents))
    output = jnp.transpose(results.reshape(MB, SEQS, LENGTH, D), (0, 2, 1, 3)).astype(jnp.bfloat16)
    input_grad = jnp.transpose(sequence_grads.reshape(MB, SEQS, LENGTH, D), (0, 2, 1, 3))
    return (output, input_grad, totals[0], totals[1], totals[2], totals[3], totals[4], totals[5], totals[6], totals[7], totals[8], totals[9], totals[10], totals[11], totals[12], totals[13], totals[14], totals[15], totals[16], totals[17], totals[18], totals[19], totals[20], totals[21], totals[22], totals[23], totals[24], totals[25], totals[26], totals[27], totals[28], totals[29], totals[30])
```

```python
import functools

import jax
import jax.numpy as jnp
from jax import lax
from jax.experimental import pallas as pl
from jax.experimental.pallas import tpu as pltpu
from jax.sharding import PartitionSpec as P

H = 16
HD = 64
LEFT = 64
RIGHT = 8
TABLE = 73
EPSILON = 1e-05
BAND = 512
MESH = pl.DeviceIdType.MESH
BF = jnp.bfloat16
F32 = jnp.float32
ANY = pl.BlockSpec(memory_space=pl.ANY)
VM = pl.BlockSpec(memory_space=pltpu.VMEM)


def here():
    rep = lax.axis_index("rep")
    z = lax.axis_index("shard")
    core = lax.rem(rep, 2)
    x = lax.rem(rep // 2, 2)
    y = rep // 4
    z0 = lax.rem(z, 2)
    z1 = z // 2
    peers = {
        "z1": (rep, lax.rem(z + 2, 4)),
        "z0": (rep, z + 1 - 2 * z0),
        "zz": (rep, 3 - z),
        "x": (rep + 2 - 4 * x, z),
        "y": (rep + 4 - 8 * y, z),
        "c": (rep + 1 - 2 * core, z),
    }
    return z, core, x, y, z0, z1, peers


def meet(peers):
    barrier = pltpu.get_barrier_semaphore()
    for name in peers:
        pl.semaphore_signal(barrier, inc=1, device_id=peers[name], device_id_type=MESH)
    pl.semaphore_wait(barrier, len(peers))


GATHER_LAG = (0, 2, 3, 4, 5)


def gather_kernel(chunks, n_arr, *refs):
    ins, small = (refs[:n_arr], refs[n_arr])
    outs, small_out = (refs[n_arr + 1 : 2 * n_arr + 1], refs[2 * n_arr + 1])
    ssem, rsem, lsem, lsem2, qsem, psem = refs[2 * n_arr + 2 : 2 * n_arr + 8]
    bufs = refs[2 * n_arr + 8 :]
    z, core, x, y, z0, z1, peers = here()
    far = ((slice(None), 1 - z0), (1 - z1, z0))
    meet(peers)
    sent = []

    def send(c, slot, src, dst, to):
        copy = pltpu.make_async_remote_copy(
            src_ref=src,
            dst_ref=dst,
            send_sem=ssem.at[c, slot],
            recv_sem=rsem.at[c, slot],
            device_id=peers[to],
            device_id_type=MESH,
        )
        copy.start()
        sent.append(copy)
        return copy

    smalls = []
    for k, to in enumerate(("z0", "z1", "zz")):
        copy = pltpu.make_async_remote_copy(
            src_ref=small,
            dst_ref=small_out.at[z],
            send_sem=qsem.at[k],
            recv_sem=psem.at[k],
            device_id=peers[to],
            device_id_type=MESH,
        )
        copy.start()
        smalls.append(copy)
    small_own = pltpu.make_async_copy(small, small_out.at[z], lsem.at[n_arr])
    small_own.start()
    state = {}

    def place(c):
        array, first, count = chunks[c]
        return (ins[array], outs[array], pl.ds(first, count))

    def wait(c, key):
        for copy in state[c, key]:
            copy.wait_recv()

    def stage_z(c):
        src, out, cols = place(c)
        src = src.at[y, x, core, :, :, cols]
        dst = out.at[z1, z0, y, x, core, :, :, cols]
        state[c, "z1"] = [send(c, 0, src, dst, "z1")]
        state[c, "z0"] = [send(c, 1, src, dst, "z0")]

    def stage_zz(c):
        _, out, cols = place(c)
        wait(c, "z1")
        view = out.at[1 - z1, z0, y, x, core, :, :, cols]
        state[c, "z0"].append(send(c, 2, view, view, "z0"))

    def stage_one(c):
        _, out, cols = place(c)
        wait(c, "z0")
        state[c, "one"] = []
        for i, (a, b) in enumerate(far):
            view = out.at[a, b, y, x, core, 0, :, cols]
            state[c, "one"].append(send(c, 3 + i, view, view, "x"))
            view = out.at[a, b, y, x, core, 1, :, cols]
            state[c, "one"].append(send(c, 5 + i, view, view, "y"))

    def stage_two(c):
        _, out, cols = place(c)
        wait(c, "one")
        state[c, "two"] = []
        for i, (a, b) in enumerate(far):
            view = out.at[a, b, y, :, core, 0, :, cols]
            state[c, "two"].append(send(c, 7 + i, view, view, "y"))
            view = out.at[a, b, :, x, core, 1, :, cols]
            state[c, "two"].append(send(c, 9 + i, view, view, "x"))

    def stage_core(c):
        _, out, cols = place(c)
        wait(c, "two")
        state[c, "core"] = []
        for i, (a, b) in enumerate(far):
            view = out.at[a, b, :, :, core, :, :, cols]
            state[c, "core"].append(send(c, 11 + i, view, view, "c"))

    stages = (stage_z, stage_zz, stage_one, stage_two, stage_core)
    local = []
    for step in range(len(chunks) + GATHER_LAG[-1]):
        for stage, lag in zip(stages, GATHER_LAG):
            if 0 <= step - lag < len(chunks):
                stage(step - lag)
        if step == 0:
            for a in range(n_arr):
                copy = pltpu.make_async_copy(ins[a], bufs[a], lsem.at[a])
                copy.start()
                local.append(copy)
        if step == 3:
            for a in range(n_arr):
                local[a].wait()
                copy = pltpu.make_async_copy(bufs[a], outs[a].at[z1, z0], lsem2.at[a])
                copy.start()
                local[a] = copy
    for c in range(len(chunks)):
        wait(c, "core")
    for copy in sent + smalls:
        copy.wait_send()
    for copy in smalls:
        copy.wait_recv()
    small_own.wait()
    for copy in local:
        copy.wait()


def gather_chunks(shapes):
    chunks = []
    for i, (rows, cols) in enumerate(shapes):
        for first in range(0, cols, 1024 * 256 // rows):
            chunks.append((i, first, 1024 * 256 // rows))
    return chunks


def gather_fast(shards, small):
    count = len(shards)
    ins = [w.reshape(2, 2, 2, 2, w.shape[0] // 16, w.shape[1]) for w in shards]
    chunks = gather_chunks([w.shape for w in shards])
    outs = [jax.ShapeDtypeStruct((2, 2) + w.shape, w.dtype) for w in ins]
    outs.append(jax.ShapeDtypeStruct((4,) + small.shape, small.dtype))
    dma = pltpu.SemaphoreType.DMA
    found = pl.pallas_call(
        functools.partial(gather_kernel, chunks, count),
        out_shape=outs,
        in_specs=[ANY] * (count + 1),
        out_specs=[ANY] * (count + 1),
        scratch_shapes=[
            dma((len(chunks), 13)),
            dma((len(chunks), 13)),
            dma((count + 1,)),
            dma((count,)),
            dma((3,)),
            dma((3,)),
        ]
        + [pltpu.VMEM(w.shape, w.dtype) for w in ins],
        compiler_params=pltpu.CompilerParams(
            collective_id=0, has_side_effects=True, vmem_limit_bytes=32 << 20
        ),
        name="gather_weights",
    )(*ins, small)
    return [w.reshape(-1, w.shape[-1]) for w in found[:count]], found[count]


REDUCE_LAG = (0, 1, 2, 3, 4, 5, 6, 7)


def reduce_kernel(groups, units, n_left, n_right, *refs):
    lefts, rights = (refs[:n_left], refs[n_left : n_left + n_right])
    out = refs[n_left + n_right]
    lbuf, rbuf, sbuf, b1, b2, b3, b4, b5, lsem, ssem, rsem, osem = refs[n_left + n_right + 1 :]
    z, core, x, y, z0, z1, peers = here()
    del peers["zz"]
    meet(peers)

    def remote(u, slot, src, dst, to):
        return pltpu.make_async_remote_copy(
            src_ref=src,
            dst_ref=dst,
            send_sem=ssem.at[u, slot],
            recv_sem=rsem.at[u, slot],
            device_id=peers[to],
            device_id_type=MESH,
        )

    def copy_core(u):
        return [remote(u, 0, sbuf.at[lax.rem(u, 2)], b1.at[u], "c")]

    def copy_first(u):
        return [
            remote(u, 1, b1.at[u, :, :, 0, 1 - x], b2.at[u, 0], "x"),
            remote(u, 2, b1.at[u, :, :, 1, 1 - y], b2.at[u, 1], "y"),
        ]

    def copy_z0(u):
        return [remote(u, 3, b2.at[u, :, :, 1 - z0], b3.at[u], "z0")]

    def copy_z1(u):
        return [remote(u, 4, b3.at[u, :, 1 - z1], b4.at[u], "z1")]

    def copy_second(u):
        return [
            remote(u, 5, b4.at[u, 0, 1 - y], b5.at[u, 0], "y"),
            remote(u, 6, b4.at[u, 1, 1 - x], b5.at[u, 1], "x"),
        ]

    def copy_own(u):
        return [
            pltpu.make_async_copy(b5.at[u, 0], out.at[u, core, 0, x, y], osem.at[u, 0]),
            pltpu.make_async_copy(b5.at[u, 1], out.at[u, core, 1, y, x], osem.at[u, 1]),
        ]

    def spread_second(u):
        return [
            remote(u, 7, b5.at[u, 0], out.at[u, core, 0, x, y], "y"),
            remote(u, 8, b5.at[u, 1], out.at[u, core, 1, y, x], "x"),
        ]

    def spread_first(u):
        return [
            remote(u, 9, out.at[u, core, 0, x], out.at[u, core, 0, x], "x"),
            remote(u, 10, out.at[u, core, 1, y], out.at[u, core, 1, y], "y"),
        ]

    def spread_core(u):
        return [remote(u, 11, out.at[u, core], out.at[u, core], "c")]

    def start(copies):
        for copy in copies:
            copy.start()

    def arrive(copies):
        for copy in copies:
            copy.wait_recv()

    def load(u):
        slot = lax.rem(u, 3)
        for li, ri, first, count, by_rows in groups:

            @pl.when(jnp.logical_and(u >= first, u < first + count))
            def _():
                k = u - first
                for part in range(4):
                    at = pl.multiple_of(part * 1024 + k * 256, 256) if by_rows else part * 256
                    pltpu.make_async_copy(
                        lefts[li].at[:, pl.ds(at, 256)], lbuf.at[slot, part], lsem.at[slot, part]
                    ).start()
                at = 0 if by_rows else pl.multiple_of(k * 1024, 1024)
                pltpu.make_async_copy(
                    rights[ri].at[:, pl.ds(at, 1024)], rbuf.at[slot], lsem.at[slot, 4]
                ).start()

    def product(u, part, half):
        slot = lax.rem(u, 3)
        left = lbuf[slot, part, :, pl.ds(pl.multiple_of(half * 128, 128), 128)]
        return lax.dot_general(
            left, rbuf[slot], (((0,), (0,)), ((), ())), preferred_element_type=F32
        ).reshape(2, 2, 2, 16, 1024)

    load(0)
    load(1)

    def stage_multiply(u):
        slot = lax.rem(u, 3)
        for part in range(4):
            pltpu.make_async_copy(
                lefts[0].at[:, pl.ds(0, 256)], lbuf.at[slot, part], lsem.at[slot, part]
            ).wait()
        pltpu.make_async_copy(
            rights[0].at[:, pl.ds(0, 1024)], rbuf.at[slot], lsem.at[slot, 4]
        ).wait()

        @pl.when(u >= 2)
        def _():
            for copy in copy_core(u - 2):
                copy.wait_send()

        def body(part, carry):
            sbuf[lax.rem(u, 2), part // 2, lax.rem(part, 2)] = product(u, part, 1 - core).astype(BF)
            return carry

        lax.fori_loop(0, 4, body, 0)
        start(copy_core(u))

    def stage_own(u):
        arrive(copy_core(u))

        def body(part, carry):
            a, b = (part // 2, lax.rem(part, 2))
            b1[u, a, b] = (product(u, part, core) + b1[u, a, b].astype(F32)).astype(BF)
            return carry

        lax.fori_loop(0, 4, body, 0)
        start(copy_first(u))

        @pl.when(u + 2 < units)
        def _():
            load(u + 2)

    def stage_first(u):
        arrive(copy_first(u))

        def body(part, carry):
            a, b = (part // 2, lax.rem(part, 2))
            for half, bit in ((0, x), (1, y)):
                b2[u, half, a, b] = (
                    b2[u, half, a, b].astype(F32) + b1[u, a, b, half, bit].astype(F32)
                ).astype(BF)
            return carry

        lax.fori_loop(0, 4, body, 0)
        start(copy_z0(u))

    def stage_z0(u):
        arrive(copy_z0(u))
        for half in range(2):
            for a in range(2):
                b3[u, half, a] = (
                    b3[u, half, a].astype(F32) + b2[u, half, a, z0].astype(F32)
                ).astype(BF)
        start(copy_z1(u))

    def stage_z1(u):
        arrive(copy_z1(u))
        for half in range(2):
            b4[u, half] = (b4[u, half].astype(F32) + b3[u, half, z1].astype(F32)).astype(BF)
        start(copy_second(u))

    def stage_second(u):
        arrive(copy_second(u))
        for half, bit in ((0, y), (1, x)):
            b5[u, half] = (b5[u, half].astype(F32) + b4[u, half, bit].astype(F32)).astype(BF)
        start(copy_own(u))
        start(spread_second(u))

    def stage_spread(u):
        arrive(spread_second(u))
        for copy in copy_own(u):
            copy.wait()
        start(spread_first(u))

    def stage_core(u):
        arrive(spread_first(u))
        start(spread_core(u))

    stages = (
        stage_multiply,
        stage_own,
        stage_first,
        stage_z0,
        stage_z1,
        stage_second,
        stage_spread,
        stage_core,
    )

    def step(i, carry):
        for stage, lag in zip(stages, REDUCE_LAG):
            u = i - lag

            @pl.when(jnp.logical_and(u >= 0, u < units))
            def _():
                stage(u)

        return carry

    lax.fori_loop(0, units + REDUCE_LAG[-1], step, 0)

    def finish(u, carry):
        arrive(spread_core(u))
        for copies in (
            copy_first,
            copy_z0,
            copy_z1,
            copy_second,
            spread_second,
            spread_first,
            spread_core,
        ):
            for copy in copies(u):
                copy.wait_send()

        @pl.when(u >= units - 2)
        def _():
            for copy in copy_core(u):
                copy.wait_send()

        return carry

    lax.fori_loop(0, units, finish, 0)


def reduce_fast(pairs):
    lefts, rights, groups, units = ([], [], [], 0)

    def index_of(arrays, array):
        for i, known in enumerate(arrays):
            if known is array:
                return i
        arrays.append(array)
        return len(arrays) - 1

    for left, right in pairs:
        by_rows = left.shape[1] > 1024
        count = left.shape[1] // 1024 if by_rows else right.shape[1] // 1024
        groups.append((index_of(lefts, left), index_of(rights, right), units, count, by_rows))
        units += count
    dma = pltpu.SemaphoreType.DMA
    found = pl.pallas_call(
        functools.partial(reduce_kernel, groups, units, len(lefts), len(rights)),
        out_shape=jax.ShapeDtypeStruct((units, 2, 2, 2, 2, 16, 1024), BF),
        in_specs=[ANY] * (len(lefts) + len(rights)),
        out_specs=ANY,
        scratch_shapes=[
            pltpu.VMEM((3, 4, 256, 256), BF),
            pltpu.VMEM((3, 256, 1024), BF),
            pltpu.VMEM((2, 2, 2, 2, 2, 2, 16, 1024), BF),
            pltpu.VMEM((units, 2, 2, 2, 2, 2, 16, 1024), BF),
            pltpu.VMEM((units, 2, 2, 2, 2, 16, 1024), BF),
            pltpu.VMEM((units, 2, 2, 2, 16, 1024), BF),
            pltpu.VMEM((units, 2, 2, 16, 1024), BF),
            pltpu.VMEM((units, 2, 16, 1024), BF),
            dma((3, 5)),
            dma((units, 12)),
            dma((units, 12)),
            dma((units, 2)),
        ],
        compiler_params=pltpu.CompilerParams(
            collective_id=1, has_side_effects=True, vmem_limit_bytes=60 << 20
        ),
        name="reduce_grads",
    )(*lefts, *rights)
    found = found.reshape(units, 256, 1024)
    grads = []
    for li, ri, first, count, by_rows in groups:
        part = found[first : first + count]
        if not by_rows:
            part = jnp.transpose(part, (1, 0, 2))
        grads.append(part.reshape((count * 256, 1024) if by_rows else (256, -1)).astype(F32))
    return grads


def reduce_plain(pairs):
    grads = []
    for left, right in pairs:
        full = lax.dot_general(left, right, (((0,), (0,)), ((), ())), preferred_element_type=F32)
        part = lax.psum_scatter(full.astype(BF), "shard", scatter_dimension=0, tiled=True)
        grads.append(lax.psum(part, "rep").astype(F32))
    return grads


def swap_kernel(n, x_ref, o_ref, ssem, rsem):
    rep = lax.axis_index("rep")
    barrier = pltpu.get_barrier_semaphore()
    for d in range(1, n):
        pl.semaphore_signal(
            barrier, inc=1, device_id={"rep": jnp.bitwise_xor(rep, d)}, device_id_type=MESH
        )
    pl.semaphore_wait(barrier, n - 1)
    copies = []
    for d in range(1, n):
        other = jnp.bitwise_xor(rep, d)
        copy = pltpu.make_async_remote_copy(
            src_ref=x_ref.at[other],
            dst_ref=o_ref.at[rep],
            send_sem=ssem.at[d],
            recv_sem=rsem.at[d],
            device_id={"rep": other},
            device_id_type=MESH,
        )
        copy.start()
        copies.append(copy)
    o_ref[rep] = x_ref[rep]
    for copy in copies:
        copy.wait()


def swap(array, which):
    n = array.shape[0]
    return pl.pallas_call(
        functools.partial(swap_kernel, n),
        out_shape=jax.ShapeDtypeStruct(array.shape, array.dtype),
        in_specs=[VM],
        out_specs=VM,
        scratch_shapes=[pltpu.SemaphoreType.DMA((n,)), pltpu.SemaphoreType.DMA((n,))],
        compiler_params=pltpu.CompilerParams(
            collective_id=2 + which, has_side_effects=True, vmem_limit_bytes=32 << 20
        ),
        name="swap_%d" % which,
    )(array)


def to_heads(arrays, n):
    batch, local, features = arrays[0].shape
    parts = [a.reshape(batch, local, n, features // n) for a in arrays]
    stacked = jnp.stack([jnp.transpose(p, (2, 0, 1, 3)) for p in parts], axis=1)
    return stacked


def from_positions(swapped):
    n, k, batch, local, width = swapped.shape
    return [
        jnp.transpose(swapped[:, i], (1, 0, 2, 3)).reshape(batch, n * local, width)
        for i in range(k)
    ]


def to_positions(arrays, n):
    batch, total, width = arrays[0].shape
    parts = [
        jnp.transpose(a.reshape(batch, n, total // n, width), (1, 0, 2, 3)) for a in arrays
    ]
    return jnp.stack(parts, axis=1)


def from_heads(swapped):
    n, k, batch, local, width = swapped.shape
    return [
        jnp.transpose(swapped[:, i], (1, 2, 0, 3)).reshape(batch * local, n * width)
        for i in range(k)
    ]


QROWS = 256


def head_mask(shape, head):
    lane = lax.broadcasted_iota(jnp.int32, shape, 1)
    return jnp.logical_and(lane >= head * HD, lane < (head + 1) * HD)


def spread_bias(bias, spread, block):
    wide = bias.shape[1]
    lane = lax.broadcasted_iota(jnp.int32, (128, wide), 1)
    bias[...] = jnp.where(lane < (block + 1) * 128, spread[:, 0:1], spread[:, 383:384])
    rolled = pltpu.roll(spread, 0, 1, stride=1, stride_axis=0)
    bias[:, pl.ds(pl.multiple_of(block * 128, 128), 384)] = rolled[:, 0:384]


def forward_kernel(q_ref, k_ref, v_ref, table_ref, mixed_ref, lse_ref, bias):
    step = pl.program_id(1)
    total, width = (k_ref.shape[1], k_ref.shape[2])
    heads = width // HD
    keys = k_ref[0]
    values = v_ref[0]
    ones = jnp.ones((total, 128), BF)
    wide_values = jnp.concatenate([values, ones], axis=1) if width == 128 else None
    for sub in range(QROWS // 128):
        rows = slice(sub * 128, (sub + 1) * 128)
        query = q_ref[0, rows, :] * jnp.asarray(0.125, BF)
        block = step * (QROWS // 128) + sub
        for head in range(heads):
            mask = head_mask((128, width), head)
            part = jnp.where(mask, query, jnp.zeros_like(query))
            spread = lax.dot_general(
                part, table_ref[...], (((1,), (1,)), ((), ())), preferred_element_type=F32
            )
            spread_bias(bias, spread.astype(BF).astype(F32), block)
            scores = lax.dot_general(
                part, keys, (((1,), (1,)), ((), ())), preferred_element_type=F32
            )
            scores = scores + bias[:, 128 : 128 + total]
            top = jnp.max(scores, axis=1, keepdims=True)
            weight = jnp.exp(scores - top)
            summed = jnp.sum(weight, axis=1, keepdims=True)
            mixed = jnp.dot(weight.astype(BF), values, preferred_element_type=F32) / summed
            logsum = jnp.broadcast_to(top + jnp.log(summed), (128, width))
            if head == 0:
                mixed_ref[0, rows, :] = mixed
                lse_ref[0, rows, :] = logsum
            else:
                mixed_ref[0, rows, :] = jnp.where(mask, mixed, mixed_ref[0, rows, :])
                lse_ref[0, rows, :] = jnp.where(mask, logsum, lse_ref[0, rows, :])


def attention_forward(query, keys, values, table):
    batch, total, width = query.shape
    part = pl.BlockSpec((1, QROWS, width), lambda b, i: (b, i, 0))
    whole = pl.BlockSpec((1, total, width), lambda b, i: (b, 0, 0))
    shape = jax.ShapeDtypeStruct((batch, total, width), F32)
    return pl.pallas_call(
        forward_kernel,
        out_shape=[shape, shape],
        grid=(batch, total // QROWS),
        in_specs=[part, whole, whole, pl.BlockSpec(table.shape, lambda b, i: (0, 0))],
        out_specs=[part, part],
        scratch_shapes=[pltpu.VMEM((128, total + 256), F32)],
        compiler_params=pltpu.CompilerParams(vmem_limit_bytes=32 << 20),
        name="attention_forward",
    )(query, keys, values, table)


def backward_kernel(
    q_ref,
    k_ref,
    v_ref,
    table_ref,
    mixed_ref,
    lse_ref,
    g_ref,
    dq_ref,
    dk_ref,
    dv_ref,
    dtable_ref,
    bias,
    keyx,
    dscore,
    prob,
    dkt,
    dvt,
):
    batch_at, step = (pl.program_id(0), pl.program_id(1))
    total, width = (k_ref.shape[1], k_ref.shape[2])
    heads = width // HD

    @pl.when(jnp.logical_and(batch_at == 0, step == 0))
    def _():
        dtable_ref[...] = jnp.zeros_like(dtable_ref)

    @pl.when(step == 0)
    def _():
        dkt[...] = jnp.zeros_like(dkt)
        dvt[...] = jnp.zeros_like(dvt)
        keyx[:, 0:width] = k_ref[0]
        row = lax.broadcasted_iota(jnp.int32, (total, 128), 0) // 128
        lane = lax.broadcasted_iota(jnp.int32, (total, 128), 1)
        keyx[:, width : width + 128] = (row == lane).astype(BF)
        dscore[:, 0:128] = jnp.zeros((128, 128), BF)
        dscore[:, 128 + total : 256 + total] = jnp.zeros((128, 128), BF)

    keys = k_ref[0]
    values = v_ref[0]
    flip = (
        lax.broadcasted_iota(jnp.int32, (128, 128), 0)
        + lax.broadcasted_iota(jnp.int32, (128, 128), 1)
        == 127
    ).astype(BF)
    lane_at = lax.broadcasted_iota(jnp.int32, (128, 128), 1)
    band_at = lax.broadcasted_iota(jnp.int32, (128, BAND), 1)
    for sub in range(QROWS // 128):
        rows = slice(sub * 128, (sub + 1) * 128)
        block = step * (QROWS // 128) + sub
        query = q_ref[0, rows, :] * jnp.asarray(0.125, BF)
        grad = g_ref[0, rows, :]
        weighed = grad.astype(F32) * mixed_ref[0, rows, :]
        query_t = jnp.transpose(query.astype(F32)).astype(BF)
        grad_t = jnp.transpose(grad.astype(F32)).astype(BF)
        for head in range(heads):
            mask = head_mask((128, width), head)
            lanes = slice(head * HD, (head + 1) * HD)
            part = jnp.where(mask, query, jnp.zeros_like(query))
            grad_part = jnp.where(mask, grad, jnp.zeros_like(grad))
            balance = jnp.sum(jnp.where(mask, weighed, 0.0), axis=1, keepdims=True)
            logsum = lse_ref[0, rows, head * HD : head * HD + 1]
            spread = lax.dot_general(
                part, table_ref[...], (((1,), (1,)), ((), ())), preferred_element_type=F32
            )
            spread_bias(bias, spread.astype(BF).astype(F32), block)
            scores = lax.dot_general(
                part, keys, (((1,), (1,)), ((), ())), preferred_element_type=F32
            )
            chance = jnp.exp(scores + bias[:, 128 : 128 + total] - logsum)
            back = lax.dot_general(
                grad_part, values, (((1,), (1,)), ((), ())), preferred_element_type=F32
            )
            prob[...] = chance.astype(BF)
            dscore[:, 128 : 128 + total] = (chance * (back - balance)).astype(BF)
            score_back = dscore[:, 128 : 128 + total]
            dkt[lanes, :] += jnp.dot(query_t[lanes, :], score_back, preferred_element_type=F32)
            dvt[lanes, :] += jnp.dot(grad_t[lanes, :], prob[...], preferred_element_type=F32)
            wide = jnp.dot(score_back, keyx[...], preferred_element_type=F32)
            sums = wide[:, width : width + 128]
            before = jnp.sum(jnp.where(lane_at < block - 1, sums, 0.0), axis=1, keepdims=True)
            after = jnp.sum(jnp.where(lane_at > block + 1, sums, 0.0), axis=1, keepdims=True)
            near = dscore[:, pl.ds(pl.multiple_of(block * 128, 128), 384)]
            near = jnp.dot(flip, near, preferred_element_type=F32)
            near = jnp.concatenate([near, jnp.zeros((128, BAND - 384), F32)], axis=1)
            near = pltpu.roll(near, BAND - 127, 1, stride=1, stride_axis=0)
            near = jnp.dot(flip, near.astype(BF), preferred_element_type=F32)
            near = near + jnp.where(band_at == 0, before, 0.0)
            near = (near + jnp.where(band_at == 383, after, 0.0)).astype(BF)
            query_back = wide[:, 0:width] + jnp.dot(
                near, table_ref[...], preferred_element_type=F32
            )
            dtable_ref[...] += lax.dot_general(
                near, part, (((0,), (0,)), ((), ())), preferred_element_type=F32
            )
            query_back = (query_back * 0.125).astype(BF)
            if head == 0:
                dq_ref[0, rows, :] = query_back
            else:
                dq_ref[0, rows, :] = jnp.where(mask, query_back, dq_ref[0, rows, :])

    @pl.when(step == pl.num_programs(1) - 1)
    def _():
        dk_ref[0] = jnp.transpose(dkt[...]).astype(BF)
        dv_ref[0] = jnp.transpose(dvt[...]).astype(BF)


def attention_backward(query, keys, values, table, mixed, logsum, grad):
    batch, total, width = query.shape
    part = pl.BlockSpec((1, QROWS, width), lambda b, i: (b, i, 0))
    whole = pl.BlockSpec((1, total, width), lambda b, i: (b, 0, 0))
    fixed = pl.BlockSpec(table.shape, lambda b, i: (0, 0))
    shape = jax.ShapeDtypeStruct((batch, total, width), BF)
    return pl.pallas_call(
        backward_kernel,
        out_shape=[shape, shape, shape, jax.ShapeDtypeStruct(table.shape, F32)],
        grid=(batch, total // QROWS),
        in_specs=[part, whole, whole, fixed, part, part, part],
        out_specs=[part, whole, whole, fixed],
        scratch_shapes=[
            pltpu.VMEM((128, total + 256), F32),
            pltpu.VMEM((total, width + 128), BF),
            pltpu.VMEM((128, total + 256), BF),
            pltpu.VMEM((128, total), BF),
            pltpu.VMEM((width, total), F32),
            pltpu.VMEM((width, total), F32),
        ],
        compiler_params=pltpu.CompilerParams(vmem_limit_bytes=40 << 20),
        name="attention_backward",
    )(query, keys, values, table, mixed, logsum, grad)


def shifted(value, axis, steps):
    count = lax.axis_size(axis)
    leading, last = (max(0, -steps), min(count, count - steps))
    return lax.ppermute(value, axis, [(source, source + steps) for source in range(leading, last)])


def statistics(values):
    centre = jnp.mean(values, axis=-1, keepdims=True)
    centred = values - centre
    spread = jnp.mean(centred * centred, axis=-1, keepdims=True)
    return centre, lax.rsqrt(spread + EPSILON)


def norm(values, gain, shift):
    centre, scale = statistics(values)
    return (values - centre) * scale * gain + shift


def norm_back(values, gain, grad):
    centre, scale = statistics(values)
    hat = (values - centre) * scale
    weighed = grad * gain
    back = (
        weighed
        - jnp.mean(weighed, axis=-1, keepdims=True)
        - hat * jnp.mean(weighed * hat, axis=-1, keepdims=True)
    ) * scale
    return back, jnp.sum(grad * hat, axis=0), jnp.sum(grad, axis=0)


def swish(values):
    return values * jax.nn.sigmoid(values)


def swish_slope(values):
    gate = jax.nn.sigmoid(values)
    return gate * (1.0 + values * (1.0 - gate))


def times(left, right):
    return jnp.dot(left, right, preferred_element_type=F32)


def times_back(left, right):
    return lax.dot_general(left, right, (((1,), (1,)), ((), ())), preferred_element_type=F32)


def column_sum(values):
    return jnp.sum(values.astype(F32), axis=0)


MATRICES = (2, 4, 8, 10, 11, 13, 18, 22, 25, 27)
VECTORS = (0, 1, 5, 6, 7, 9, 12, 14, 16, 17, 20, 21, 23, 24, 28, 29, 30)
OFFSETS = (3, 26)
TABLE_AT = 15
TAPS_AT = 19


def pack_small(shards):
    width = shards[0].shape[0]
    rows = [shards[i].reshape(1, width) for i in VECTORS]
    rows += [shards[i].reshape(-1, width) for i in OFFSETS]
    rows.append(shards[TAPS_AT])
    table = shards[TABLE_AT].reshape(-1)
    spare = -table.shape[0] % width
    rows.append(jnp.pad(table, (0, spare)).reshape(-1, width))
    count = sum(r.shape[0] for r in rows)
    rows.append(jnp.zeros((-count % 16, width), rows[0].dtype))
    return jnp.concatenate(rows, axis=0)


def unpack_small(gathered, shards):
    n, _, width = gathered.shape
    full = {}
    at = 0
    for i in VECTORS:
        full[i] = gathered[:, at].reshape(n * width).astype(F32)
        at += 1
    for i in OFFSETS:
        count = shards[i].shape[0] // width
        full[i] = gathered[:, at : at + count].reshape(n * width * count).astype(F32)
        at += count
    count = shards[TAPS_AT].shape[0]
    full[TAPS_AT] = jnp.transpose(gathered[:, at : at + count], (1, 0, 2)).reshape(count, -1)
    at += count
    rows, cols = shards[TABLE_AT].shape
    count = -(-rows * cols // width)
    table = gathered[:, at : at + count].reshape(n, -1)[:, : rows * cols].reshape(n, rows, cols)
    full[TABLE_AT] = jnp.transpose(table, (1, 0, 2)).reshape(rows, n * cols)
    return full


def sum_small(grads, shards):
    n = lax.axis_size("shard")
    order = VECTORS + OFFSETS + (TAPS_AT, TABLE_AT)
    flat = jnp.concatenate([grads[i].reshape(-1) for i in order])
    spare = -flat.shape[0] % 16384
    flat = jnp.pad(flat, (0, spare)).astype(BF).reshape(-1, 1024)
    flat = lax.psum(flat, ("rep", "shard")).astype(F32).reshape(-1)
    z = lax.axis_index("shard")
    found = {}
    at = 0
    for i in order:
        size = grads[i].size
        whole = flat[at : at + size].reshape(grads[i].shape)
        at += size
        axis = whole.ndim - 1
        part = whole.shape[axis] // n
        found[i] = lax.dynamic_slice_in_dim(whole, z * part, part, axis)
    return found


def feed_forward(entering, gain, shift, widen, offset, narrow, bias):
    normed = norm(entering, gain, shift).astype(BF)
    act = times(normed, widen) + offset
    hidden = swish(act).astype(BF)
    return entering + 0.5 * (times(hidden, narrow) + bias), (normed, act, hidden)


def feed_backward(entering, gain, widen, narrow, saved, out_grad):
    normed, act, hidden = saved
    out_low = (0.5 * out_grad).astype(BF)
    act_grad = (times_back(out_low, narrow) * swish_slope(act)).astype(BF)
    normed_grad = times_back(act_grad, widen)
    back, grad_gain, grad_shift = norm_back(entering, gain, normed_grad)
    return (
        out_grad + back,
        (grad_gain, grad_shift, column_sum(act_grad), column_sum(out_low)),
        [(hidden, out_low), (normed, act_grad)],
    )


def conv_taps(padded, taps, local):
    total = padded[:, 0:local] * taps[0]
    for j in range(1, taps.shape[0]):
        total = total + padded[:, j : j + local] * taps[j]
    return total


def on_device(*arguments):
    inputs, shards, cotangent = (arguments[0], arguments[1:32], arguments[32])
    n_rep, n_shard = (lax.axis_size("rep"), lax.axis_size("shard"))
    micro, local, seqs, features = inputs.shape
    batch = micro * seqs
    fast = (
        n_rep == 8
        and n_shard == 4
        and features == 1024
        and batch * local == 256
        and all(shards[i].shape[0] % 256 == 0 for i in MATRICES)
    )

    def rows_of(array):
        return jnp.transpose(array, (0, 2, 1, 3)).reshape(batch * local, features)

    def whole_of(rows):
        return jnp.transpose(rows.reshape(micro, seqs, local, features), (0, 2, 1, 3))

    small = pack_small(shards)
    if fast:
        full, gathered = gather_fast([shards[i] for i in MATRICES], small)
    else:
        full = [lax.all_gather(shards[i], "shard", axis=0, tiled=True) for i in MATRICES]
        gathered = lax.all_gather(small, "shard", axis=0, tiled=False)
    w = dict(zip(MATRICES, full))
    w.update(unpack_small(gathered, shards))

    level0 = rows_of(inputs).astype(F32)
    level1, early = feed_forward(level0, w[0], w[1], w[2], w[3], w[4], w[5])

    attend_in = norm(level1, w[6], w[7]).astype(BF)
    query = (times(attend_in, w[8]) + w[9]).astype(BF).reshape(batch, local, features)
    keys = times(attend_in, w[10]).astype(BF).reshape(batch, local, features)
    values = (times(attend_in, w[11]) + w[12]).astype(BF).reshape(batch, local, features)
    query_h, keys_h, values_h = from_positions(swap(to_heads([query, keys, values], n_rep), 0))
    place = jnp.clip(jnp.arange(BAND) - 64, 0, TABLE - 1)
    place = jnp.where(jnp.arange(BAND) >= 384, 0, place)
    table = w[TABLE_AT]
    spread_table = jnp.tile(jnp.take(table, place, axis=0), (1, query_h.shape[2] // HD))
    mixed_h, logsum = attention_forward(query_h, keys_h, values_h, spread_table)
    mixed = from_heads(swap(to_positions([mixed_h.astype(BF)], n_rep), 1))[0]
    level2 = level1 + times(mixed, w[13]) + w[14]

    conv_in = norm(level2, w[16], w[17]).astype(BF)
    doubled = times(conv_in, w[18])
    side_a, side_b = (doubled[:, :features], doubled[:, features:])
    gate = jax.nn.sigmoid(side_b)
    gated = (side_a * gate).reshape(batch, local, features)
    taps = w[TAPS_AT].astype(F32)
    rim = taps.shape[0] - 1
    rim_in = shifted(gated[:, local - rim :].astype(BF), "rep", 1).astype(F32)
    padded = jnp.concatenate([rim_in, gated], axis=1)
    depth = conv_taps(padded, taps, local).reshape(batch * local, features)
    depth_normed = norm(depth, w[20], w[21])
    acted = swish(depth_normed).astype(BF)
    level3 = level2 + times(acted, w[22])

    level4, later = feed_forward(level3, w[23], w[24], w[25], w[26], w[27], w[28])
    output = norm(level4, w[29], w[30]).astype(BF)

    grads = {}
    incoming = rows_of(cotangent).astype(F32)
    back4, grads[29], grads[30] = norm_back(level4, w[29], incoming)
    back3, found, later_pairs = feed_backward(level3, w[23], w[25], w[27], later, back4)
    grads[23], grads[24], grads[26], grads[28] = found

    conv_out = back3.astype(BF)
    depth_mid = times_back(conv_out, w[22]) * swish_slope(depth_normed)
    depth_back, grads[20], grads[21] = norm_back(depth, w[20], depth_mid)
    depth_back = depth_back.reshape(batch, local, features)
    rim_back = shifted(depth_back[:, :rim].astype(BF), "rep", -1).astype(F32)
    after = jnp.concatenate([depth_back, rim_back], axis=1)
    grads[TAPS_AT] = jnp.stack(
        [jnp.sum(depth_back * padded[:, j : j + local], axis=(0, 1)) for j in range(rim + 1)]
    )
    gated_back = conv_taps(after, taps[::-1], local).reshape(batch * local, features)
    doubled_back = jnp.concatenate(
        [gated_back * gate, gated_back * side_a * gate * (1.0 - gate)], axis=1
    ).astype(BF)
    conv_back = times_back(doubled_back, w[18])
    back, grads[16], grads[17] = norm_back(level2, w[16], conv_back)
    back2 = back3 + back

    mixer_out = back2.astype(BF)
    grads[14] = column_sum(mixer_out)
    mixed_back = times_back(mixer_out, w[13]).astype(BF).reshape(batch, local, features)
    grad_h = from_positions(swap(to_heads([mixed_back], n_rep), 2))[0]
    query_b, keys_b, values_b, table_b = attention_backward(
        query_h, keys_h, values_h, spread_table, mixed_h, logsum, grad_h
    )
    query_back, key_back, value_back = from_heads(
        swap(to_positions([query_b, keys_b, values_b], n_rep), 3)
    )
    folded = table_b.reshape(BAND, -1, HD).sum(axis=1)
    grads[TABLE_AT] = jnp.concatenate(
        [
            (folded[0:65].sum(axis=0) + folded[384:].sum(axis=0))[None],
            folded[65:136],
            folded[136:384].sum(axis=0)[None],
        ]
    )
    grads[9] = column_sum(query_back)
    grads[12] = column_sum(value_back)
    attend_back = (
        times_back(query_back, w[8]) + times_back(key_back, w[10]) + times_back(value_back, w[11])
    )
    back, grads[6], grads[7] = norm_back(level1, w[6], attend_back)
    back1 = back2 + back
    back0, found, early_pairs = feed_backward(level0, w[0], w[2], w[4], early, back1)
    grads[0], grads[1], grads[3], grads[5] = found

    pairs = (
        (27, later_pairs[0]),
        (25, later_pairs[1]),
        (22, (acted, conv_out)),
        (18, (conv_in, doubled_back)),
        (13, (mixed, mixer_out)),
        (8, (attend_in, query_back)),
        (10, (attend_in, key_back)),
        (11, (attend_in, value_back)),
        (4, early_pairs[0]),
        (2, early_pairs[1]),
    )
    reduce = reduce_fast if fast else reduce_plain
    summed = dict(zip([i for i, _ in pairs], reduce([pair for _, pair in pairs])))
    summed.update(sum_small(grads, shards))
    return (whole_of(output), whole_of(back0)) + tuple(summed[i] for i in range(31))


def solution(mesh):
    rows, vector, matrix = (P(None, "rep", "shard", None), P("shard"), P("shard", None))
    columns = P(None, "shard")
    weights = tuple(
        matrix if i in MATRICES else columns if i in (TABLE_AT, TAPS_AT) else vector
        for i in range(31)
    )
    return jax.shard_map(
        on_device,
        mesh=mesh,
        in_specs=(rows,) + weights + (rows,),
        out_specs=(rows, rows) + weights,
        check_vma=False,
    )
```

```python
import functools

import jax
import jax.numpy as jnp
from jax import lax
from jax.experimental import pallas as pl
from jax.experimental.pallas import tpu as pltpu
from jax.sharding import PartitionSpec as P

H = 16
HD = 64
LEFT = 64
RIGHT = 8
TABLE = 73
EPSILON = 1e-05
BAND = 512
MESH = pl.DeviceIdType.MESH
BF = jnp.bfloat16
F32 = jnp.float32
ANY = pl.BlockSpec(memory_space=pltpu.HBM)
VM = pl.BlockSpec(memory_space=pltpu.VMEM)


def here():
    rep = lax.axis_index("rep")
    z = lax.axis_index("shard")
    core = lax.rem(rep, 2)
    x = lax.rem(rep // 2, 2)
    y = rep // 4
    z0 = lax.rem(z, 2)
    z1 = z // 2
    peers = {
        "z1": (rep, lax.rem(z + 2, 4)),
        "z0": (rep, z + 1 - 2 * z0),
        "zz": (rep, 3 - z),
        "x": (rep + 2 - 4 * x, z),
        "y": (rep + 4 - 8 * y, z),
        "c": (rep + 1 - 2 * core, z),
    }
    return z, core, x, y, z0, z1, peers


def meet(peers):
    barrier = pltpu.get_barrier_semaphore()
    for name in peers:
        pl.semaphore_signal(barrier, inc=1, device_id=peers[name], device_id_type=MESH)
    pl.semaphore_wait(barrier, len(peers))


GATHER_LAG = (0, 2, 3, 4, 5)


def fill_rows(packed, smalls):
    width = packed.shape[1]
    packed[...] = jnp.zeros_like(packed)
    at = 0
    for ref in smalls:
        if len(ref.shape) == 1:
            for k in range(ref.shape[0] // width):
                packed[at, :] = ref[pl.ds(k * width, width)].astype(F32)
                at += 1
        else:
            packed[at : at + ref.shape[0], 0 : ref.shape[1]] = ref[...].astype(F32)
            at += ref.shape[0]


def gather_kernel(chunks, n_arr, n_small, *refs):
    ins, smalls = (refs[:n_arr], refs[n_arr : n_arr + n_small])
    refs = refs[n_arr + n_small :]
    outs, small_out = (refs[:n_arr], refs[n_arr])
    ssem, rsem, lsem, lsem2, qsem, psem, packed, small = refs[n_arr + 1 : n_arr + 9]
    bufs = refs[n_arr + 9 :]
    z, core, x, y, z0, z1, peers = here()
    fill_rows(packed, smalls)
    small[...] = packed[...].astype(BF)
    far = ((slice(None), 1 - z0), (1 - z1, z0))
    meet(peers)
    sent = []

    def send(c, slot, src, dst, to):
        copy = pltpu.make_async_remote_copy(
            src_ref=src,
            dst_ref=dst,
            send_sem=ssem.at[c, slot],
            recv_sem=rsem.at[c, slot],
            device_id=peers[to],
            device_id_type=MESH,
        )
        copy.start()
        sent.append(copy)
        return copy

    around = []
    for k, to in enumerate(("z0", "z1", "zz")):
        copy = pltpu.make_async_remote_copy(
            src_ref=small,
            dst_ref=small_out.at[z],
            send_sem=qsem.at[k],
            recv_sem=psem.at[k],
            device_id=peers[to],
            device_id_type=MESH,
        )
        copy.start()
        around.append(copy)
    small_own = pltpu.make_async_copy(small, small_out.at[z], lsem.at[n_arr])
    small_own.start()
    state = {}

    def place(c):
        array, first, count = chunks[c]
        return (ins[array], outs[array], pl.ds(first, count))

    def wait(c, key):
        for copy in state[c, key]:
            copy.wait_recv()

    def stage_z(c):
        src, out, cols = place(c)
        src = src.at[y, x, core, :, :, cols]
        dst = out.at[z1, z0, y, x, core, :, :, cols]
        state[c, "z1"] = [send(c, 0, src, dst, "z1")]
        state[c, "z0"] = [send(c, 1, src, dst, "z0")]

    def stage_zz(c):
        _, out, cols = place(c)
        wait(c, "z1")
        view = out.at[1 - z1, z0, y, x, core, :, :, cols]
        state[c, "z0"].append(send(c, 2, view, view, "z0"))

    def stage_one(c):
        _, out, cols = place(c)
        wait(c, "z0")
        state[c, "one"] = []
        for i, (a, b) in enumerate(far):
            view = out.at[a, b, y, x, core, 0, :, cols]
            state[c, "one"].append(send(c, 3 + i, view, view, "x"))
            view = out.at[a, b, y, x, core, 1, :, cols]
            state[c, "one"].append(send(c, 5 + i, view, view, "y"))

    def stage_two(c):
        _, out, cols = place(c)
        wait(c, "one")
        state[c, "two"] = []
        for i, (a, b) in enumerate(far):
            view = out.at[a, b, y, :, core, 0, :, cols]
            state[c, "two"].append(send(c, 7 + i, view, view, "y"))
            view = out.at[a, b, :, x, core, 1, :, cols]
            state[c, "two"].append(send(c, 9 + i, view, view, "x"))

    def stage_core(c):
        _, out, cols = place(c)
        wait(c, "two")
        state[c, "core"] = []
        for i, (a, b) in enumerate(far):
            view = out.at[a, b, :, :, core, :, :, cols]
            state[c, "core"].append(send(c, 11 + i, view, view, "c"))

    stages = (stage_z, stage_zz, stage_one, stage_two, stage_core)
    local = []
    for step in range(len(chunks) + GATHER_LAG[-1]):
        for stage, lag in zip(stages, GATHER_LAG):
            if 0 <= step - lag < len(chunks):
                stage(step - lag)
        if step == 0:
            for a in range(n_arr):
                copy = pltpu.make_async_copy(ins[a], bufs[a], lsem.at[a])
                copy.start()
                local.append(copy)
        if step == 3:
            for a in range(n_arr):
                local[a].wait()
                copy = pltpu.make_async_copy(bufs[a], outs[a].at[z1, z0], lsem2.at[a])
                copy.start()
                local[a] = copy
    for c in range(len(chunks)):
        wait(c, "core")
    for copy in sent + around:
        copy.wait_send()
    for copy in around:
        copy.wait_recv()
    small_own.wait()
    for copy in local:
        copy.wait()


def gather_chunks(shapes):
    chunks = []
    for i, (rows, cols) in enumerate(shapes):
        for first in range(0, cols, 1024 * 256 // rows):
            chunks.append((i, first, 1024 * 256 // rows))
    return chunks


def gather_fast(shards, smalls, rows):
    count, width = (len(shards), smalls[0].shape[0])
    ins = [w.reshape(2, 2, 2, 2, w.shape[0] // 16, w.shape[1]) for w in shards]
    chunks = gather_chunks([w.shape for w in shards])
    outs = [jax.ShapeDtypeStruct((2, 2) + w.shape, w.dtype) for w in ins]
    outs.append(jax.ShapeDtypeStruct((4, rows, width), BF))
    dma = pltpu.SemaphoreType.DMA
    found = pl.pallas_call(
        functools.partial(gather_kernel, chunks, count, len(smalls)),
        out_shape=outs,
        in_specs=[ANY] * count + [VM] * len(smalls),
        out_specs=[ANY] * (count + 1),
        scratch_shapes=[
            dma((len(chunks), 13)),
            dma((len(chunks), 13)),
            dma((count + 1,)),
            dma((count,)),
            dma((3,)),
            dma((3,)),
            pltpu.VMEM((rows, width), F32),
            pltpu.VMEM((rows, width), BF),
        ]
        + [pltpu.VMEM(w.shape, w.dtype) for w in ins],
        compiler_params=pltpu.CompilerParams(
            collective_id=0, has_side_effects=True, vmem_limit_bytes=58 << 20
        ),
        name="gather_weights",
    )(*ins, *smalls)
    return [w.reshape(-1, w.shape[-1]) for w in found[:count]], found[count]


def fill_sums(total, smalls):
    width = total.shape[1] // 4
    total[...] = jnp.zeros_like(total)
    at = 0
    for ref in smalls:
        if len(ref.shape) > 1:
            total[at : at + ref.shape[0], :] = ref[...]
            at += ref.shape[0]
        elif ref.shape[0] == 4 * width:
            total[at, :] = ref[...]
            at += 1
        else:
            each = ref.shape[0] // (4 * width)
            for k in range(each):
                for z in range(4):
                    total[at, pl.ds(z * width, width)] = ref[pl.ds((z * each + k) * width, width)]
                at += 1


REDUCE_LAG = (0, 1, 2, 3, 4, 5, 6, 7)


def reduce_kernel(groups, units, n_left, n_right, n_small, *refs):
    lefts, rights = (refs[:n_left], refs[n_left : n_left + n_right])
    refs = refs[n_left + n_right :]
    smalls, outs, small_out = (refs[:n_small], refs[n_small:-18], refs[-18])
    lbuf, rbuf, sbuf, b1, b2, b3, b4, b5, hop_out, hop_in, hop_total = refs[-17:-6]
    lsem, ssem, rsem, osem, hsem, isem = refs[-6:]
    z, core, x, y, z0, z1, peers = here()
    del peers["zz"]
    meet(peers)

    def remote(u, slot, src, dst, to):
        return pltpu.make_async_remote_copy(
            src_ref=src,
            dst_ref=dst,
            send_sem=ssem.at[u, slot],
            recv_sem=rsem.at[u, slot],
            device_id=peers[to],
            device_id_type=MESH,
        )

    def copy_core(u):
        return [remote(u, 0, sbuf.at[lax.rem(u, 2)], b1.at[u], "c")]

    def copy_first(u):
        return [
            remote(u, 1, b1.at[u, :, :, 0, 1 - x], b2.at[u, 0], "x"),
            remote(u, 2, b1.at[u, :, :, 1, 1 - y], b2.at[u, 1], "y"),
        ]

    def copy_z0(u):
        return [remote(u, 3, b2.at[u, :, :, 1 - z0], b3.at[u], "z0")]

    def copy_z1(u):
        return [remote(u, 4, b3.at[u, :, 1 - z1], b4.at[u], "z1")]

    def copy_second(u):
        return [
            remote(u, 5, b4.at[u, 0, 1 - y], b5.at[u, 0], "y"),
            remote(u, 6, b4.at[u, 1, 1 - x], b5.at[u, 1], "x"),
        ]

    def block(group, k, *at):
        if groups[group][4]:
            return outs[group].at[(k,) + at]
        at = at + (slice(None),) * (5 - len(at))
        return outs[group].at[at + (pl.ds(pl.multiple_of(k * 1024, 1024), 1024),)]

    def copy_own(u, group=0, k=0):
        return [
            pltpu.make_async_copy(b5.at[u, 0], block(group, k, core, 0, x, y), osem.at[u, 0]),
            pltpu.make_async_copy(b5.at[u, 1], block(group, k, core, 1, y, x), osem.at[u, 1]),
        ]

    def spread_second(u, group=0, k=0):
        return [
            remote(u, 7, b5.at[u, 0], block(group, k, core, 0, x, y), "y"),
            remote(u, 8, b5.at[u, 1], block(group, k, core, 1, y, x), "x"),
        ]

    def spread_first(u, group=0, k=0):
        a, b = (block(group, k, core, 0, x), block(group, k, core, 1, y))
        return [remote(u, 9, a, a, "x"), remote(u, 10, b, b, "y")]

    def spread_core(u, group=0, k=0):
        a = block(group, k, core)
        return [remote(u, 11, a, a, "c")]

    def start_out(u, *makers):
        for group, (_, _, first, count, _) in enumerate(groups):

            @pl.when(jnp.logical_and(u >= first, u < first + count))
            def _():
                for make in makers:
                    start(make(u, group, u - first))

    def start(copies):
        for copy in copies:
            copy.start()

    def arrive(copies):
        for copy in copies:
            copy.wait_recv()

    def load(u):
        slot = lax.rem(u, 3)
        for li, ri, first, count, by_rows in groups:

            @pl.when(jnp.logical_and(u >= first, u < first + count))
            def _():
                k = u - first
                for part in range(4):
                    at = pl.multiple_of(part * 1024 + k * 256, 256) if by_rows else part * 256
                    pltpu.make_async_copy(
                        lefts[li].at[:, pl.ds(at, 256)], lbuf.at[slot, part], lsem.at[slot, part]
                    ).start()
                at = 0 if by_rows else pl.multiple_of(k * 1024, 1024)
                pltpu.make_async_copy(
                    rights[ri].at[:, pl.ds(at, 1024)], rbuf.at[slot], lsem.at[slot, 4]
                ).start()

    def product(u, part, half):
        slot = lax.rem(u, 3)
        left = lbuf[slot, part, :, pl.ds(pl.multiple_of(half * 128, 128), 128)]
        return lax.dot_general(
            left, rbuf[slot], (((0,), (0,)), ((), ())), preferred_element_type=F32
        ).reshape(2, 2, 2, 16, 1024)

    load(0)
    load(1)

    def stage_multiply(u):
        slot = lax.rem(u, 3)
        for part in range(4):
            pltpu.make_async_copy(
                lefts[0].at[:, pl.ds(0, 256)], lbuf.at[slot, part], lsem.at[slot, part]
            ).wait()
        pltpu.make_async_copy(
            rights[0].at[:, pl.ds(0, 1024)], rbuf.at[slot], lsem.at[slot, 4]
        ).wait()

        @pl.when(u >= 2)
        def _():
            for copy in copy_core(u - 2):
                copy.wait_send()

        def body(part, carry):
            sbuf[lax.rem(u, 2), part // 2, lax.rem(part, 2)] = product(u, part, 1 - core).astype(BF)
            return carry

        lax.fori_loop(0, 4, body, 0)
        start(copy_core(u))

    def stage_own(u):
        arrive(copy_core(u))

        def body(part, carry):
            a, b = (part // 2, lax.rem(part, 2))
            b1[u, a, b] = (product(u, part, core) + b1[u, a, b].astype(F32)).astype(BF)
            return carry

        lax.fori_loop(0, 4, body, 0)
        start(copy_first(u))

        @pl.when(u + 2 < units)
        def _():
            load(u + 2)

    def stage_first(u):
        arrive(copy_first(u))

        def body(part, carry):
            a, b = (part // 2, lax.rem(part, 2))
            for half, bit in ((0, x), (1, y)):
                b2[u, half, a, b] = (
                    b2[u, half, a, b].astype(F32) + b1[u, a, b, half, bit].astype(F32)
                ).astype(BF)
            return carry

        lax.fori_loop(0, 4, body, 0)
        start(copy_z0(u))

    def stage_z0(u):
        arrive(copy_z0(u))
        for half in range(2):
            for a in range(2):
                b3[u, half, a] = (
                    b3[u, half, a].astype(F32) + b2[u, half, a, z0].astype(F32)
                ).astype(BF)
        start(copy_z1(u))

    def stage_z1(u):
        arrive(copy_z1(u))
        for half in range(2):
            b4[u, half] = (b4[u, half].astype(F32) + b3[u, half, z1].astype(F32)).astype(BF)
        start(copy_second(u))

    def stage_second(u):
        arrive(copy_second(u))
        for half, bit in ((0, y), (1, x)):
            b5[u, half] = (b5[u, half].astype(F32) + b4[u, half, bit].astype(F32)).astype(BF)
        start_out(u, copy_own, spread_second)

    def stage_spread(u):
        arrive(spread_second(u))
        for copy in copy_own(u):
            copy.wait()
        start_out(u, spread_first)

    def stage_core(u):
        arrive(spread_first(u))
        start_out(u, spread_core)

    stages = (
        stage_multiply,
        stage_own,
        stage_first,
        stage_z0,
        stage_z1,
        stage_second,
        stage_spread,
        stage_core,
    )

    hops = ("c", "x", "y", "z0", "z1")

    def hop(k):
        return pltpu.make_async_remote_copy(
            src_ref=hop_out.at[k],
            dst_ref=hop_in.at[k],
            send_sem=hsem.at[k],
            recv_sem=isem.at[k],
            device_id=peers[hops[k]],
            device_id_type=MESH,
        )

    fill_sums(hop_total, smalls)
    hop_out[0] = hop_total[...].astype(BF)
    hop(0).start()

    def stage_hop(k):
        hop(k).wait_recv()
        total = hop_out[k].astype(F32) + hop_in[k].astype(F32)
        if k + 1 < len(hops):
            hop_out[k + 1] = total.astype(BF)
            hop(k + 1).start()
        else:
            width = small_out.shape[1]
            hop_total[...] = total
            small_out[...] = hop_total[:, pl.ds(pl.multiple_of(z * width, width), width)]

    def step(i, carry):
        for k in range(len(hops)):

            @pl.when(i == 2 * k + 1)
            def _():
                stage_hop(k)

        for stage, lag in zip(stages, REDUCE_LAG):
            u = i - lag

            @pl.when(jnp.logical_and(u >= 0, u < units))
            def _():
                stage(u)

        return carry

    lax.fori_loop(0, units + REDUCE_LAG[-1], step, 0)

    def finish(u, carry):
        arrive(spread_core(u))
        for copies in (
            copy_first,
            copy_z0,
            copy_z1,
            copy_second,
            spread_second,
            spread_first,
            spread_core,
        ):
            for copy in copies(u):
                copy.wait_send()

        @pl.when(u >= units - 2)
        def _():
            for copy in copy_core(u):
                copy.wait_send()

        return carry

    lax.fori_loop(0, units, finish, 0)
    for k in range(len(hops)):
        hop(k).wait_send()


def reduce_fast(pairs, smalls):
    lefts, rights, groups, units = ([], [], [], 0)

    def index_of(arrays, array):
        for i, known in enumerate(arrays):
            if known is array:
                return i
        arrays.append(array)
        return len(arrays) - 1

    for left, right in pairs:
        by_rows = left.shape[1] > 1024
        count = left.shape[1] // 1024 if by_rows else right.shape[1] // 1024
        groups.append((index_of(lefts, left), index_of(rights, right), units, count, by_rows))
        units += count
    dma = pltpu.SemaphoreType.DMA
    rows = sum(a.shape[0] if a.ndim > 1 else a.shape[0] // 1024 for a in smalls)
    rows = -(-rows // 16) * 16
    outs = []
    for _, _, _, count, by_rows in groups:
        shape = (count, 2, 2, 2, 2, 16, 1024) if by_rows else (2, 2, 2, 2, 16, count * 1024)
        outs.append(jax.ShapeDtypeStruct(shape, BF))
    found = pl.pallas_call(
        functools.partial(reduce_kernel, groups, units, len(lefts), len(rights), len(smalls)),
        out_shape=outs + [jax.ShapeDtypeStruct((rows, 256), F32)],
        in_specs=[ANY] * (len(lefts) + len(rights)) + [VM] * len(smalls),
        out_specs=[ANY] * len(outs) + [VM],
        scratch_shapes=[
            pltpu.VMEM((3, 4, 256, 256), BF),
            pltpu.VMEM((3, 256, 1024), BF),
            pltpu.VMEM((2, 2, 2, 2, 2, 2, 16, 1024), BF),
            pltpu.VMEM((units, 2, 2, 2, 2, 2, 16, 1024), BF),
            pltpu.VMEM((units, 2, 2, 2, 2, 16, 1024), BF),
            pltpu.VMEM((units, 2, 2, 2, 16, 1024), BF),
            pltpu.VMEM((units, 2, 2, 16, 1024), BF),
            pltpu.VMEM((units, 2, 16, 1024), BF),
            pltpu.VMEM((5, rows, 1024), BF),
            pltpu.VMEM((5, rows, 1024), BF),
            pltpu.VMEM((rows, 1024), F32),
            dma((3, 5)),
            dma((units, 12)),
            dma((units, 12)),
            dma((units, 2)),
            dma((5,)),
            dma((5,)),
        ],
        compiler_params=pltpu.CompilerParams(
            collective_id=1, has_side_effects=True, vmem_limit_bytes=60 << 20
        ),
        name="reduce_grads",
    )(*lefts, *rights, *smalls)
    return [w.reshape(-1, w.shape[-1]).astype(F32) for w in found[:-1]], found[-1]


def reduce_plain(pairs, small):
    small = pack_sums(small, lax.axis_size("shard"))
    grads = []
    for left, right in pairs:
        full = lax.dot_general(left, right, (((0,), (0,)), ((), ())), preferred_element_type=F32)
        part = lax.psum_scatter(full.astype(BF), "shard", scatter_dimension=0, tiled=True)
        grads.append(lax.psum(part, "rep").astype(F32))
    summed = lax.psum(small.astype(BF), ("rep", "shard")).astype(F32)
    width = small.shape[1] // lax.axis_size("shard")
    return grads, lax.dynamic_slice_in_dim(summed, lax.axis_index("shard") * width, width, 1)


def swap_kernel(n, x_ref, o_ref, ssem, rsem):
    rep = lax.axis_index("rep")
    barrier = pltpu.get_barrier_semaphore()
    for d in range(1, n):
        pl.semaphore_signal(
            barrier, inc=1, device_id={"rep": jnp.bitwise_xor(rep, d)}, device_id_type=MESH
        )
    pl.semaphore_wait(barrier, n - 1)
    copies = []
    for d in range(1, n):
        other = jnp.bitwise_xor(rep, d)
        copy = pltpu.make_async_remote_copy(
            src_ref=x_ref.at[other],
            dst_ref=o_ref.at[rep],
            send_sem=ssem.at[d],
            recv_sem=rsem.at[d],
            device_id={"rep": other},
            device_id_type=MESH,
        )
        copy.start()
        copies.append(copy)
    o_ref[rep] = x_ref[rep]
    for copy in copies:
        copy.wait()


def swap(array, which):
    n = array.shape[0]
    return pl.pallas_call(
        functools.partial(swap_kernel, n),
        out_shape=jax.ShapeDtypeStruct(array.shape, array.dtype),
        in_specs=[VM],
        out_specs=VM,
        scratch_shapes=[pltpu.SemaphoreType.DMA((n,)), pltpu.SemaphoreType.DMA((n,))],
        compiler_params=pltpu.CompilerParams(
            collective_id=2 + which, has_side_effects=True, vmem_limit_bytes=32 << 20
        ),
        name="swap_%d" % which,
    )(array)


def to_heads(arrays, n):
    batch, local, features = arrays[0].shape
    parts = [a.reshape(batch, local, n, features // n) for a in arrays]
    stacked = jnp.stack([jnp.transpose(p, (2, 0, 1, 3)) for p in parts], axis=1)
    return stacked


def from_positions(swapped):
    n, k, batch, local, width = swapped.shape
    return [
        jnp.transpose(swapped[:, i], (1, 0, 2, 3)).reshape(batch, n * local, width)
        for i in range(k)
    ]


def to_positions(arrays, n):
    batch, total, width = arrays[0].shape
    parts = [
        jnp.transpose(a.reshape(batch, n, total // n, width), (1, 0, 2, 3)) for a in arrays
    ]
    return jnp.stack(parts, axis=1)


def from_heads(swapped):
    n, k, batch, local, width = swapped.shape
    return [
        jnp.transpose(swapped[:, i], (1, 2, 0, 3)).reshape(batch * local, n * width)
        for i in range(k)
    ]


QROWS = 128


def head_mask(shape, head):
    lane = lax.broadcasted_iota(jnp.int32, shape, 1)
    return jnp.logical_and(lane >= head * HD, lane < (head + 1) * HD)


def spread_bias(bias, spread, block):
    wide = bias.shape[1]
    lane = lax.broadcasted_iota(jnp.int32, (128, wide), 1)
    bias[...] = jnp.where(lane < (block + 1) * 128, spread[:, 0:1], spread[:, 383:384])
    rolled = pltpu.roll(spread, 0, 1, stride=1, stride_axis=0)
    bias[:, pl.ds(pl.multiple_of(block * 128, 128), 384)] = rolled[:, 0:384]


def forward_kernel(q_ref, k_ref, v_ref, table_ref, mixed_ref, lse_ref, bias):
    step = pl.program_id(1)
    total, width = (k_ref.shape[1], k_ref.shape[2])
    heads = width // HD
    keys = k_ref[0]
    values = v_ref[0]
    ones = jnp.ones((total, 128), BF)
    wide_values = jnp.concatenate([values, ones], axis=1) if width == 128 else None
    for sub in range(QROWS // 128):
        rows = slice(sub * 128, (sub + 1) * 128)
        query = q_ref[0, rows, :] * jnp.asarray(0.125, BF)
        block = step * (QROWS // 128) + sub
        for head in range(heads):
            mask = head_mask((128, width), head)
            part = jnp.where(mask, query, jnp.zeros_like(query))
            spread = lax.dot_general(
                part, table_ref[...], (((1,), (1,)), ((), ())), preferred_element_type=F32
            )
            spread_bias(bias, spread.astype(BF).astype(F32), block)
            scores = lax.dot_general(
                part, keys, (((1,), (1,)), ((), ())), preferred_element_type=F32
            )
            scores = scores + bias[:, 128 : 128 + total]
            top = jnp.max(scores, axis=1, keepdims=True)
            weight = jnp.exp(scores - top)
            summed = jnp.sum(weight, axis=1, keepdims=True)
            mixed = jnp.dot(weight.astype(BF), values, preferred_element_type=F32) / summed
            logsum = jnp.broadcast_to(top + jnp.log(summed), (128, width))
            if head == 0:
                mixed_ref[0, rows, :] = mixed
                lse_ref[0, rows, :] = logsum
            else:
                mixed_ref[0, rows, :] = jnp.where(mask, mixed, mixed_ref[0, rows, :])
                lse_ref[0, rows, :] = jnp.where(mask, logsum, lse_ref[0, rows, :])


def attention_forward(query, keys, values, table):
    batch, total, width = query.shape
    part = pl.BlockSpec((1, QROWS, width), lambda b, i: (b, i, 0))
    whole = pl.BlockSpec((1, total, width), lambda b, i: (b, 0, 0))
    shape = jax.ShapeDtypeStruct((batch, total, width), F32)
    return pl.pallas_call(
        forward_kernel,
        out_shape=[shape, shape],
        grid=(batch, total // QROWS),
        in_specs=[part, whole, whole, pl.BlockSpec(table.shape, lambda b, i: (0, 0))],
        out_specs=[part, part],
        scratch_shapes=[pltpu.VMEM((128, total + 256), F32)],
        compiler_params=pltpu.CompilerParams(vmem_limit_bytes=32 << 20),
        name="attention_forward",
    )(query, keys, values, table)


def backward_kernel(
    q_ref,
    k_ref,
    v_ref,
    table_ref,
    mixed_ref,
    lse_ref,
    g_ref,
    dq_ref,
    dk_ref,
    dv_ref,
    dtable_ref,
    bias,
    keyx,
    dscore,
    prob,
    dkt,
    dvt,
):
    batch_at, step = (pl.program_id(0), pl.program_id(1))
    total, width = (k_ref.shape[1], k_ref.shape[2])
    heads = width // HD

    @pl.when(jnp.logical_and(batch_at == 0, step == 0))
    def _():
        dtable_ref[...] = jnp.zeros_like(dtable_ref)

    @pl.when(step == 0)
    def _():
        dkt[...] = jnp.zeros_like(dkt)
        dvt[...] = jnp.zeros_like(dvt)
        keyx[:, 0:width] = k_ref[0]
        row = lax.broadcasted_iota(jnp.int32, (total, 128), 0) // 128
        lane = lax.broadcasted_iota(jnp.int32, (total, 128), 1)
        keyx[:, width : width + 128] = (row == lane).astype(BF)
        dscore[:, 0:128] = jnp.zeros((128, 128), BF)
        dscore[:, 128 + total : 256 + total] = jnp.zeros((128, 128), BF)

    keys = k_ref[0]
    values = v_ref[0]
    flip = (
        lax.broadcasted_iota(jnp.int32, (128, 128), 0)
        + lax.broadcasted_iota(jnp.int32, (128, 128), 1)
        == 127
    ).astype(BF)
    lane_at = lax.broadcasted_iota(jnp.int32, (128, 128), 1)
    band_at = lax.broadcasted_iota(jnp.int32, (128, BAND), 1)
    for sub in range(QROWS // 128):
        rows = slice(sub * 128, (sub + 1) * 128)
        block = step * (QROWS // 128) + sub
        query = q_ref[0, rows, :] * jnp.asarray(0.125, BF)
        grad = g_ref[0, rows, :]
        weighed = grad.astype(F32) * mixed_ref[0, rows, :]
        query_t = jnp.transpose(query.astype(F32)).astype(BF)
        grad_t = jnp.transpose(grad.astype(F32)).astype(BF)
        for head in range(heads):
            mask = head_mask((128, width), head)
            lanes = slice(head * HD, (head + 1) * HD)
            part = jnp.where(mask, query, jnp.zeros_like(query))
            grad_part = jnp.where(mask, grad, jnp.zeros_like(grad))
            balance = jnp.sum(jnp.where(mask, weighed, 0.0), axis=1, keepdims=True)
            logsum = lse_ref[0, rows, head * HD : head * HD + 1]
            spread = lax.dot_general(
                part, table_ref[...], (((1,), (1,)), ((), ())), preferred_element_type=F32
            )
            spread_bias(bias, spread.astype(BF).astype(F32), block)
            scores = lax.dot_general(
                part, keys, (((1,), (1,)), ((), ())), preferred_element_type=F32
            )
            chance = jnp.exp(scores + bias[:, 128 : 128 + total] - logsum)
            back = lax.dot_general(
                grad_part, values, (((1,), (1,)), ((), ())), preferred_element_type=F32
            )
            prob[...] = chance.astype(BF)
            dscore[:, 128 : 128 + total] = (chance * (back - balance)).astype(BF)
            score_back = dscore[:, 128 : 128 + total]
            dkt[lanes, :] += jnp.dot(query_t[lanes, :], score_back, preferred_element_type=F32)
            dvt[lanes, :] += jnp.dot(grad_t[lanes, :], prob[...], preferred_element_type=F32)
            wide = jnp.dot(score_back, keyx[...], preferred_element_type=F32)
            sums = wide[:, width : width + 128]
            before = jnp.sum(jnp.where(lane_at < block - 1, sums, 0.0), axis=1, keepdims=True)
            after = jnp.sum(jnp.where(lane_at > block + 1, sums, 0.0), axis=1, keepdims=True)
            near = dscore[:, pl.ds(pl.multiple_of(block * 128, 128), 384)]
            near = jnp.dot(flip, near, preferred_element_type=F32)
            near = jnp.concatenate([near, jnp.zeros((128, BAND - 384), F32)], axis=1)
            near = pltpu.roll(near, BAND - 127, 1, stride=1, stride_axis=0)
            near = jnp.dot(flip, near.astype(BF), preferred_element_type=F32)
            near = near + jnp.where(band_at == 0, before, 0.0)
            near = (near + jnp.where(band_at == 383, after, 0.0)).astype(BF)
            query_back = wide[:, 0:width] + jnp.dot(
                near, table_ref[...], preferred_element_type=F32
            )
            dtable_ref[...] += lax.dot_general(
                near, part, (((0,), (0,)), ((), ())), preferred_element_type=F32
            )
            query_back = (query_back * 0.125).astype(BF)
            if head == 0:
                dq_ref[0, rows, :] = query_back
            else:
                dq_ref[0, rows, :] = jnp.where(mask, query_back, dq_ref[0, rows, :])

    @pl.when(step == pl.num_programs(1) - 1)
    def _():
        dk_ref[0] = jnp.transpose(dkt[...]).astype(BF)
        dv_ref[0] = jnp.transpose(dvt[...]).astype(BF)


def attention_backward(query, keys, values, table, mixed, logsum, grad):
    batch, total, width = query.shape
    part = pl.BlockSpec((1, QROWS, width), lambda b, i: (b, i, 0))
    whole = pl.BlockSpec((1, total, width), lambda b, i: (b, 0, 0))
    fixed = pl.BlockSpec(table.shape, lambda b, i: (0, 0))
    shape = jax.ShapeDtypeStruct((batch, total, width), BF)
    return pl.pallas_call(
        backward_kernel,
        out_shape=[shape, shape, shape, jax.ShapeDtypeStruct(table.shape, F32)],
        grid=(batch, total // QROWS),
        in_specs=[part, whole, whole, fixed, part, part, part],
        out_specs=[part, whole, whole, fixed],
        scratch_shapes=[
            pltpu.VMEM((128, total + 256), F32),
            pltpu.VMEM((total, width + 128), BF),
            pltpu.VMEM((128, total + 256), BF),
            pltpu.VMEM((128, total), BF),
            pltpu.VMEM((width, total), F32),
            pltpu.VMEM((width, total), F32),
        ],
        compiler_params=pltpu.CompilerParams(vmem_limit_bytes=40 << 20),
        name="attention_backward",
    )(query, keys, values, table, mixed, logsum, grad)


def shifted(value, axis, steps):
    count = lax.axis_size(axis)
    leading, last = (max(0, -steps), min(count, count - steps))
    return lax.ppermute(value, axis, [(source, source + steps) for source in range(leading, last)])


def statistics(values):
    centre = jnp.mean(values, axis=-1, keepdims=True)
    centred = values - centre
    spread = jnp.mean(centred * centred, axis=-1, keepdims=True)
    return centre, lax.rsqrt(spread + EPSILON)


def norm(values, gain, shift):
    centre, scale = statistics(values)
    return (values - centre) * scale * gain + shift


def norm_back(values, gain, grad):
    centre, scale = statistics(values)
    hat = (values - centre) * scale
    weighed = grad * gain
    back = (
        weighed
        - jnp.mean(weighed, axis=-1, keepdims=True)
        - hat * jnp.mean(weighed * hat, axis=-1, keepdims=True)
    ) * scale
    return back, jnp.sum(grad * hat, axis=0), jnp.sum(grad, axis=0)


def swish(values):
    return values * jax.nn.sigmoid(values)


def swish_slope(values):
    gate = jax.nn.sigmoid(values)
    return gate * (1.0 + values * (1.0 - gate))


def times(left, right):
    return jnp.dot(left, right, preferred_element_type=F32)


def times_back(left, right):
    return lax.dot_general(left, right, (((1,), (1,)), ((), ())), preferred_element_type=F32)


def column_sum(values):
    return jnp.sum(values.astype(F32), axis=0)


MATRICES = (2, 4, 8, 10, 11, 13, 18, 22, 25, 27)
VECTORS = (0, 1, 5, 6, 7, 9, 12, 14, 16, 17, 20, 21, 23, 24, 28, 29, 30)
OFFSETS = (3, 26)
TABLE_AT = 15
TAPS_AT = 19


SMALLS = VECTORS + OFFSETS + (TAPS_AT, TABLE_AT)


def small_rows(shards):
    width = shards[0].shape[0]
    count = len(VECTORS) + sum(shards[i].shape[0] // width for i in OFFSETS)
    count += shards[TAPS_AT].shape[0] + shards[TABLE_AT].shape[0]
    return -(-count // 16) * 16


def pack_small(shards):
    width = shards[0].shape[0]
    rows = [shards[i].reshape(-1, width) for i in VECTORS + OFFSETS]
    rows.append(shards[TAPS_AT])
    table = shards[TABLE_AT]
    rows.append(jnp.pad(table, ((0, 0), (0, width - table.shape[1]))))
    packed = jnp.concatenate(rows, axis=0)
    return jnp.pad(packed, ((0, small_rows(shards) - packed.shape[0]), (0, 0)))


def unpack_small(gathered, shards):
    n, _, width = gathered.shape
    full = {}
    at = 0
    for i in VECTORS:
        full[i] = gathered[:, at].reshape(n * width).astype(F32)
        at += 1
    for i in OFFSETS:
        count = shards[i].shape[0] // width
        full[i] = gathered[:, at : at + count].reshape(n * width * count).astype(F32)
        at += count
    count = shards[TAPS_AT].shape[0]
    full[TAPS_AT] = jnp.transpose(gathered[:, at : at + count], (1, 0, 2)).reshape(count, -1)
    at += count
    rows, cols = shards[TABLE_AT].shape
    table = gathered[:, at : at + rows, :cols]
    full[TABLE_AT] = jnp.transpose(table, (1, 0, 2)).reshape(rows, n * cols)
    return full


def list_sums(grads, n):
    table = grads[TABLE_AT]
    width = grads[0].shape[0] // n
    parts = jnp.transpose(table.reshape(table.shape[0], n, -1), (1, 0, 2)).reshape(n, -1)
    parts = jnp.pad(parts, ((0, 0), (0, -parts.shape[1] % width))).reshape(n, -1, width)
    parts = jnp.transpose(parts, (1, 0, 2)).reshape(-1, n * width)
    return [grads[i] for i in VECTORS + OFFSETS + (TAPS_AT,)] + [parts]


def pack_sums(smalls, n):
    features = smalls[0].shape[0]
    rows = []
    for a in smalls:
        if a.ndim == 1:
            a = jnp.transpose(a.reshape(n, -1, features // n), (1, 0, 2)).reshape(-1, features)
        rows.append(a)
    return jnp.concatenate(rows, axis=0)


def split_kernel(offset_rows, tap_rows, x_ref, *outs):
    width = x_ref.shape[1]
    at = 0
    for i in range(len(VECTORS)):
        outs[i][...] = x_ref[at, :]
        at += 1
    for i in range(len(OFFSETS)):
        for k in range(offset_rows):
            outs[len(VECTORS) + i][pl.ds(k * width, width)] = x_ref[at, :]
            at += 1
    outs[len(VECTORS) + len(OFFSETS)][...] = x_ref[at : at + tap_rows, :]


def split_sums(summed, shards):
    width = summed.shape[1]
    order = VECTORS + OFFSETS + (TAPS_AT,)
    offset_rows = shards[OFFSETS[0]].shape[0] // width
    tap_rows = shards[TAPS_AT].shape[0]
    if width % 128 == 0:
        parts = pl.pallas_call(
            functools.partial(split_kernel, offset_rows, tap_rows),
            out_shape=[jax.ShapeDtypeStruct(shards[i].shape, F32) for i in order],
            in_specs=[VM],
            out_specs=[VM] * len(order),
            name="split_sums",
        )(summed)
        at = sum(shards[i].size for i in order) // width
    else:
        parts, at = ([], 0)
        for i in order:
            count = shards[i].size // width
            parts.append(summed[at : at + count].reshape(shards[i].shape))
            at += count
    found = dict(zip(order, parts))
    table = shards[TABLE_AT]
    found[TABLE_AT] = summed[at:].reshape(-1)[: table.size].reshape(table.shape)
    return found


def feed_forward(entering, gain, shift, widen, offset, narrow, bias):
    normed = norm(entering, gain, shift).astype(BF)
    act = times(normed, widen) + offset
    hidden = swish(act).astype(BF)
    return entering + 0.5 * (times(hidden, narrow) + bias), (normed, act, hidden)


def feed_backward(entering, gain, widen, narrow, saved, out_grad):
    normed, act, hidden = saved
    out_low = (0.5 * out_grad).astype(BF)
    act_grad = (times_back(out_low, narrow) * swish_slope(act)).astype(BF)
    normed_grad = times_back(act_grad, widen)
    back, grad_gain, grad_shift = norm_back(entering, gain, normed_grad)
    return (
        out_grad + back,
        (grad_gain, grad_shift, column_sum(act_grad), column_sum(out_low)),
        [(hidden, out_low), (normed, act_grad)],
    )


def sigmoid(values):
    return 1.0 / (1.0 + jnp.exp(-values))


def conv_forward_kernel(doubled_ref, rim_ref, taps_ref, gain_ref, shift_ref, depth_ref, acted_ref, padded):
    local, features = (depth_ref.shape[1], depth_ref.shape[2])
    rim = rim_ref.shape[1]
    taps = taps_ref.shape[0]
    padded[32 - rim : 32, :] = rim_ref[0].astype(F32)

    def gate_rows(i, carry):
        rows = pl.ds(pl.multiple_of(i * 32, 32), 32)
        both = doubled_ref[0, rows, :]
        padded[pl.ds(pl.multiple_of(32 + i * 32, 32), 32), :] = both[:, :features] * sigmoid(
            both[:, features:]
        )
        return carry

    lax.fori_loop(0, local // 32, gate_rows, 0)

    def columns(i, carry):
        cols = pl.ds(pl.multiple_of(i * 128, 128), 128)
        first = 32 - (taps - 1)
        total = padded[first : first + local, cols] * taps_ref[0:1, cols]
        for j in range(1, taps):
            total = total + padded[first + j : first + j + local, cols] * taps_ref[j : j + 1, cols]
        depth_ref[0, :, cols] = total
        return carry

    lax.fori_loop(0, features // 128, columns, 0)

    def norm_rows(i, carry):
        rows = pl.ds(pl.multiple_of(i * 32, 32), 32)
        normed = norm(depth_ref[0, rows, :], gain_ref[...], shift_ref[...])
        acted_ref[0, rows, :] = (normed * sigmoid(normed)).astype(BF)
        return carry

    lax.fori_loop(0, local // 32, norm_rows, 0)


def block_spec(shape):
    return pl.BlockSpec((1,) + shape[1:], lambda b: (b,) + (0,) * (len(shape) - 1))


def fixed_spec(shape):
    return pl.BlockSpec(shape, lambda b: (0,) * len(shape))


def conv_forward(doubled, rim_in, taps, gain, shift):
    batch, local, features = (doubled.shape[0], doubled.shape[1], taps.shape[1])
    shape = (batch, local, features)
    return pl.pallas_call(
        conv_forward_kernel,
        out_shape=[jax.ShapeDtypeStruct(shape, F32), jax.ShapeDtypeStruct(shape, BF)],
        grid=(batch,),
        in_specs=[
            block_spec(doubled.shape),
            block_spec(rim_in.shape),
            fixed_spec(taps.shape),
            fixed_spec(gain.shape),
            fixed_spec(shift.shape),
        ],
        out_specs=[block_spec(shape), block_spec(shape)],
        scratch_shapes=[pltpu.VMEM((32 + local, features), F32)],
        compiler_params=pltpu.CompilerParams(vmem_limit_bytes=32 << 20),
        name="conv_forward",
    )(doubled, rim_in, taps, gain, shift)


def depth_backward_kernel(depth_ref, grad_ref, gain_ref, shift_ref, back_ref, sums_ref):
    local = depth_ref.shape[1]

    @pl.when(pl.program_id(0) == 0)
    def _():
        sums_ref[...] = jnp.zeros_like(sums_ref)

    def body(i, carry):
        rows = pl.ds(pl.multiple_of(i * 32, 32), 32)
        values = depth_ref[0, rows, :]
        centre, scale = statistics(values)
        hat = (values - centre) * scale
        gain = gain_ref[...]
        normed = hat * gain + shift_ref[...]
        gate = sigmoid(normed)
        grad = grad_ref[0, rows, :] * gate * (1.0 + normed * (1.0 - gate))
        weighed = grad * gain
        back_ref[0, rows, :] = (
            weighed
            - jnp.mean(weighed, axis=-1, keepdims=True)
            - hat * jnp.mean(weighed * hat, axis=-1, keepdims=True)
        ) * scale
        sums_ref[0:1, :] += jnp.sum(grad * hat, axis=0, keepdims=True)
        sums_ref[1:2, :] += jnp.sum(grad, axis=0, keepdims=True)
        return carry

    lax.fori_loop(0, local // 32, body, 0)


def depth_backward(depth, grad, gain, shift):
    return pl.pallas_call(
        depth_backward_kernel,
        out_shape=[
            jax.ShapeDtypeStruct(depth.shape, F32),
            jax.ShapeDtypeStruct((8, depth.shape[2]), F32),
        ],
        grid=(depth.shape[0],),
        in_specs=[
            block_spec(depth.shape),
            block_spec(grad.shape),
            fixed_spec(gain.shape),
            fixed_spec(shift.shape),
        ],
        out_specs=[block_spec(depth.shape), fixed_spec((8, depth.shape[2]))],
        compiler_params=pltpu.CompilerParams(vmem_limit_bytes=32 << 20),
        name="depth_backward",
    )(depth, grad, gain, shift)


def conv_backward_kernel(
    back_ref, after_ref, doubled_ref, rim_ref, taps_ref, out_ref, dtaps_ref, padded, behind
):
    local, features = (back_ref.shape[1], back_ref.shape[2])
    rim = rim_ref.shape[1]
    taps = taps_ref.shape[0]

    @pl.when(pl.program_id(0) == 0)
    def _():
        dtaps_ref[...] = jnp.zeros_like(dtaps_ref)

    padded[32 - rim : 32, :] = rim_ref[0].astype(F32)
    behind[local : local + rim, :] = after_ref[0].astype(F32)

    def gate_rows(i, carry):
        rows = pl.ds(pl.multiple_of(i * 32, 32), 32)
        both = doubled_ref[0, rows, :]
        padded[pl.ds(pl.multiple_of(32 + i * 32, 32), 32), :] = both[:, :features] * sigmoid(
            both[:, features:]
        )
        behind[rows, :] = back_ref[0, rows, :]
        return carry

    lax.fori_loop(0, local // 32, gate_rows, 0)

    def columns(i, carry):
        cols = pl.ds(pl.multiple_of(i * 128, 128), 128)
        first = 32 - (taps - 1)
        own = back_ref[0, :, cols]
        total = own * taps_ref[taps - 1 : taps, cols]
        dtaps_ref[taps - 1 : taps, cols] += jnp.sum(
            own * padded[first + taps - 1 : first + taps - 1 + local, cols], axis=0, keepdims=True
        )
        for j in range(taps - 1):
            ahead = taps - 1 - j
            total = total + behind[ahead : ahead + local, cols] * taps_ref[j : j + 1, cols]
            dtaps_ref[j : j + 1, cols] += jnp.sum(
                own * padded[first + j : first + j + local, cols], axis=0, keepdims=True
            )
        side = doubled_ref[0, :, cols]
        gate = sigmoid(doubled_ref[0, :, pl.ds(pl.multiple_of(features + i * 128, 128), 128)])
        gated = total * gate
        out_ref[0, :, cols] = gated.astype(BF)
        out_ref[0, :, pl.ds(pl.multiple_of(features + i * 128, 128), 128)] = (
            gated * side * (1.0 - gate)
        ).astype(BF)
        return carry

    lax.fori_loop(0, features // 128, columns, 0)


def conv_backward(back, after, doubled, rim_in, taps):
    batch, local, features = back.shape
    padded_taps = (-(-taps.shape[0] // 8) * 8, features)
    found, dtaps = pl.pallas_call(
        conv_backward_kernel,
        out_shape=[
            jax.ShapeDtypeStruct(doubled.shape, BF),
            jax.ShapeDtypeStruct(padded_taps, F32),
        ],
        grid=(batch,),
        in_specs=[
            block_spec(back.shape),
            block_spec(after.shape),
            block_spec(doubled.shape),
            block_spec(rim_in.shape),
            fixed_spec(taps.shape),
        ],
        out_specs=[block_spec(doubled.shape), fixed_spec(padded_taps)],
        scratch_shapes=[
            pltpu.VMEM((32 + local, features), F32),
            pltpu.VMEM((32 + local, features), F32),
        ],
        compiler_params=pltpu.CompilerParams(vmem_limit_bytes=32 << 20),
        name="conv_backward",
    )(back, after, doubled, rim_in, taps)
    return found, dtaps[: taps.shape[0]]


def on_device(*arguments):
    inputs, shards, cotangent = (arguments[0], arguments[1:32], arguments[32])
    n_rep, n_shard = (lax.axis_size("rep"), lax.axis_size("shard"))
    micro, local, seqs, features = inputs.shape
    batch = micro * seqs
    fast = (
        n_rep == 8
        and n_shard == 4
        and features == 1024
        and batch * local == 256
        and all(shards[i].shape[0] % 256 == 0 for i in MATRICES)
    )

    def rows_of(array):
        return jnp.transpose(array, (0, 2, 1, 3)).reshape(batch * local, features)

    def whole_of(rows):
        return jnp.transpose(rows.reshape(micro, seqs, local, features), (0, 2, 1, 3))

    if fast:
        smalls = [shards[i] for i in SMALLS]
        full, gathered = gather_fast([shards[i] for i in MATRICES], smalls, small_rows(shards))
    else:
        small = pack_small(shards)
        full = [lax.all_gather(shards[i], "shard", axis=0, tiled=True) for i in MATRICES]
        gathered = lax.all_gather(small, "shard", axis=0, tiled=False)
    w = dict(zip(MATRICES, full))
    w.update(unpack_small(gathered, shards))

    level0 = rows_of(inputs).astype(F32)
    level1, early = feed_forward(level0, w[0], w[1], w[2], w[3], w[4], w[5])

    attend_in = norm(level1, w[6], w[7]).astype(BF)
    query = (times(attend_in, w[8]) + w[9]).astype(BF).reshape(batch, local, features)
    keys = times(attend_in, w[10]).astype(BF).reshape(batch, local, features)
    values = (times(attend_in, w[11]) + w[12]).astype(BF).reshape(batch, local, features)
    query_h, keys_h, values_h = from_positions(swap(to_heads([query, keys, values], n_rep), 0))
    place = jnp.clip(jnp.arange(BAND) - 64, 0, TABLE - 1)
    place = jnp.where(jnp.arange(BAND) >= 384, 0, place)
    table = w[TABLE_AT]
    spread_table = jnp.tile(jnp.take(table, place, axis=0), (1, query_h.shape[2] // HD))
    mixed_h, logsum = attention_forward(query_h, keys_h, values_h, spread_table)
    mixed = from_heads(swap(to_positions([mixed_h.astype(BF)], n_rep), 1))[0]
    level2 = level1 + times(mixed, w[13]) + w[14]

    conv_in = norm(level2, w[16], w[17]).astype(BF)
    doubled = times(conv_in, w[18])
    doubled = doubled.reshape(batch, local, 2 * features)
    taps = w[TAPS_AT].astype(F32)
    rim = taps.shape[0] - 1
    edge = doubled[:, local - rim :]
    edge = (edge[:, :, :features] * jax.nn.sigmoid(edge[:, :, features:])).astype(BF)
    rim_in = shifted(edge, "rep", 1)
    depth, acted = conv_forward(doubled, rim_in, taps, w[20][None], w[21][None])
    acted = acted.reshape(batch * local, features)
    level3 = level2 + times(acted, w[22])

    level4, later = feed_forward(level3, w[23], w[24], w[25], w[26], w[27], w[28])
    output = norm(level4, w[29], w[30]).astype(BF)

    grads = {}
    incoming = rows_of(cotangent).astype(F32)
    back4, grads[29], grads[30] = norm_back(level4, w[29], incoming)
    back3, found, later_pairs = feed_backward(level3, w[23], w[25], w[27], later, back4)
    grads[23], grads[24], grads[26], grads[28] = found

    conv_out = back3.astype(BF)
    acted_grad = times_back(conv_out, w[22]).reshape(batch, local, features)
    depth_back, sums = depth_backward(depth, acted_grad, w[20][None], w[21][None])
    grads[20], grads[21] = (sums[0], sums[1])
    after = shifted(depth_back[:, :rim].astype(BF), "rep", -1)
    doubled_back, grads[TAPS_AT] = conv_backward(depth_back, after, doubled, rim_in, taps)
    doubled_back = doubled_back.reshape(batch * local, 2 * features)
    conv_back = times_back(doubled_back, w[18])
    back, grads[16], grads[17] = norm_back(level2, w[16], conv_back)
    back2 = back3 + back

    mixer_out = back2.astype(BF)
    grads[14] = column_sum(mixer_out)
    mixed_back = times_back(mixer_out, w[13]).astype(BF).reshape(batch, local, features)
    grad_h = from_positions(swap(to_heads([mixed_back], n_rep), 2))[0]
    query_b, keys_b, values_b, table_b = attention_backward(
        query_h, keys_h, values_h, spread_table, mixed_h, logsum, grad_h
    )
    query_back, key_back, value_back = from_heads(
        swap(to_positions([query_b, keys_b, values_b], n_rep), 3)
    )
    folded = table_b.reshape(BAND, -1, HD).sum(axis=1)
    grads[TABLE_AT] = jnp.concatenate(
        [
            (folded[0:65].sum(axis=0) + folded[384:].sum(axis=0))[None],
            folded[65:136],
            folded[136:384].sum(axis=0)[None],
        ]
    )
    grads[9] = column_sum(query_back)
    grads[12] = column_sum(value_back)
    attend_back = (
        times_back(query_back, w[8]) + times_back(key_back, w[10]) + times_back(value_back, w[11])
    )
    back, grads[6], grads[7] = norm_back(level1, w[6], attend_back)
    back1 = back2 + back
    back0, found, early_pairs = feed_backward(level0, w[0], w[2], w[4], early, back1)
    grads[0], grads[1], grads[3], grads[5] = found

    pairs = (
        (27, later_pairs[0]),
        (25, later_pairs[1]),
        (22, (acted, conv_out)),
        (18, (conv_in, doubled_back)),
        (13, (mixed, mixer_out)),
        (8, (attend_in, query_back)),
        (10, (attend_in, key_back)),
        (11, (attend_in, value_back)),
        (4, early_pairs[0]),
        (2, early_pairs[1]),
    )
    reduce = reduce_fast if fast else reduce_plain
    matrices, smalls = reduce([pair for _, pair in pairs], list_sums(grads, n_shard))
    summed = dict(zip([i for i, _ in pairs], matrices))
    summed.update(split_sums(smalls, shards))
    return (whole_of(output), whole_of(back0)) + tuple(summed[i] for i in range(31))


def solution(mesh):
    rows, vector, matrix = (P(None, "rep", "shard", None), P("shard"), P("shard", None))
    columns = P(None, "shard")
    weights = tuple(
        matrix if i in MATRICES else columns if i in (TABLE_AT, TAPS_AT) else vector
        for i in range(31)
    )
    return jax.shard_map(
        on_device,
        mesh=mesh,
        in_specs=(rows,) + weights + (rows,),
        out_specs=(rows, rows) + weights,
        check_vma=False,
    )
```

```python
import functools

import jax
import jax.numpy as jnp
from jax import lax
from jax.experimental import pallas as pl
from jax.experimental.pallas import tpu as pltpu
from jax.sharding import PartitionSpec as P

H = 16
HD = 64
LEFT = 64
RIGHT = 8
TABLE = 73
EPSILON = 1e-05
BAND = 512
MESH = pl.DeviceIdType.MESH
BF = jnp.bfloat16
F32 = jnp.float32
ANY = pl.BlockSpec(memory_space=pltpu.HBM)
VM = pl.BlockSpec(memory_space=pltpu.VMEM)


def here():
    rep = lax.axis_index("rep")
    z = lax.axis_index("shard")
    core = lax.rem(rep, 2)
    x = lax.rem(rep // 2, 2)
    y = rep // 4
    z0 = lax.rem(z, 2)
    z1 = z // 2
    peers = {
        "z1": (rep, lax.rem(z + 2, 4)),
        "z0": (rep, z + 1 - 2 * z0),
        "zz": (rep, 3 - z),
        "x": (rep + 2 - 4 * x, z),
        "y": (rep + 4 - 8 * y, z),
        "c": (rep + 1 - 2 * core, z),
    }
    return z, core, x, y, z0, z1, peers


def meet(peers):
    barrier = pltpu.get_barrier_semaphore()
    for name in peers:
        pl.semaphore_signal(barrier, inc=1, device_id=peers[name], device_id_type=MESH)
    pl.semaphore_wait(barrier, len(peers))


GATHER_LAG = (0, 1, 2, 3, 4)


def fill_rows(packed, smalls):
    width = packed.shape[1]
    packed[...] = jnp.zeros_like(packed)
    at = 0
    for ref in smalls:
        if len(ref.shape) == 1:
            for k in range(ref.shape[0] // width):
                packed[at, :] = ref[pl.ds(k * width, width)].astype(F32)
                at += 1
        else:
            packed[at : at + ref.shape[0], 0 : ref.shape[1]] = ref[...].astype(F32)
            at += ref.shape[0]


def gather_kernel(chunks, n_arr, n_small, *refs):
    ins, smalls = (refs[:n_arr], refs[n_arr : n_arr + n_small])
    refs = refs[n_arr + n_small :]
    outs, small_out = (refs[:n_arr], refs[n_arr])
    ssem, rsem, lsem, lsem2, qsem, psem, packed, small = refs[n_arr + 1 : n_arr + 9]
    bufs = refs[n_arr + 9 :]
    z, core, x, y, z0, z1, peers = here()
    far = ((slice(None), 1 - z0), (1 - z1, z0))
    meet(peers)
    sent = []

    def send(c, slot, src, dst, to):
        copy = pltpu.make_async_remote_copy(
            src_ref=src,
            dst_ref=dst,
            send_sem=ssem.at[c, slot],
            recv_sem=rsem.at[c, slot],
            device_id=peers[to],
            device_id_type=MESH,
        )
        copy.start()
        sent.append(copy)
        return copy

    around = []
    state = {}

    def place(c):
        array, first, count = chunks[c]
        return (ins[array], outs[array], pl.ds(first, count))

    def wait(c, key):
        for copy in state[c, key]:
            copy.wait_recv()

    def stage_z(c):
        src, out, cols = place(c)
        src = src.at[y, x, core, :, :, cols]
        dst = out.at[z1, z0, y, x, core, :, :, cols]
        state[c, "z1"] = [send(c, 0, src, dst, "z1")]
        state[c, "z0"] = [send(c, 1, src, dst, "z0")]

    def stage_zz(c):
        _, out, cols = place(c)
        wait(c, "z1")
        view = out.at[1 - z1, z0, y, x, core, :, :, cols]
        state[c, "z0"].append(send(c, 2, view, view, "z0"))

    def stage_one(c):
        _, out, cols = place(c)
        wait(c, "z0")
        state[c, "one"] = []
        for i, (a, b) in enumerate(far):
            view = out.at[a, b, y, x, core, 0, :, cols]
            state[c, "one"].append(send(c, 3 + i, view, view, "x"))
            view = out.at[a, b, y, x, core, 1, :, cols]
            state[c, "one"].append(send(c, 5 + i, view, view, "y"))

    def stage_two(c):
        _, out, cols = place(c)
        wait(c, "one")
        state[c, "two"] = []
        for i, (a, b) in enumerate(far):
            view = out.at[a, b, y, :, core, 0, :, cols]
            state[c, "two"].append(send(c, 7 + i, view, view, "y"))
            view = out.at[a, b, :, x, core, 1, :, cols]
            state[c, "two"].append(send(c, 9 + i, view, view, "x"))

    def stage_core(c):
        _, out, cols = place(c)
        wait(c, "two")
        state[c, "core"] = []
        for i, (a, b) in enumerate(far):
            view = out.at[a, b, :, :, core, :, :, cols]
            state[c, "core"].append(send(c, 11 + i, view, view, "c"))

    stages = (stage_z, stage_zz, stage_one, stage_two, stage_core)
    local = []
    for step in range(len(chunks) + GATHER_LAG[-1]):
        for stage, lag in zip(stages, GATHER_LAG):
            if 0 <= step - lag < len(chunks):
                stage(step - lag)
        if step == 0:
            for a in range(n_arr):
                copy = pltpu.make_async_copy(ins[a], bufs[a], lsem.at[a])
                copy.start()
                local.append(copy)
            fill_rows(packed, smalls)
            small[...] = packed[...].astype(BF)
            for k, to in enumerate(("z0", "z1", "zz")):
                copy = pltpu.make_async_remote_copy(
                    src_ref=small,
                    dst_ref=small_out.at[z],
                    send_sem=qsem.at[k],
                    recv_sem=psem.at[k],
                    device_id=peers[to],
                    device_id_type=MESH,
                )
                copy.start()
                around.append(copy)
            small_own = pltpu.make_async_copy(small, small_out.at[z], lsem.at[n_arr])
            small_own.start()
        if step == 2:
            for a in range(n_arr):
                local[a].wait()
                copy = pltpu.make_async_copy(bufs[a], outs[a].at[z1, z0], lsem2.at[a])
                copy.start()
                local[a] = copy
    for c in range(len(chunks)):
        wait(c, "core")
    for copy in sent + around:
        copy.wait_send()
    for copy in around:
        copy.wait_recv()
    small_own.wait()
    for copy in local:
        copy.wait()


def gather_chunks(shapes):
    chunks = []
    for i, (rows, cols) in enumerate(shapes):
        for first in range(0, cols, 1024 * 256 // rows):
            chunks.append((i, first, 1024 * 256 // rows))
    return chunks


def gather_fast(shards, smalls, rows):
    count, width = (len(shards), smalls[0].shape[0])
    ins = [w.reshape(2, 2, 2, 2, w.shape[0] // 16, w.shape[1]) for w in shards]
    chunks = gather_chunks([w.shape for w in shards])
    outs = [jax.ShapeDtypeStruct((2, 2) + w.shape, w.dtype) for w in ins]
    outs.append(jax.ShapeDtypeStruct((4, rows, width), BF))
    dma = pltpu.SemaphoreType.DMA
    found = pl.pallas_call(
        functools.partial(gather_kernel, chunks, count, len(smalls)),
        out_shape=outs,
        in_specs=[ANY] * count + [VM] * len(smalls),
        out_specs=[ANY] * (count + 1),
        scratch_shapes=[
            dma((len(chunks), 13)),
            dma((len(chunks), 13)),
            dma((count + 1,)),
            dma((count,)),
            dma((3,)),
            dma((3,)),
            pltpu.VMEM((rows, width), F32),
            pltpu.VMEM((rows, width), BF),
        ]
        + [pltpu.VMEM(w.shape, w.dtype) for w in ins],
        compiler_params=pltpu.CompilerParams(
            collective_id=0, has_side_effects=True, vmem_limit_bytes=58 << 20
        ),
        name="gather_weights",
    )(*ins, *smalls)
    return [w.reshape(-1, w.shape[-1]) for w in found[:count]], found[count]


def fill_sums(total, smalls):
    width = total.shape[1] // 4
    total[...] = jnp.zeros_like(total)
    at = 0
    for ref in smalls:
        if len(ref.shape) > 1:
            total[at : at + ref.shape[0], :] = ref[...]
            at += ref.shape[0]
        elif ref.shape[0] == 4 * width:
            total[at, :] = ref[...]
            at += 1
        else:
            each = ref.shape[0] // (4 * width)
            for k in range(each):
                for z in range(4):
                    total[at, pl.ds(z * width, width)] = ref[pl.ds((z * each + k) * width, width)]
                at += 1


REDUCE_LAG = (0, 1, 2, 3, 4, 5, 6, 7)


def reduce_kernel(groups, units, n_left, n_right, n_small, *refs):
    lefts, rights = (refs[:n_left], refs[n_left : n_left + n_right])
    refs = refs[n_left + n_right :]
    smalls, outs, small_out = (refs[:n_small], refs[n_small:-18], refs[-18])
    lbuf, rbuf, sbuf, b1, b2, b3, b4, b5, hop_out, hop_in, hop_total = refs[-17:-6]
    lsem, ssem, rsem, osem, hsem, isem = refs[-6:]
    z, core, x, y, z0, z1, peers = here()
    del peers["zz"]
    meet(peers)

    def remote(u, slot, src, dst, to):
        return pltpu.make_async_remote_copy(
            src_ref=src,
            dst_ref=dst,
            send_sem=ssem.at[u, slot],
            recv_sem=rsem.at[u, slot],
            device_id=peers[to],
            device_id_type=MESH,
        )

    def copy_core(u):
        return [remote(u, 0, sbuf.at[lax.rem(u, 2)], b1.at[u], "c")]

    def copy_first(u):
        return [
            remote(u, 1, b1.at[u, :, :, 0, 1 - x], b2.at[u, 0], "x"),
            remote(u, 2, b1.at[u, :, :, 1, 1 - y], b2.at[u, 1], "y"),
        ]

    def copy_z0(u):
        return [remote(u, 3, b2.at[u, :, :, 1 - z0], b3.at[u], "z0")]

    def copy_z1(u):
        return [remote(u, 4, b3.at[u, :, 1 - z1], b4.at[u], "z1")]

    def copy_second(u):
        return [
            remote(u, 5, b4.at[u, 0, 1 - y], b5.at[u, 0], "y"),
            remote(u, 6, b4.at[u, 1, 1 - x], b5.at[u, 1], "x"),
        ]

    def block(group, k, *at):
        if groups[group][4]:
            return outs[group].at[(k,) + at]
        at = at + (slice(None),) * (5 - len(at))
        return outs[group].at[at + (pl.ds(pl.multiple_of(k * 1024, 1024), 1024),)]

    def copy_own(u, group=0, k=0):
        return [
            pltpu.make_async_copy(b5.at[u, 0], block(group, k, core, 0, x, y), osem.at[u, 0]),
            pltpu.make_async_copy(b5.at[u, 1], block(group, k, core, 1, y, x), osem.at[u, 1]),
        ]

    def spread_second(u, group=0, k=0):
        return [
            remote(u, 7, b5.at[u, 0], block(group, k, core, 0, x, y), "y"),
            remote(u, 8, b5.at[u, 1], block(group, k, core, 1, y, x), "x"),
        ]

    def spread_first(u, group=0, k=0):
        a, b = (block(group, k, core, 0, x), block(group, k, core, 1, y))
        return [remote(u, 9, a, a, "x"), remote(u, 10, b, b, "y")]

    def spread_core(u, group=0, k=0):
        a = block(group, k, core)
        return [remote(u, 11, a, a, "c")]

    def start_out(u, *makers):
        for group, (_, _, first, count, _) in enumerate(groups):

            @pl.when(jnp.logical_and(u >= first, u < first + count))
            def _():
                for make in makers:
                    start(make(u, group, u - first))

    def start(copies):
        for copy in copies:
            copy.start()

    def arrive(copies):
        for copy in copies:
            copy.wait_recv()

    def load(u):
        slot = lax.rem(u, 3)
        for li, ri, first, count, by_rows in groups:

            @pl.when(jnp.logical_and(u >= first, u < first + count))
            def _():
                k = u - first
                for part in range(4):
                    at = pl.multiple_of(part * 1024 + k * 256, 256) if by_rows else part * 256
                    pltpu.make_async_copy(
                        lefts[li].at[:, pl.ds(at, 256)], lbuf.at[slot, part], lsem.at[slot, part]
                    ).start()
                at = 0 if by_rows else pl.multiple_of(k * 1024, 1024)
                pltpu.make_async_copy(
                    rights[ri].at[:, pl.ds(at, 1024)], rbuf.at[slot], lsem.at[slot, 4]
                ).start()

    def product(u, part, half):
        slot = lax.rem(u, 3)
        left = lbuf[slot, part, :, pl.ds(pl.multiple_of(half * 128, 128), 128)]
        return lax.dot_general(
            left, rbuf[slot], (((0,), (0,)), ((), ())), preferred_element_type=F32
        ).reshape(2, 2, 2, 16, 1024)

    load(0)
    load(1)

    def stage_multiply(u):
        slot = lax.rem(u, 3)
        for part in range(4):
            pltpu.make_async_copy(
                lefts[0].at[:, pl.ds(0, 256)], lbuf.at[slot, part], lsem.at[slot, part]
            ).wait()
        pltpu.make_async_copy(
            rights[0].at[:, pl.ds(0, 1024)], rbuf.at[slot], lsem.at[slot, 4]
        ).wait()

        @pl.when(u >= 2)
        def _():
            for copy in copy_core(u - 2):
                copy.wait_send()

        def body(part, carry):
            sbuf[lax.rem(u, 2), part // 2, lax.rem(part, 2)] = product(u, part, 1 - core).astype(BF)
            return carry

        lax.fori_loop(0, 4, body, 0)
        start(copy_core(u))

    def stage_own(u):
        arrive(copy_core(u))

        def body(part, carry):
            a, b = (part // 2, lax.rem(part, 2))
            b1[u, a, b] = (product(u, part, core) + b1[u, a, b].astype(F32)).astype(BF)
            return carry

        lax.fori_loop(0, 4, body, 0)
        start(copy_first(u))

        @pl.when(u + 2 < units)
        def _():
            load(u + 2)

    def stage_first(u):
        arrive(copy_first(u))

        def body(part, carry):
            a, b = (part // 2, lax.rem(part, 2))
            for half, bit in ((0, x), (1, y)):
                b2[u, half, a, b] = (
                    b2[u, half, a, b].astype(F32) + b1[u, a, b, half, bit].astype(F32)
                ).astype(BF)
            return carry

        lax.fori_loop(0, 4, body, 0)
        start(copy_z0(u))

    def stage_z0(u):
        arrive(copy_z0(u))
        for half in range(2):
            for a in range(2):
                b3[u, half, a] = (
                    b3[u, half, a].astype(F32) + b2[u, half, a, z0].astype(F32)
                ).astype(BF)
        start(copy_z1(u))

    def stage_z1(u):
        arrive(copy_z1(u))
        for half in range(2):
            b4[u, half] = (b4[u, half].astype(F32) + b3[u, half, z1].astype(F32)).astype(BF)
        start(copy_second(u))

    def stage_second(u):
        arrive(copy_second(u))
        for half, bit in ((0, y), (1, x)):
            b5[u, half] = (b5[u, half].astype(F32) + b4[u, half, bit].astype(F32)).astype(BF)
        start_out(u, copy_own, spread_second)

    def stage_spread(u):
        arrive(spread_second(u))
        for copy in copy_own(u):
            copy.wait()
        start_out(u, spread_first)

    def stage_core(u):
        arrive(spread_first(u))
        start_out(u, spread_core)

    stages = (
        stage_multiply,
        stage_own,
        stage_first,
        stage_z0,
        stage_z1,
        stage_second,
        stage_spread,
        stage_core,
    )

    hops = ("c", "x", "y", "z0", "z1")

    def hop(k):
        return pltpu.make_async_remote_copy(
            src_ref=hop_out.at[k],
            dst_ref=hop_in.at[k],
            send_sem=hsem.at[k],
            recv_sem=isem.at[k],
            device_id=peers[hops[k]],
            device_id_type=MESH,
        )

    fill_sums(hop_total, smalls)
    hop_out[0] = hop_total[...].astype(BF)
    hop(0).start()

    def stage_hop(k):
        hop(k).wait_recv()
        total = hop_out[k].astype(F32) + hop_in[k].astype(F32)
        if k + 1 < len(hops):
            hop_out[k + 1] = total.astype(BF)
            hop(k + 1).start()
        else:
            width = small_out.shape[1]
            hop_total[...] = total
            small_out[...] = hop_total[:, pl.ds(pl.multiple_of(z * width, width), width)]

    def step(i, carry):
        for k in range(len(hops)):

            @pl.when(i == 2 * k + 1)
            def _():
                stage_hop(k)

        for stage, lag in zip(stages, REDUCE_LAG):
            u = i - lag

            @pl.when(jnp.logical_and(u >= 0, u < units))
            def _():
                stage(u)

        return carry

    lax.fori_loop(0, units + REDUCE_LAG[-1], step, 0)

    def finish(u, carry):
        arrive(spread_core(u))
        for copies in (
            copy_first,
            copy_z0,
            copy_z1,
            copy_second,
            spread_second,
            spread_first,
            spread_core,
        ):
            for copy in copies(u):
                copy.wait_send()

        @pl.when(u >= units - 2)
        def _():
            for copy in copy_core(u):
                copy.wait_send()

        return carry

    lax.fori_loop(0, units, finish, 0)
    for k in range(len(hops)):
        hop(k).wait_send()


def reduce_fast(pairs, smalls):
    lefts, rights, groups, units = ([], [], [], 0)

    def index_of(arrays, array):
        for i, known in enumerate(arrays):
            if known is array:
                return i
        arrays.append(array)
        return len(arrays) - 1

    for left, right in pairs:
        by_rows = left.shape[1] > 1024
        count = left.shape[1] // 1024 if by_rows else right.shape[1] // 1024
        groups.append((index_of(lefts, left), index_of(rights, right), units, count, by_rows))
        units += count
    dma = pltpu.SemaphoreType.DMA
    rows = sum(a.shape[0] if a.ndim > 1 else a.shape[0] // 1024 for a in smalls)
    rows = -(-rows // 16) * 16
    outs = []
    for _, _, _, count, by_rows in groups:
        shape = (count, 2, 2, 2, 2, 16, 1024) if by_rows else (2, 2, 2, 2, 16, count * 1024)
        outs.append(jax.ShapeDtypeStruct(shape, BF))
    found = pl.pallas_call(
        functools.partial(reduce_kernel, groups, units, len(lefts), len(rights), len(smalls)),
        out_shape=outs + [jax.ShapeDtypeStruct((rows, 256), F32)],
        in_specs=[ANY] * (len(lefts) + len(rights)) + [VM] * len(smalls),
        out_specs=[ANY] * len(outs) + [VM],
        scratch_shapes=[
            pltpu.VMEM((3, 4, 256, 256), BF),
            pltpu.VMEM((3, 256, 1024), BF),
            pltpu.VMEM((2, 2, 2, 2, 2, 2, 16, 1024), BF),
            pltpu.VMEM((units, 2, 2, 2, 2, 2, 16, 1024), BF),
            pltpu.VMEM((units, 2, 2, 2, 2, 16, 1024), BF),
            pltpu.VMEM((units, 2, 2, 2, 16, 1024), BF),
            pltpu.VMEM((units, 2, 2, 16, 1024), BF),
            pltpu.VMEM((units, 2, 16, 1024), BF),
            pltpu.VMEM((5, rows, 1024), BF),
            pltpu.VMEM((5, rows, 1024), BF),
            pltpu.VMEM((rows, 1024), F32),
            dma((3, 5)),
            dma((units, 12)),
            dma((units, 12)),
            dma((units, 2)),
            dma((5,)),
            dma((5,)),
        ],
        compiler_params=pltpu.CompilerParams(
            collective_id=1, has_side_effects=True, vmem_limit_bytes=60 << 20
        ),
        name="reduce_grads",
    )(*lefts, *rights, *smalls)
    return [w.reshape(-1, w.shape[-1]).astype(F32) for w in found[:-1]], found[-1]


def reduce_plain(pairs, small):
    small = pack_sums(small, lax.axis_size("shard"))
    grads = []
    for left, right in pairs:
        full = lax.dot_general(left, right, (((0,), (0,)), ((), ())), preferred_element_type=F32)
        part = lax.psum_scatter(full.astype(BF), "shard", scatter_dimension=0, tiled=True)
        grads.append(lax.psum(part, "rep").astype(F32))
    summed = lax.psum(small.astype(BF), ("rep", "shard")).astype(F32)
    width = small.shape[1] // lax.axis_size("shard")
    return grads, lax.dynamic_slice_in_dim(summed, lax.axis_index("shard") * width, width, 1)


def greet(n):
    rep = lax.axis_index("rep")
    others = [jnp.bitwise_xor(rep, d) for d in range(1, n)]
    barrier = pltpu.get_barrier_semaphore()
    for other in others:
        pl.semaphore_signal(barrier, inc=1, device_id={"rep": other}, device_id_type=MESH)
    pl.semaphore_wait(barrier, n - 1)
    return rep, others


def send_all(others, src_of, dst, ssem, rsem):
    copies = []
    for d, other in enumerate(others):
        copy = pltpu.make_async_remote_copy(
            src_ref=src_of(other),
            dst_ref=dst,
            send_sem=ssem.at[d],
            recv_sem=rsem.at[d],
            device_id={"rep": other},
            device_id_type=MESH,
        )
        copy.start()
        copies.append(copy)
    return copies


def to_heads(arrays, n):
    batch, local, features = arrays[0].shape
    parts = [a.reshape(batch, local, n, features // n) for a in arrays]
    stacked = jnp.stack([jnp.transpose(p, (2, 0, 1, 3)) for p in parts], axis=1)
    return stacked


def from_heads(swapped):
    n, k, batch, local, width = swapped.shape
    return [
        jnp.transpose(swapped[:, i], (1, 2, 0, 3)).reshape(batch * local, n * width)
        for i in range(k)
    ]


def head_mask(shape, head):
    lane = lax.broadcasted_iota(jnp.int32, shape, 1)
    return jnp.logical_and(lane >= head * HD, lane < (head + 1) * HD)


def spread_bias(bias, spread, block):
    wide = bias.shape[1]
    lane = lax.broadcasted_iota(jnp.int32, (128, wide), 1)
    bias[...] = jnp.where(lane < (block + 1) * 128, spread[:, 0:1], spread[:, 383:384])
    rolled = pltpu.roll(spread, 0, 1, stride=1, stride_axis=0)
    bias[:, pl.ds(pl.multiple_of(block * 128, 128), 384)] = rolled[:, 0:384]


def forward_kernel(
    x_ref, table_ref, heads_ref, mixed_ref, lse_ref, out_ref, bias, low, ssem, rsem, tsem, usem
):
    batch, _, n, local, width = heads_ref.shape
    total = n * local
    rep, others = greet(n)
    arriving, leaving = ([], [])
    for b in range(batch):
        arriving.append(
            send_all(
                others,
                lambda other: x_ref.at[other, :, b],
                heads_ref.at[b, :, rep],
                ssem.at[b],
                rsem.at[b],
            )
        )
    for b in range(batch):
        for part in range(3):
            heads_ref[b, part, rep] = x_ref[rep, part, b]
    for b in range(batch):
        for copy in arriving[b]:
            copy.wait_recv()

        def one_block(block, carry):
            keys = heads_ref[b, 1].reshape(total, width)
            values = heads_ref[b, 2].reshape(total, width)
            query = heads_ref[b, 0, block] * jnp.asarray(0.125, BF)
            mixed, logsum = (None, None)
            for head in range(width // HD):
                mask = head_mask((128, width), head)
                part = jnp.where(mask, query, jnp.zeros_like(query))
                spread = lax.dot_general(
                    part, table_ref[...], (((1,), (1,)), ((), ())), preferred_element_type=F32
                )
                spread_bias(bias, spread.astype(BF).astype(F32), block)
                scores = lax.dot_general(
                    part, keys, (((1,), (1,)), ((), ())), preferred_element_type=F32
                )
                scores = scores + bias[:, 128 : 128 + total]
                top = jnp.max(scores, axis=1, keepdims=True)
                weight = jnp.exp(scores - top)
                summed = jnp.sum(weight, axis=1, keepdims=True)
                one = jnp.dot(weight.astype(BF), values, preferred_element_type=F32) / summed
                own = jnp.broadcast_to(top + jnp.log(summed), (128, width))
                mixed = one if mixed is None else jnp.where(mask, one, mixed)
                logsum = own if logsum is None else jnp.where(mask, own, logsum)
            mixed_ref[b, block] = mixed
            lse_ref[b, block] = logsum
            low[b, block] = mixed.astype(BF)
            return carry

        lax.fori_loop(0, n, one_block, 0)
        leaving.append(
            send_all(
                others, lambda other: low.at[b, other], out_ref.at[rep, b], tsem.at[b], usem.at[b]
            )
        )
        out_ref[rep, b] = low[b, rep]
    for copies in arriving:
        for copy in copies:
            copy.wait_send()
    for copies in leaving:
        for copy in copies:
            copy.wait()


def attention_forward(stacked, table):
    n, _, batch, local, width = stacked.shape
    shape = jax.ShapeDtypeStruct((batch, n, local, width), F32)
    dma = pltpu.SemaphoreType.DMA
    return pl.pallas_call(
        forward_kernel,
        out_shape=[
            jax.ShapeDtypeStruct((batch, 3, n, local, width), BF),
            shape,
            shape,
            jax.ShapeDtypeStruct((n, batch, local, width), BF),
        ],
        in_specs=[VM, VM],
        out_specs=[VM] * 4,
        scratch_shapes=[
            pltpu.VMEM((128, n * local + 256), F32),
            pltpu.VMEM((batch, n, local, width), BF),
        ]
        + [dma((batch, n - 1))] * 4,
        compiler_params=pltpu.CompilerParams(
            collective_id=2, has_side_effects=True, vmem_limit_bytes=40 << 20
        ),
        name="attention_forward",
    )(stacked, table)


def backward_kernel(
    x_ref,
    heads_ref,
    table_ref,
    mixed_ref,
    lse_ref,
    out_ref,
    dtable_ref,
    grads,
    low,
    bias,
    keyx,
    dscore,
    prob,
    dkt,
    dvt,
    ssem,
    rsem,
    tsem,
    usem,
):
    batch, _, n, local, width = heads_ref.shape
    total = n * local
    rep, others = greet(n)
    arriving, leaving = ([], [])
    for b in range(batch):
        arriving.append(
            send_all(
                others,
                lambda other: x_ref.at[other, 0, b],
                grads.at[b, rep],
                ssem.at[b],
                rsem.at[b],
            )
        )
    dtable_ref[...] = jnp.zeros_like(dtable_ref)
    dscore[:, 0:128] = jnp.zeros((128, 128), BF)
    dscore[:, 128 + total : 256 + total] = jnp.zeros((128, 128), BF)
    row = lax.broadcasted_iota(jnp.int32, (total, 128), 0) // 128
    lane = lax.broadcasted_iota(jnp.int32, (total, 128), 1)
    keyx[:, width : width + 128] = (row == lane).astype(BF)
    flip = (
        lax.broadcasted_iota(jnp.int32, (128, 128), 0)
        + lax.broadcasted_iota(jnp.int32, (128, 128), 1)
        == 127
    ).astype(BF)
    lane_at = lax.broadcasted_iota(jnp.int32, (128, 128), 1)
    band_at = lax.broadcasted_iota(jnp.int32, (128, BAND), 1)
    for b in range(batch):
        grads[b, rep] = x_ref[rep, 0, b]
    for b in range(batch):
        dkt[...] = jnp.zeros_like(dkt)
        dvt[...] = jnp.zeros_like(dvt)
        keyx[:, 0:width] = heads_ref[b, 1].reshape(total, width)
        for copy in arriving[b]:
            copy.wait_recv()

        def one_block(block, carry):
            keys = heads_ref[b, 1].reshape(total, width)
            values = heads_ref[b, 2].reshape(total, width)
            query = heads_ref[b, 0, block] * jnp.asarray(0.125, BF)
            grad = grads[b, block]
            weighed = grad.astype(F32) * mixed_ref[b, block]
            logsums = lse_ref[b, block]
            query_t = jnp.transpose(query.astype(F32)).astype(BF)
            grad_t = jnp.transpose(grad.astype(F32)).astype(BF)
            found = None
            for head in range(width // HD):
                mask = head_mask((128, width), head)
                lanes = slice(head * HD, (head + 1) * HD)
                part = jnp.where(mask, query, jnp.zeros_like(query))
                grad_part = jnp.where(mask, grad, jnp.zeros_like(grad))
                balance = jnp.sum(jnp.where(mask, weighed, 0.0), axis=1, keepdims=True)
                logsum = logsums[:, head * HD : head * HD + 1]
                spread = lax.dot_general(
                    part, table_ref[...], (((1,), (1,)), ((), ())), preferred_element_type=F32
                )
                spread_bias(bias, spread.astype(BF).astype(F32), block)
                scores = lax.dot_general(
                    part, keys, (((1,), (1,)), ((), ())), preferred_element_type=F32
                )
                chance = jnp.exp(scores + bias[:, 128 : 128 + total] - logsum)
                back = lax.dot_general(
                    grad_part, values, (((1,), (1,)), ((), ())), preferred_element_type=F32
                )
                prob[...] = chance.astype(BF)
                dscore[:, 128 : 128 + total] = (chance * (back - balance)).astype(BF)
                score_back = dscore[:, 128 : 128 + total]
                dkt[lanes, :] += jnp.dot(
                    query_t[lanes, :], score_back, preferred_element_type=F32
                )
                dvt[lanes, :] += jnp.dot(grad_t[lanes, :], prob[...], preferred_element_type=F32)
                wide = jnp.dot(score_back, keyx[...], preferred_element_type=F32)
                sums = wide[:, width : width + 128]
                before = jnp.sum(jnp.where(lane_at < block - 1, sums, 0.0), axis=1, keepdims=True)
                after = jnp.sum(jnp.where(lane_at > block + 1, sums, 0.0), axis=1, keepdims=True)
                near = dscore[:, pl.ds(pl.multiple_of(block * 128, 128), 384)]
                near = jnp.dot(flip, near, preferred_element_type=F32)
                near = jnp.concatenate([near, jnp.zeros((128, BAND - 384), F32)], axis=1)
                near = pltpu.roll(near, BAND - 127, 1, stride=1, stride_axis=0)
                near = jnp.dot(flip, near.astype(BF), preferred_element_type=F32)
                near = near + jnp.where(band_at == 0, before, 0.0)
                near = (near + jnp.where(band_at == 383, after, 0.0)).astype(BF)
                query_back = wide[:, 0:width] + jnp.dot(
                    near, table_ref[...], preferred_element_type=F32
                )
                dtable_ref[...] += lax.dot_general(
                    near, part, (((0,), (0,)), ((), ())), preferred_element_type=F32
                )
                found = query_back if found is None else jnp.where(mask, query_back, found)
            low[b, 0, block] = (found * 0.125).astype(BF)
            return carry

        lax.fori_loop(0, n, one_block, 0)
        low[b, 1] = jnp.transpose(dkt[...]).astype(BF).reshape(n, local, width)
        low[b, 2] = jnp.transpose(dvt[...]).astype(BF).reshape(n, local, width)
        leaving.append(
            send_all(
                others,
                lambda other: low.at[b, :, other],
                out_ref.at[rep, :, b],
                tsem.at[b],
                usem.at[b],
            )
        )
        for part in range(3):
            out_ref[rep, part, b] = low[b, part, rep]
    for copies in arriving:
        for copy in copies:
            copy.wait_send()
    for copies in leaving:
        for copy in copies:
            copy.wait()


def attention_backward(stacked, heads, table, mixed, logsum):
    batch, _, n, local, width = heads.shape
    total = n * local
    dma = pltpu.SemaphoreType.DMA
    return pl.pallas_call(
        backward_kernel,
        out_shape=[
            jax.ShapeDtypeStruct((n, 3, batch, local, width), BF),
            jax.ShapeDtypeStruct(table.shape, F32),
        ],
        in_specs=[VM] * 5,
        out_specs=[VM] * 2,
        scratch_shapes=[
            pltpu.VMEM((batch, n, local, width), BF),
            pltpu.VMEM((batch, 3, n, local, width), BF),
            pltpu.VMEM((128, total + 256), F32),
            pltpu.VMEM((total, width + 128), BF),
            pltpu.VMEM((128, total + 256), BF),
            pltpu.VMEM((128, total), BF),
            pltpu.VMEM((width, total), F32),
            pltpu.VMEM((width, total), F32),
        ]
        + [dma((batch, n - 1))] * 4,
        compiler_params=pltpu.CompilerParams(
            collective_id=3, has_side_effects=True, vmem_limit_bytes=48 << 20
        ),
        name="attention_backward",
    )(stacked, heads, table, mixed, logsum)


def shifted(value, axis, steps):
    count = lax.axis_size(axis)
    leading, last = (max(0, -steps), min(count, count - steps))
    return lax.ppermute(value, axis, [(source, source + steps) for source in range(leading, last)])


def statistics(values):
    centre = jnp.mean(values, axis=-1, keepdims=True)
    centred = values - centre
    spread = jnp.mean(centred * centred, axis=-1, keepdims=True)
    return centre, lax.rsqrt(spread + EPSILON)


def norm(values, gain, shift):
    centre, scale = statistics(values)
    return (values - centre) * scale * gain + shift


def norm_back(values, gain, grad):
    centre, scale = statistics(values)
    hat = (values - centre) * scale
    weighed = grad * gain
    back = (
        weighed
        - jnp.mean(weighed, axis=-1, keepdims=True)
        - hat * jnp.mean(weighed * hat, axis=-1, keepdims=True)
    ) * scale
    return back, jnp.sum(grad * hat, axis=0), jnp.sum(grad, axis=0)


def swish(values):
    return values * jax.nn.sigmoid(values)


def swish_slope(values):
    gate = jax.nn.sigmoid(values)
    return gate * (1.0 + values * (1.0 - gate))


def times(left, right):
    return jnp.dot(left, right, preferred_element_type=F32)


def times_back(left, right):
    return lax.dot_general(left, right, (((1,), (1,)), ((), ())), preferred_element_type=F32)


def column_sum(values):
    return jnp.sum(values.astype(F32), axis=0)


MATRICES = (2, 4, 8, 10, 11, 13, 18, 22, 25, 27)
VECTORS = (0, 1, 5, 6, 7, 9, 12, 14, 16, 17, 20, 21, 23, 24, 28, 29, 30)
OFFSETS = (3, 26)
TABLE_AT = 15
TAPS_AT = 19


SMALLS = VECTORS + OFFSETS + (TAPS_AT, TABLE_AT)


def small_rows(shards):
    width = shards[0].shape[0]
    count = len(VECTORS) + sum(shards[i].shape[0] // width for i in OFFSETS)
    count += shards[TAPS_AT].shape[0] + shards[TABLE_AT].shape[0]
    return -(-count // 16) * 16


def pack_small(shards):
    width = shards[0].shape[0]
    rows = [shards[i].reshape(-1, width) for i in VECTORS + OFFSETS]
    rows.append(shards[TAPS_AT])
    table = shards[TABLE_AT]
    rows.append(jnp.pad(table, ((0, 0), (0, width - table.shape[1]))))
    packed = jnp.concatenate(rows, axis=0)
    return jnp.pad(packed, ((0, small_rows(shards) - packed.shape[0]), (0, 0)))


def unpack_small(gathered, shards):
    n, _, width = gathered.shape
    full = {}
    at = 0
    for i in VECTORS:
        full[i] = gathered[:, at].reshape(n * width).astype(F32)
        at += 1
    for i in OFFSETS:
        count = shards[i].shape[0] // width
        full[i] = gathered[:, at : at + count].reshape(n * width * count).astype(F32)
        at += count
    count = shards[TAPS_AT].shape[0]
    full[TAPS_AT] = jnp.transpose(gathered[:, at : at + count], (1, 0, 2)).reshape(count, -1)
    at += count
    rows, cols = shards[TABLE_AT].shape
    table = gathered[:, at : at + rows, :cols]
    full[TABLE_AT] = jnp.transpose(table, (1, 0, 2)).reshape(rows, n * cols)
    return full


def list_sums(grads, n):
    table = grads[TABLE_AT]
    width = grads[0].shape[0] // n
    parts = jnp.transpose(table.reshape(table.shape[0], n, -1), (1, 0, 2)).reshape(n, -1)
    parts = jnp.pad(parts, ((0, 0), (0, -parts.shape[1] % width))).reshape(n, -1, width)
    parts = jnp.transpose(parts, (1, 0, 2)).reshape(-1, n * width)
    return [grads[i] for i in VECTORS + OFFSETS + (TAPS_AT,)] + [parts]


def pack_sums(smalls, n):
    features = smalls[0].shape[0]
    rows = []
    for a in smalls:
        if a.ndim == 1:
            a = jnp.transpose(a.reshape(n, -1, features // n), (1, 0, 2)).reshape(-1, features)
        rows.append(a)
    return jnp.concatenate(rows, axis=0)


def split_kernel(offset_rows, tap_rows, x_ref, *outs):
    width = x_ref.shape[1]
    at = 0
    for i in range(len(VECTORS)):
        outs[i][...] = x_ref[at, :]
        at += 1
    for i in range(len(OFFSETS)):
        for k in range(offset_rows):
            outs[len(VECTORS) + i][pl.ds(k * width, width)] = x_ref[at, :]
            at += 1
    outs[len(VECTORS) + len(OFFSETS)][...] = x_ref[at : at + tap_rows, :]


def split_sums(summed, shards):
    width = summed.shape[1]
    order = VECTORS + OFFSETS + (TAPS_AT,)
    offset_rows = shards[OFFSETS[0]].shape[0] // width
    tap_rows = shards[TAPS_AT].shape[0]
    if width % 128 == 0:
        parts = pl.pallas_call(
            functools.partial(split_kernel, offset_rows, tap_rows),
            out_shape=[jax.ShapeDtypeStruct(shards[i].shape, F32) for i in order],
            in_specs=[VM],
            out_specs=[VM] * len(order),
            name="split_sums",
        )(summed)
        at = sum(shards[i].size for i in order) // width
    else:
        parts, at = ([], 0)
        for i in order:
            count = shards[i].size // width
            parts.append(summed[at : at + count].reshape(shards[i].shape))
            at += count
    found = dict(zip(order, parts))
    table = shards[TABLE_AT]
    found[TABLE_AT] = summed[at:].reshape(-1)[: table.size].reshape(table.shape)
    return found


def feed_forward(entering, gain, shift, widen, offset, narrow, bias):
    normed = norm(entering, gain, shift).astype(BF)
    act = times(normed, widen) + offset
    hidden = swish(act).astype(BF)
    return entering + 0.5 * (times(hidden, narrow) + bias), (normed, act, hidden)


def feed_backward(entering, gain, widen, narrow, saved, out_grad):
    normed, act, hidden = saved
    out_low = (0.5 * out_grad).astype(BF)
    act_grad = (times_back(out_low, narrow) * swish_slope(act)).astype(BF)
    normed_grad = times_back(act_grad, widen)
    back, grad_gain, grad_shift = norm_back(entering, gain, normed_grad)
    return (
        out_grad + back,
        (grad_gain, grad_shift, column_sum(act_grad), column_sum(out_low)),
        [(hidden, out_low), (normed, act_grad)],
    )


def sigmoid(values):
    return 1.0 / (1.0 + jnp.exp(-values))


def conv_forward_kernel(doubled_ref, rim_ref, taps_ref, gain_ref, shift_ref, depth_ref, acted_ref, padded):
    local, features = (depth_ref.shape[1], depth_ref.shape[2])
    rim = rim_ref.shape[1]
    taps = taps_ref.shape[0]
    padded[32 - rim : 32, :] = rim_ref[0].astype(F32)

    def gate_rows(i, carry):
        rows = pl.ds(pl.multiple_of(i * 32, 32), 32)
        both = doubled_ref[0, rows, :]
        padded[pl.ds(pl.multiple_of(32 + i * 32, 32), 32), :] = both[:, :features] * sigmoid(
            both[:, features:]
        )
        return carry

    lax.fori_loop(0, local // 32, gate_rows, 0)

    def columns(i, carry):
        cols = pl.ds(pl.multiple_of(i * 128, 128), 128)
        first = 32 - (taps - 1)
        total = padded[first : first + local, cols] * taps_ref[0:1, cols]
        for j in range(1, taps):
            total = total + padded[first + j : first + j + local, cols] * taps_ref[j : j + 1, cols]
        depth_ref[0, :, cols] = total
        return carry

    lax.fori_loop(0, features // 128, columns, 0)

    def norm_rows(i, carry):
        rows = pl.ds(pl.multiple_of(i * 32, 32), 32)
        normed = norm(depth_ref[0, rows, :], gain_ref[...], shift_ref[...])
        acted_ref[0, rows, :] = (normed * sigmoid(normed)).astype(BF)
        return carry

    lax.fori_loop(0, local // 32, norm_rows, 0)


def block_spec(shape):
    return pl.BlockSpec((1,) + shape[1:], lambda b: (b,) + (0,) * (len(shape) - 1))


def fixed_spec(shape):
    return pl.BlockSpec(shape, lambda b: (0,) * len(shape))


def conv_forward(doubled, rim_in, taps, gain, shift):
    batch, local, features = (doubled.shape[0], doubled.shape[1], taps.shape[1])
    shape = (batch, local, features)
    return pl.pallas_call(
        conv_forward_kernel,
        out_shape=[jax.ShapeDtypeStruct(shape, F32), jax.ShapeDtypeStruct(shape, BF)],
        grid=(batch,),
        in_specs=[
            block_spec(doubled.shape),
            block_spec(rim_in.shape),
            fixed_spec(taps.shape),
            fixed_spec(gain.shape),
            fixed_spec(shift.shape),
        ],
        out_specs=[block_spec(shape), block_spec(shape)],
        scratch_shapes=[pltpu.VMEM((32 + local, features), F32)],
        compiler_params=pltpu.CompilerParams(vmem_limit_bytes=32 << 20),
        name="conv_forward",
    )(doubled, rim_in, taps, gain, shift)


def depth_backward_kernel(depth_ref, grad_ref, gain_ref, shift_ref, back_ref, sums_ref):
    local = depth_ref.shape[1]

    @pl.when(pl.program_id(0) == 0)
    def _():
        sums_ref[...] = jnp.zeros_like(sums_ref)

    def body(i, carry):
        rows = pl.ds(pl.multiple_of(i * 32, 32), 32)
        values = depth_ref[0, rows, :]
        centre, scale = statistics(values)
        hat = (values - centre) * scale
        gain = gain_ref[...]
        normed = hat * gain + shift_ref[...]
        gate = sigmoid(normed)
        grad = grad_ref[0, rows, :] * gate * (1.0 + normed * (1.0 - gate))
        weighed = grad * gain
        back_ref[0, rows, :] = (
            weighed
            - jnp.mean(weighed, axis=-1, keepdims=True)
            - hat * jnp.mean(weighed * hat, axis=-1, keepdims=True)
        ) * scale
        sums_ref[0:1, :] += jnp.sum(grad * hat, axis=0, keepdims=True)
        sums_ref[1:2, :] += jnp.sum(grad, axis=0, keepdims=True)
        return carry

    lax.fori_loop(0, local // 32, body, 0)


def depth_backward(depth, grad, gain, shift):
    return pl.pallas_call(
        depth_backward_kernel,
        out_shape=[
            jax.ShapeDtypeStruct(depth.shape, F32),
            jax.ShapeDtypeStruct((8, depth.shape[2]), F32),
        ],
        grid=(depth.shape[0],),
        in_specs=[
            block_spec(depth.shape),
            block_spec(grad.shape),
            fixed_spec(gain.shape),
            fixed_spec(shift.shape),
        ],
        out_specs=[block_spec(depth.shape), fixed_spec((8, depth.shape[2]))],
        compiler_params=pltpu.CompilerParams(vmem_limit_bytes=32 << 20),
        name="depth_backward",
    )(depth, grad, gain, shift)


def conv_backward_kernel(
    back_ref, after_ref, doubled_ref, rim_ref, taps_ref, out_ref, dtaps_ref, padded, behind
):
    local, features = (back_ref.shape[1], back_ref.shape[2])
    rim = rim_ref.shape[1]
    taps = taps_ref.shape[0]

    @pl.when(pl.program_id(0) == 0)
    def _():
        dtaps_ref[...] = jnp.zeros_like(dtaps_ref)

    padded[32 - rim : 32, :] = rim_ref[0].astype(F32)
    behind[local : local + rim, :] = after_ref[0].astype(F32)

    def gate_rows(i, carry):
        rows = pl.ds(pl.multiple_of(i * 32, 32), 32)
        both = doubled_ref[0, rows, :]
        padded[pl.ds(pl.multiple_of(32 + i * 32, 32), 32), :] = both[:, :features] * sigmoid(
            both[:, features:]
        )
        behind[rows, :] = back_ref[0, rows, :]
        return carry

    lax.fori_loop(0, local // 32, gate_rows, 0)

    def columns(i, carry):
        cols = pl.ds(pl.multiple_of(i * 128, 128), 128)
        first = 32 - (taps - 1)
        own = back_ref[0, :, cols]
        total = own * taps_ref[taps - 1 : taps, cols]
        dtaps_ref[taps - 1 : taps, cols] += jnp.sum(
            own * padded[first + taps - 1 : first + taps - 1 + local, cols], axis=0, keepdims=True
        )
        for j in range(taps - 1):
            ahead = taps - 1 - j
            total = total + behind[ahead : ahead + local, cols] * taps_ref[j : j + 1, cols]
            dtaps_ref[j : j + 1, cols] += jnp.sum(
                own * padded[first + j : first + j + local, cols], axis=0, keepdims=True
            )
        side = doubled_ref[0, :, cols]
        gate = sigmoid(doubled_ref[0, :, pl.ds(pl.multiple_of(features + i * 128, 128), 128)])
        gated = total * gate
        out_ref[0, :, cols] = gated.astype(BF)
        out_ref[0, :, pl.ds(pl.multiple_of(features + i * 128, 128), 128)] = (
            gated * side * (1.0 - gate)
        ).astype(BF)
        return carry

    lax.fori_loop(0, features // 128, columns, 0)


def conv_backward(back, after, doubled, rim_in, taps):
    batch, local, features = back.shape
    padded_taps = (-(-taps.shape[0] // 8) * 8, features)
    found, dtaps = pl.pallas_call(
        conv_backward_kernel,
        out_shape=[
            jax.ShapeDtypeStruct(doubled.shape, BF),
            jax.ShapeDtypeStruct(padded_taps, F32),
        ],
        grid=(batch,),
        in_specs=[
            block_spec(back.shape),
            block_spec(after.shape),
            block_spec(doubled.shape),
            block_spec(rim_in.shape),
            fixed_spec(taps.shape),
        ],
        out_specs=[block_spec(doubled.shape), fixed_spec(padded_taps)],
        scratch_shapes=[
            pltpu.VMEM((32 + local, features), F32),
            pltpu.VMEM((32 + local, features), F32),
        ],
        compiler_params=pltpu.CompilerParams(vmem_limit_bytes=32 << 20),
        name="conv_backward",
    )(back, after, doubled, rim_in, taps)
    return found, dtaps[: taps.shape[0]]


def on_device(*arguments):
    inputs, shards, cotangent = (arguments[0], arguments[1:32], arguments[32])
    n_rep, n_shard = (lax.axis_size("rep"), lax.axis_size("shard"))
    micro, local, seqs, features = inputs.shape
    batch = micro * seqs
    fast = (
        n_rep == 8
        and n_shard == 4
        and features == 1024
        and batch * local == 256
        and all(shards[i].shape[0] % 256 == 0 for i in MATRICES)
    )

    def rows_of(array):
        return jnp.transpose(array, (0, 2, 1, 3)).reshape(batch * local, features)

    def whole_of(rows):
        return jnp.transpose(rows.reshape(micro, seqs, local, features), (0, 2, 1, 3))

    if fast:
        smalls = [shards[i] for i in SMALLS]
        full, gathered = gather_fast([shards[i] for i in MATRICES], smalls, small_rows(shards))
    else:
        small = pack_small(shards)
        full = [lax.all_gather(shards[i], "shard", axis=0, tiled=True) for i in MATRICES]
        gathered = lax.all_gather(small, "shard", axis=0, tiled=False)
    w = dict(zip(MATRICES, full))
    w.update(unpack_small(gathered, shards))

    level0 = rows_of(inputs).astype(F32)
    level1, early = feed_forward(level0, w[0], w[1], w[2], w[3], w[4], w[5])

    attend_in = norm(level1, w[6], w[7]).astype(BF)
    query = (times(attend_in, w[8]) + w[9]).astype(BF).reshape(batch, local, features)
    keys = times(attend_in, w[10]).astype(BF).reshape(batch, local, features)
    values = (times(attend_in, w[11]) + w[12]).astype(BF).reshape(batch, local, features)
    place = jnp.clip(jnp.arange(BAND) - 64, 0, TABLE - 1)
    place = jnp.where(jnp.arange(BAND) >= 384, 0, place)
    table = w[TABLE_AT]
    spread_table = jnp.tile(jnp.take(table, place, axis=0), (1, features // n_rep // HD))
    heads, mixed_h, logsum, mixed = attention_forward(
        to_heads([query, keys, values], n_rep), spread_table
    )
    mixed = from_heads(mixed[:, None])[0]
    level2 = level1 + times(mixed, w[13]) + w[14]

    conv_in = norm(level2, w[16], w[17]).astype(BF)
    doubled = times(conv_in, w[18])
    doubled = doubled.reshape(batch, local, 2 * features)
    taps = w[TAPS_AT].astype(F32)
    rim = taps.shape[0] - 1
    edge = doubled[:, local - rim :]
    edge = (edge[:, :, :features] * jax.nn.sigmoid(edge[:, :, features:])).astype(BF)
    rim_in = shifted(edge, "rep", 1)
    depth, acted = conv_forward(doubled, rim_in, taps, w[20][None], w[21][None])
    acted = acted.reshape(batch * local, features)
    level3 = level2 + times(acted, w[22])

    level4, later = feed_forward(level3, w[23], w[24], w[25], w[26], w[27], w[28])
    output = norm(level4, w[29], w[30]).astype(BF)

    grads = {}
    incoming = rows_of(cotangent).astype(F32)
    back4, grads[29], grads[30] = norm_back(level4, w[29], incoming)
    back3, found, later_pairs = feed_backward(level3, w[23], w[25], w[27], later, back4)
    grads[23], grads[24], grads[26], grads[28] = found

    conv_out = back3.astype(BF)
    acted_grad = times_back(conv_out, w[22]).reshape(batch, local, features)
    depth_back, sums = depth_backward(depth, acted_grad, w[20][None], w[21][None])
    grads[20], grads[21] = (sums[0], sums[1])
    after = shifted(depth_back[:, :rim].astype(BF), "rep", -1)
    doubled_back, grads[TAPS_AT] = conv_backward(depth_back, after, doubled, rim_in, taps)
    doubled_back = doubled_back.reshape(batch * local, 2 * features)
    conv_back = times_back(doubled_back, w[18])
    back, grads[16], grads[17] = norm_back(level2, w[16], conv_back)
    back2 = back3 + back

    mixer_out = back2.astype(BF)
    grads[14] = column_sum(mixer_out)
    mixed_back = times_back(mixer_out, w[13]).astype(BF).reshape(batch, local, features)
    found, table_b = attention_backward(
        to_heads([mixed_back], n_rep), heads, spread_table, mixed_h, logsum
    )
    query_back, key_back, value_back = from_heads(found)
    folded = table_b.reshape(BAND, -1, HD).sum(axis=1)
    grads[TABLE_AT] = jnp.concatenate(
        [
            (folded[0:65].sum(axis=0) + folded[384:].sum(axis=0))[None],
            folded[65:136],
            folded[136:384].sum(axis=0)[None],
        ]
    )
    grads[9] = column_sum(query_back)
    grads[12] = column_sum(value_back)
    attend_back = (
        times_back(query_back, w[8]) + times_back(key_back, w[10]) + times_back(value_back, w[11])
    )
    back, grads[6], grads[7] = norm_back(level1, w[6], attend_back)
    back1 = back2 + back
    back0, found, early_pairs = feed_backward(level0, w[0], w[2], w[4], early, back1)
    grads[0], grads[1], grads[3], grads[5] = found

    pairs = (
        (27, later_pairs[0]),
        (25, later_pairs[1]),
        (22, (acted, conv_out)),
        (18, (conv_in, doubled_back)),
        (13, (mixed, mixer_out)),
        (8, (attend_in, query_back)),
        (10, (attend_in, key_back)),
        (11, (attend_in, value_back)),
        (4, early_pairs[0]),
        (2, early_pairs[1]),
    )
    reduce = reduce_fast if fast else reduce_plain
    matrices, smalls = reduce([pair for _, pair in pairs], list_sums(grads, n_shard))
    summed = dict(zip([i for i, _ in pairs], matrices))
    summed.update(split_sums(smalls, shards))
    return (whole_of(output), whole_of(back0)) + tuple(summed[i] for i in range(31))


def solution(mesh):
    rows, vector, matrix = (P(None, "rep", "shard", None), P("shard"), P("shard", None))
    columns = P(None, "shard")
    weights = tuple(
        matrix if i in MATRICES else columns if i in (TABLE_AT, TAPS_AT) else vector
        for i in range(31)
    )
    return jax.shard_map(
        on_device,
        mesh=mesh,
        in_specs=(rows,) + weights + (rows,),
        out_specs=(rows, rows) + weights,
        check_vma=False,
    )
```

```python
import functools

import jax
import jax.numpy as jnp
from jax import lax
from jax.experimental import pallas as pl
from jax.experimental.pallas import tpu as pltpu
from jax.sharding import PartitionSpec as P

H = 16
HD = 64
LEFT = 64
RIGHT = 8
TABLE = 73
EPSILON = 1e-05
BAND = 512
MESH = pl.DeviceIdType.MESH
BF = jnp.bfloat16
F32 = jnp.float32
ANY = pl.BlockSpec(memory_space=pltpu.HBM)
VM = pl.BlockSpec(memory_space=pltpu.VMEM)


def here():
    rep = lax.axis_index("rep")
    z = lax.axis_index("shard")
    core = lax.rem(rep, 2)
    x = lax.rem(rep // 2, 2)
    y = rep // 4
    z0 = lax.rem(z, 2)
    z1 = z // 2
    peers = {
        "z1": (rep, lax.rem(z + 2, 4)),
        "z0": (rep, z + 1 - 2 * z0),
        "zz": (rep, 3 - z),
        "x": (rep + 2 - 4 * x, z),
        "y": (rep + 4 - 8 * y, z),
        "c": (rep + 1 - 2 * core, z),
    }
    return z, core, x, y, z0, z1, peers


def meet(peers):
    barrier = pltpu.get_barrier_semaphore()
    for name in peers:
        pl.semaphore_signal(barrier, inc=1, device_id=peers[name], device_id_type=MESH)
    pl.semaphore_wait(barrier, len(peers))


GATHER_LAG = (0, 1, 2, 3, 4)


def fill_rows(packed, smalls):
    width = packed.shape[1]
    packed[...] = jnp.zeros_like(packed)
    at = 0
    for ref in smalls:
        if len(ref.shape) == 1:
            for k in range(ref.shape[0] // width):
                packed[at, :] = ref[pl.ds(k * width, width)].astype(F32)
                at += 1
        else:
            packed[at : at + ref.shape[0], 0 : ref.shape[1]] = ref[...].astype(F32)
            at += ref.shape[0]


def gather_kernel(chunks, n_arr, n_small, *refs):
    ins, smalls = (refs[:n_arr], refs[n_arr : n_arr + n_small])
    refs = refs[n_arr + n_small :]
    outs, small_out = (refs[:n_arr], refs[n_arr])
    ssem, rsem, lsem, lsem2, qsem, psem, packed, small = refs[n_arr + 1 : n_arr + 9]
    bufs = refs[n_arr + 9 :]
    z, core, x, y, z0, z1, peers = here()
    far = ((slice(None), 1 - z0), (1 - z1, z0))
    meet(peers)
    sent = []

    def send(c, slot, src, dst, to):
        copy = pltpu.make_async_remote_copy(
            src_ref=src,
            dst_ref=dst,
            send_sem=ssem.at[c, slot],
            recv_sem=rsem.at[c, slot],
            device_id=peers[to],
            device_id_type=MESH,
        )
        copy.start()
        sent.append(copy)
        return copy

    around = []
    state = {}

    def place(c):
        array, first, count = chunks[c]
        return (ins[array], outs[array], pl.ds(first, count))

    def wait(c, key):
        for copy in state[c, key]:
            copy.wait_recv()

    def stage_z(c):
        src, out, cols = place(c)
        src = src.at[y, x, core, :, :, cols]
        dst = out.at[z1, z0, y, x, core, :, :, cols]
        state[c, "z1"] = [send(c, 0, src, dst, "z1")]
        state[c, "z0"] = [send(c, 1, src, dst, "z0")]

    def stage_zz(c):
        _, out, cols = place(c)
        wait(c, "z1")
        view = out.at[1 - z1, z0, y, x, core, :, :, cols]
        state[c, "z0"].append(send(c, 2, view, view, "z0"))

    def stage_one(c):
        _, out, cols = place(c)
        wait(c, "z0")
        state[c, "one"] = []
        for i, (a, b) in enumerate(far):
            view = out.at[a, b, y, x, core, 0, :, cols]
            state[c, "one"].append(send(c, 3 + i, view, view, "x"))
            view = out.at[a, b, y, x, core, 1, :, cols]
            state[c, "one"].append(send(c, 5 + i, view, view, "y"))

    def stage_two(c):
        _, out, cols = place(c)
        wait(c, "one")
        state[c, "two"] = []
        for i, (a, b) in enumerate(far):
            view = out.at[a, b, y, :, core, 0, :, cols]
            state[c, "two"].append(send(c, 7 + i, view, view, "y"))
            view = out.at[a, b, :, x, core, 1, :, cols]
            state[c, "two"].append(send(c, 9 + i, view, view, "x"))

    def stage_core(c):
        _, out, cols = place(c)
        wait(c, "two")
        state[c, "core"] = []
        for i, (a, b) in enumerate(far):
            view = out.at[a, b, :, :, core, :, :, cols]
            state[c, "core"].append(send(c, 11 + i, view, view, "c"))

    stages = (stage_z, stage_zz, stage_one, stage_two, stage_core)
    local = []
    for step in range(len(chunks) + GATHER_LAG[-1]):
        for stage, lag in zip(stages, GATHER_LAG):
            if 0 <= step - lag < len(chunks):
                stage(step - lag)
        if step == 0:
            for a in range(n_arr):
                copy = pltpu.make_async_copy(ins[a], bufs[a], lsem.at[a])
                copy.start()
                local.append(copy)
            fill_rows(packed, smalls)
            small[...] = packed[...].astype(BF)
            for k, to in enumerate(("z0", "z1", "zz")):
                copy = pltpu.make_async_remote_copy(
                    src_ref=small,
                    dst_ref=small_out.at[z],
                    send_sem=qsem.at[k],
                    recv_sem=psem.at[k],
                    device_id=peers[to],
                    device_id_type=MESH,
                )
                copy.start()
                around.append(copy)
            small_own = pltpu.make_async_copy(small, small_out.at[z], lsem.at[n_arr])
            small_own.start()
        if step == 2:
            for a in range(n_arr):
                local[a].wait()
                copy = pltpu.make_async_copy(bufs[a], outs[a].at[z1, z0], lsem2.at[a])
                copy.start()
                local[a] = copy
    for c in range(len(chunks)):
        wait(c, "core")
    for copy in sent + around:
        copy.wait_send()
    for copy in around:
        copy.wait_recv()
    small_own.wait()
    for copy in local:
        copy.wait()


def gather_chunks(shapes):
    chunks = []
    for i, (rows, cols) in enumerate(shapes):
        for first in range(0, cols, 1024 * 256 // rows):
            chunks.append((i, first, 1024 * 256 // rows))
    return chunks


def gather_fast(shards, smalls, rows):
    count, width = (len(shards), smalls[0].shape[0])
    ins = [w.reshape(2, 2, 2, 2, w.shape[0] // 16, w.shape[1]) for w in shards]
    chunks = gather_chunks([w.shape for w in shards])
    outs = [jax.ShapeDtypeStruct((2, 2) + w.shape, w.dtype) for w in ins]
    outs.append(jax.ShapeDtypeStruct((4, rows, width), BF))
    dma = pltpu.SemaphoreType.DMA
    found = pl.pallas_call(
        functools.partial(gather_kernel, chunks, count, len(smalls)),
        out_shape=outs,
        in_specs=[ANY] * count + [VM] * len(smalls),
        out_specs=[ANY] * (count + 1),
        scratch_shapes=[
            dma((len(chunks), 13)),
            dma((len(chunks), 13)),
            dma((count + 1,)),
            dma((count,)),
            dma((3,)),
            dma((3,)),
            pltpu.VMEM((rows, width), F32),
            pltpu.VMEM((rows, width), BF),
        ]
        + [pltpu.VMEM(w.shape, w.dtype) for w in ins],
        compiler_params=pltpu.CompilerParams(
            collective_id=0, has_side_effects=True, vmem_limit_bytes=58 << 20
        ),
        name="gather_weights",
    )(*ins, *smalls)
    return [w.reshape(-1, w.shape[-1]) for w in found[:count]], found[count]


def fill_sums(total, smalls):
    width = total.shape[1] // 4
    total[...] = jnp.zeros_like(total)
    at = 0
    for ref in smalls:
        if len(ref.shape) > 1:
            total[at : at + ref.shape[0], :] = ref[...]
            at += ref.shape[0]
        elif ref.shape[0] == 4 * width:
            total[at, :] = ref[...]
            at += 1
        else:
            each = ref.shape[0] // (4 * width)
            for k in range(each):
                for z in range(4):
                    total[at, pl.ds(z * width, width)] = ref[pl.ds((z * each + k) * width, width)]
                at += 1


REDUCE_LAG = (0, 1, 2, 3, 4, 5, 6, 7)
BESIDE_LAG = (0, 1, 2, 4, 6, 7, 8, 9)


def reducer(groups, units, lefts, rights, outs, buffers, lags):
    lbuf, rbuf, sbuf, b1, b2, b3, b4, b5, lsem, ssem, rsem, osem = buffers
    z, core, x, y, z0, z1, peers = here()

    def remote(u, slot, src, dst, to):
        return pltpu.make_async_remote_copy(
            src_ref=src,
            dst_ref=dst,
            send_sem=ssem.at[u, slot],
            recv_sem=rsem.at[u, slot],
            device_id=peers[to],
            device_id_type=MESH,
        )

    def copy_core(u):
        return [remote(u, 0, sbuf.at[lax.rem(u, 2)], b1.at[u], "c")]

    def copy_first(u):
        return [
            remote(u, 1, b1.at[u, :, :, 0, 1 - x], b2.at[u, 0], "x"),
            remote(u, 2, b1.at[u, :, :, 1, 1 - y], b2.at[u, 1], "y"),
        ]

    def copy_z0(u):
        return [remote(u, 3, b2.at[u, :, :, 1 - z0], b3.at[u], "z0")]

    def copy_z1(u):
        return [remote(u, 4, b3.at[u, :, 1 - z1], b4.at[u], "z1")]

    def copy_second(u):
        return [
            remote(u, 5, b4.at[u, 0, 1 - y], b5.at[u, 0], "y"),
            remote(u, 6, b4.at[u, 1, 1 - x], b5.at[u, 1], "x"),
        ]

    def block(group, k, *at):
        if groups[group][4]:
            return outs[group].at[(k,) + at]
        at = at + (slice(None),) * (5 - len(at))
        return outs[group].at[at + (pl.ds(pl.multiple_of(k * 1024, 1024), 1024),)]

    def copy_own(u, group=0, k=0):
        return [
            pltpu.make_async_copy(b5.at[u, 0], block(group, k, core, 0, x, y), osem.at[u, 0]),
            pltpu.make_async_copy(b5.at[u, 1], block(group, k, core, 1, y, x), osem.at[u, 1]),
        ]

    def spread_second(u, group=0, k=0):
        return [
            remote(u, 7, b5.at[u, 0], block(group, k, core, 0, x, y), "y"),
            remote(u, 8, b5.at[u, 1], block(group, k, core, 1, y, x), "x"),
        ]

    def spread_first(u, group=0, k=0):
        a, b = (block(group, k, core, 0, x), block(group, k, core, 1, y))
        return [remote(u, 9, a, a, "x"), remote(u, 10, b, b, "y")]

    def spread_core(u, group=0, k=0):
        a = block(group, k, core)
        return [remote(u, 11, a, a, "c")]

    def start_out(u, *makers):
        for group, (_, _, first, count, _) in enumerate(groups):

            @pl.when(jnp.logical_and(u >= first, u < first + count))
            def _():
                for make in makers:
                    start(make(u, group, u - first))

    def start(copies):
        for copy in copies:
            copy.start()

    def arrive(copies):
        for copy in copies:
            copy.wait_recv()

    def load(u):
        slot = lax.rem(u, 3)
        for li, ri, first, count, by_rows in groups:

            @pl.when(jnp.logical_and(u >= first, u < first + count))
            def _():
                k = u - first
                for part in range(4):
                    at = pl.multiple_of(part * 1024 + k * 256, 256) if by_rows else part * 256
                    pltpu.make_async_copy(
                        lefts[li].at[:, pl.ds(at, 256)], lbuf.at[slot, part], lsem.at[slot, part]
                    ).start()
                at = 0 if by_rows else pl.multiple_of(k * 1024, 1024)
                pltpu.make_async_copy(
                    rights[ri].at[:, pl.ds(at, 1024)], rbuf.at[slot], lsem.at[slot, 4]
                ).start()

    def product(u, part, half):
        slot = lax.rem(u, 3)
        left = lbuf[slot, part, :, pl.ds(pl.multiple_of(half * 128, 128), 128)]
        return lax.dot_general(
            left, rbuf[slot], (((0,), (0,)), ((), ())), preferred_element_type=F32
        ).reshape(2, 2, 2, 16, 1024)

    def begin():
        load(0)
        load(1)

    def stage_multiply(u):
        slot = lax.rem(u, 3)
        for part in range(4):
            pltpu.make_async_copy(
                lefts[0].at[:, pl.ds(0, 256)], lbuf.at[slot, part], lsem.at[slot, part]
            ).wait()
        pltpu.make_async_copy(
            rights[0].at[:, pl.ds(0, 1024)], rbuf.at[slot], lsem.at[slot, 4]
        ).wait()

        @pl.when(u >= 2)
        def _():
            for copy in copy_core(u - 2):
                copy.wait_send()

        def body(part, carry):
            sbuf[lax.rem(u, 2), part // 2, lax.rem(part, 2)] = product(u, part, 1 - core).astype(BF)
            return carry

        lax.fori_loop(0, 4, body, 0)
        start(copy_core(u))

    def stage_own(u):
        arrive(copy_core(u))

        def body(part, carry):
            a, b = (part // 2, lax.rem(part, 2))
            b1[u, a, b] = (product(u, part, core) + b1[u, a, b].astype(F32)).astype(BF)
            return carry

        lax.fori_loop(0, 4, body, 0)
        start(copy_first(u))

        @pl.when(u + 2 < units)
        def _():
            load(u + 2)

    def stage_first(u):
        arrive(copy_first(u))

        def body(part, carry):
            a, b = (part // 2, lax.rem(part, 2))
            for half, bit in ((0, x), (1, y)):
                b2[u, half, a, b] = (
                    b2[u, half, a, b].astype(F32) + b1[u, a, b, half, bit].astype(F32)
                ).astype(BF)
            return carry

        lax.fori_loop(0, 4, body, 0)
        start(copy_z0(u))

    def stage_z0(u):
        arrive(copy_z0(u))
        for half in range(2):
            for a in range(2):
                b3[u, half, a] = (
                    b3[u, half, a].astype(F32) + b2[u, half, a, z0].astype(F32)
                ).astype(BF)
        start(copy_z1(u))

    def stage_z1(u):
        arrive(copy_z1(u))
        for half in range(2):
            b4[u, half] = (b4[u, half].astype(F32) + b3[u, half, z1].astype(F32)).astype(BF)
        start(copy_second(u))

    def stage_second(u):
        arrive(copy_second(u))
        for half, bit in ((0, y), (1, x)):
            b5[u, half] = (b5[u, half].astype(F32) + b4[u, half, bit].astype(F32)).astype(BF)
        start_out(u, copy_own, spread_second)

    def stage_spread(u):
        arrive(spread_second(u))
        for copy in copy_own(u):
            copy.wait()
        start_out(u, spread_first)

    def stage_core(u):
        arrive(spread_first(u))
        start_out(u, spread_core)

    stages = (
        stage_multiply,
        stage_own,
        stage_first,
        stage_z0,
        stage_z1,
        stage_second,
        stage_spread,
        stage_core,
    )

    def step(i):
        for stage, lag in zip(stages, lags):
            u = i - lag

            @pl.when(jnp.logical_and(u >= 0, u < units))
            def _():
                stage(u)

    def finish_one(u, carry):
        arrive(spread_core(u))
        for copies in (
            copy_first,
            copy_z0,
            copy_z1,
            copy_second,
            spread_second,
            spread_first,
            spread_core,
        ):
            for copy in copies(u):
                copy.wait_send()

        @pl.when(u >= units - 2)
        def _():
            for copy in copy_core(u):
                copy.wait_send()

        return carry

    def finish():
        lax.fori_loop(0, units, finish_one, 0)

    return begin, step, finish


def reducer_buffers(units):
    dma = pltpu.SemaphoreType.DMA
    return [
        pltpu.VMEM((3, 4, 256, 256), BF),
        pltpu.VMEM((3, 256, 1024), BF),
        pltpu.VMEM((2, 2, 2, 2, 2, 2, 16, 1024), BF),
        pltpu.VMEM((units, 2, 2, 2, 2, 2, 16, 1024), BF),
        pltpu.VMEM((units, 2, 2, 2, 2, 16, 1024), BF),
        pltpu.VMEM((units, 2, 2, 2, 16, 1024), BF),
        pltpu.VMEM((units, 2, 2, 16, 1024), BF),
        pltpu.VMEM((units, 2, 16, 1024), BF),
        dma((3, 5)),
        dma((units, 12)),
        dma((units, 12)),
        dma((units, 2)),
    ]


def reducer_plan(pairs):
    lefts, rights, groups, units = ([], [], [], 0)

    def index_of(arrays, array):
        for i, known in enumerate(arrays):
            if known is array:
                return i
        arrays.append(array)
        return len(arrays) - 1

    for left, right in pairs:
        by_rows = left.shape[1] > 1024
        count = left.shape[1] // 1024 if by_rows else right.shape[1] // 1024
        groups.append((index_of(lefts, left), index_of(rights, right), units, count, by_rows))
        units += count
    outs = []
    for _, _, _, count, by_rows in groups:
        shape = (count, 2, 2, 2, 2, 16, 1024) if by_rows else (2, 2, 2, 2, 16, count * 1024)
        outs.append(jax.ShapeDtypeStruct(shape, BF))
    return lefts, rights, groups, units, outs


def reduce_kernel(groups, units, n_left, n_right, n_small, *refs):
    lefts, rights = (refs[:n_left], refs[n_left : n_left + n_right])
    refs = refs[n_left + n_right :]
    smalls, outs, small_out = (refs[:n_small], refs[n_small:-18], refs[-18])
    hop_out, hop_in, hop_total, hsem, isem = refs[-17:-12]
    z, _, _, _, _, _, peers = here()
    del peers["zz"]
    begin, step, finish = reducer(groups, units, lefts, rights, outs, refs[-12:], REDUCE_LAG)
    begin()
    meet(peers)
    hops = ("c", "x", "y", "z0", "z1")

    def hop(k):
        return pltpu.make_async_remote_copy(
            src_ref=hop_out.at[k],
            dst_ref=hop_in.at[k],
            send_sem=hsem.at[k],
            recv_sem=isem.at[k],
            device_id=peers[hops[k]],
            device_id_type=MESH,
        )

    def stage_hop(k):
        hop(k).wait_recv()
        total = hop_out[k].astype(F32) + hop_in[k].astype(F32)
        if k + 1 < len(hops):
            hop_out[k + 1] = total.astype(BF)
            hop(k + 1).start()
        else:
            width = small_out.shape[1]
            hop_total[...] = total
            small_out[...] = hop_total[:, pl.ds(pl.multiple_of(z * width, width), width)]

    def body(i, carry):
        step(i)

        @pl.when(i == 0)
        def _():
            fill_sums(hop_total, smalls)
            hop_out[0] = hop_total[...].astype(BF)
            hop(0).start()

        for k in range(len(hops)):

            @pl.when(i == 2 * k + 2)
            def _():
                stage_hop(k)

        return carry

    lax.fori_loop(0, units + REDUCE_LAG[-1], body, 0)
    finish()
    for k in range(len(hops)):
        hop(k).wait_send()


def reduce_fast(pairs, smalls, before=()):
    lefts, rights, groups, units, outs = reducer_plan(pairs)
    dma = pltpu.SemaphoreType.DMA
    rows = sum(a.shape[0] if a.ndim > 1 else a.shape[0] // 1024 for a in smalls)
    rows = -(-rows // 16) * 16
    found = pl.pallas_call(
        functools.partial(reduce_kernel, groups, units, len(lefts), len(rights), len(smalls)),
        out_shape=outs + [jax.ShapeDtypeStruct((rows, 256), F32)],
        in_specs=[ANY] * (len(lefts) + len(rights)) + [VM] * len(smalls),
        out_specs=[ANY] * len(outs) + [VM],
        scratch_shapes=[
            pltpu.VMEM((5, rows, 1024), BF),
            pltpu.VMEM((5, rows, 1024), BF),
            pltpu.VMEM((rows, 1024), F32),
            dma((5,)),
            dma((5,)),
        ]
        + reducer_buffers(units),
        compiler_params=pltpu.CompilerParams(
            collective_id=1, has_side_effects=True, vmem_limit_bytes=60 << 20
        ),
        name="reduce_grads",
    )(*lefts, *rights, *smalls)
    found, summed = (list(before) + list(found[:-1]), found[-1])
    return widened([w.reshape(-1, w.shape[-1]) for w in found]), summed


def widen_kernel(*refs):
    count = len(refs) // 2
    for i in range(count):
        refs[count + i][...] = refs[i][...].astype(F32)


def widened(arrays):
    specs = [pl.BlockSpec((a.shape[0] // 16, a.shape[1]), lambda i: (i, 0)) for a in arrays]
    return pl.pallas_call(
        widen_kernel,
        out_shape=[jax.ShapeDtypeStruct(a.shape, F32) for a in arrays],
        grid=(16,),
        in_specs=specs,
        out_specs=specs,
        compiler_params=pltpu.CompilerParams(vmem_limit_bytes=60 << 20),
        name="widen_sums",
    )(*arrays)


def reduce_plain(pairs, small):
    small = pack_sums(small, lax.axis_size("shard"))
    grads = []
    for left, right in pairs:
        full = lax.dot_general(left, right, (((0,), (0,)), ((), ())), preferred_element_type=F32)
        part = lax.psum_scatter(full.astype(BF), "shard", scatter_dimension=0, tiled=True)
        grads.append(lax.psum(part, "rep").astype(F32))
    summed = lax.psum(small.astype(BF), ("rep", "shard")).astype(F32)
    width = small.shape[1] // lax.axis_size("shard")
    return grads, lax.dynamic_slice_in_dim(summed, lax.axis_index("shard") * width, width, 1)


def greet(n, more=()):
    rep = lax.axis_index("rep")
    others = [jnp.bitwise_xor(rep, d) for d in range(1, n)]
    barrier = pltpu.get_barrier_semaphore()
    for other in others:
        pl.semaphore_signal(barrier, inc=1, device_id={"rep": other}, device_id_type=MESH)
    for other in more:
        pl.semaphore_signal(barrier, inc=1, device_id=other, device_id_type=MESH)
    pl.semaphore_wait(barrier, n - 1 + len(more))
    return rep, others


def send_all(others, src_of, dst, ssem, rsem):
    copies = []
    for d, other in enumerate(others):
        copy = pltpu.make_async_remote_copy(
            src_ref=src_of(other),
            dst_ref=dst,
            send_sem=ssem.at[d],
            recv_sem=rsem.at[d],
            device_id={"rep": other},
            device_id_type=MESH,
        )
        copy.start()
        copies.append(copy)
    return copies


def to_heads(arrays, n):
    batch, local, features = arrays[0].shape
    parts = [a.reshape(batch, local, n, features // n) for a in arrays]
    stacked = jnp.stack([jnp.transpose(p, (2, 0, 1, 3)) for p in parts], axis=1)
    return stacked


def from_heads(swapped):
    if swapped.ndim == 4:
        k, batch, local, features = swapped.shape
        return [swapped[i].reshape(batch * local, features) for i in range(k)]
    n, k, batch, local, width = swapped.shape
    return [
        jnp.transpose(swapped[:, i], (1, 2, 0, 3)).reshape(batch * local, n * width)
        for i in range(k)
    ]


def head_mask(shape, head):
    lane = lax.broadcasted_iota(jnp.int32, shape, 1)
    return jnp.logical_and(lane >= head * HD, lane < (head + 1) * HD)


def spread_bias(bias, spread, block):
    wide = bias.shape[1]
    lane = lax.broadcasted_iota(jnp.int32, (128, wide), 1)
    bias[...] = jnp.where(lane < (block + 1) * 128, spread[:, 0:1], spread[:, 383:384])
    rolled = pltpu.roll(spread, 0, 1, stride=1, stride_axis=0)
    bias[:, pl.ds(pl.multiple_of(block * 128, 128), 384)] = rolled[:, 0:384]


def features_of(out_ref, rep, width):
    if width % 128:
        return None
    return pl.ds(pl.multiple_of(rep * width, width), width)


def forward_kernel(
    x_ref, table_ref, heads_ref, mixed_ref, lse_ref, out_ref, bias, low, ssem, rsem, tsem, usem
):
    batch, _, n, local, width = heads_ref.shape
    total = n * local
    rep, others = greet(n)
    arriving, leaving = ([], [])
    for b in range(batch):
        arriving.append(
            send_all(
                others,
                lambda other: x_ref.at[other, :, b],
                heads_ref.at[b, :, rep],
                ssem.at[b],
                rsem.at[b],
            )
        )
    for b in range(batch):
        for part in range(3):
            heads_ref[b, part, rep] = x_ref[rep, part, b]
    for b in range(batch):
        for copy in arriving[b]:
            copy.wait_recv()

        def one_block(block, carry):
            keys = heads_ref[b, 1].reshape(total, width)
            values = heads_ref[b, 2].reshape(total, width)
            query = heads_ref[b, 0, block] * jnp.asarray(0.125, BF)
            mixed, logsum = (None, None)
            for head in range(width // HD):
                mask = head_mask((128, width), head)
                part = jnp.where(mask, query, jnp.zeros_like(query))
                spread = lax.dot_general(
                    part, table_ref[...], (((1,), (1,)), ((), ())), preferred_element_type=F32
                )
                spread_bias(bias, spread.astype(BF).astype(F32), block)
                scores = lax.dot_general(
                    part, keys, (((1,), (1,)), ((), ())), preferred_element_type=F32
                )
                scores = scores + bias[:, 128 : 128 + total]
                top = jnp.max(scores, axis=1, keepdims=True)
                weight = jnp.exp(scores - top)
                summed = jnp.sum(weight, axis=1, keepdims=True)
                one = jnp.dot(weight.astype(BF), values, preferred_element_type=F32) / summed
                own = jnp.broadcast_to(top + jnp.log(summed), (128, width))
                mixed = one if mixed is None else jnp.where(mask, one, mixed)
                logsum = own if logsum is None else jnp.where(mask, own, logsum)
            mixed_ref[b, block] = mixed
            lse_ref[b, block] = logsum
            low[b, block] = mixed.astype(BF)
            return carry

        lax.fori_loop(0, n, one_block, 0)
        place = features_of(out_ref, rep, width)
        target = out_ref.at[rep, 0, b] if place is None else out_ref.at[0, b, :, place]
        leaving.append(
            send_all(others, lambda other: low.at[b, other], target, tsem.at[b], usem.at[b])
        )
        target[...] = low[b, rep]
    for copies in arriving:
        for copy in copies:
            copy.wait_send()
    for copies in leaving:
        for copy in copies:
            copy.wait()


def sent_shape(count, n, batch, local, width):
    if width % 128:
        return (n, count, batch, local, width)
    return (count, batch, local, n * width)


def attention_forward(stacked, table):
    n, _, batch, local, width = stacked.shape
    shape = jax.ShapeDtypeStruct((batch, n, local, width), F32)
    dma = pltpu.SemaphoreType.DMA
    return pl.pallas_call(
        forward_kernel,
        out_shape=[
            jax.ShapeDtypeStruct((batch, 3, n, local, width), BF),
            shape,
            shape,
            jax.ShapeDtypeStruct(sent_shape(1, n, batch, local, width), BF),
        ],
        in_specs=[VM, VM],
        out_specs=[VM] * 4,
        scratch_shapes=[
            pltpu.VMEM((128, n * local + 256), F32),
            pltpu.VMEM((batch, n, local, width), BF),
        ]
        + [dma((batch, n - 1))] * 4,
        compiler_params=pltpu.CompilerParams(
            collective_id=2, has_side_effects=True, vmem_limit_bytes=40 << 20
        ),
        name="attention_forward",
    )(stacked, table)


def backward_kernel(plan, *refs):
    x_ref, heads_ref, table_ref, mixed_ref, lse_ref = refs[:5]
    refs = refs[5:]
    batch, _, n, local, width = heads_ref.shape
    total = n * local
    if plan is None:
        out_ref, dtable_ref = refs[:2]
        refs = refs[2:]
        rep, others = greet(n)
    else:
        n_left, n_right, groups, units = plan
        lefts, rights = (refs[:n_left], refs[n_left : n_left + n_right])
        refs = refs[n_left + n_right :]
        out_ref, dtable_ref = refs[:2]
        outs = refs[2 : 2 + len(groups)]
        refs = refs[2 + len(groups) :]
        begin, step, finish = reducer(
            groups, units, lefts, rights, outs, refs[12:], BESIDE_LAG
        )
        begin()
        peers = here()[-1]
        rep, others = greet(n, (peers["z0"], peers["z1"]))
    grads, low, bias, keyx, dscore, prob, dkt, dvt, ssem, rsem, tsem, usem = refs[:12]
    arriving, leaving = ([], [])
    for b in range(batch):
        arriving.append(
            send_all(
                others,
                lambda other: x_ref.at[other, 0, b],
                grads.at[b, rep],
                ssem.at[b],
                rsem.at[b],
            )
        )
    dtable_ref[...] = jnp.zeros_like(dtable_ref)
    dscore[:, 0:128] = jnp.zeros((128, 128), BF)
    dscore[:, 128 + total : 256 + total] = jnp.zeros((128, 128), BF)
    row = lax.broadcasted_iota(jnp.int32, (total, 128), 0) // 128
    lane = lax.broadcasted_iota(jnp.int32, (total, 128), 1)
    keyx[:, width : width + 128] = (row == lane).astype(BF)
    flip = (
        lax.broadcasted_iota(jnp.int32, (128, 128), 0)
        + lax.broadcasted_iota(jnp.int32, (128, 128), 1)
        == 127
    ).astype(BF)
    lane_at = lax.broadcasted_iota(jnp.int32, (128, 128), 1)
    band_at = lax.broadcasted_iota(jnp.int32, (128, BAND), 1)
    for b in range(batch):
        grads[b, rep] = x_ref[rep, 0, b]
    for b in range(batch):
        dkt[...] = jnp.zeros_like(dkt)
        dvt[...] = jnp.zeros_like(dvt)
        keyx[:, 0:width] = heads_ref[b, 1].reshape(total, width)
        for copy in arriving[b]:
            copy.wait_recv()

        def one_block(block, carry):
            keys = heads_ref[b, 1].reshape(total, width)
            values = heads_ref[b, 2].reshape(total, width)
            query = heads_ref[b, 0, block] * jnp.asarray(0.125, BF)
            grad = grads[b, block]
            weighed = grad.astype(F32) * mixed_ref[b, block]
            logsums = lse_ref[b, block]
            query_t = jnp.transpose(query.astype(F32)).astype(BF)
            grad_t = jnp.transpose(grad.astype(F32)).astype(BF)
            found = None
            for head in range(width // HD):
                mask = head_mask((128, width), head)
                lanes = slice(head * HD, (head + 1) * HD)
                part = jnp.where(mask, query, jnp.zeros_like(query))
                grad_part = jnp.where(mask, grad, jnp.zeros_like(grad))
                balance = jnp.sum(jnp.where(mask, weighed, 0.0), axis=1, keepdims=True)
                logsum = logsums[:, head * HD : head * HD + 1]
                spread = lax.dot_general(
                    part, table_ref[...], (((1,), (1,)), ((), ())), preferred_element_type=F32
                )
                spread_bias(bias, spread.astype(BF).astype(F32), block)
                scores = lax.dot_general(
                    part, keys, (((1,), (1,)), ((), ())), preferred_element_type=F32
                )
                chance = jnp.exp(scores + bias[:, 128 : 128 + total] - logsum)
                back = lax.dot_general(
                    grad_part, values, (((1,), (1,)), ((), ())), preferred_element_type=F32
                )
                prob[...] = chance.astype(BF)
                dscore[:, 128 : 128 + total] = (chance * (back - balance)).astype(BF)
                score_back = dscore[:, 128 : 128 + total]
                dkt[lanes, :] += jnp.dot(
                    query_t[lanes, :], score_back, preferred_element_type=F32
                )
                dvt[lanes, :] += jnp.dot(grad_t[lanes, :], prob[...], preferred_element_type=F32)
                wide = jnp.dot(score_back, keyx[...], preferred_element_type=F32)
                sums = wide[:, width : width + 128]
                before = jnp.sum(jnp.where(lane_at < block - 1, sums, 0.0), axis=1, keepdims=True)
                after = jnp.sum(jnp.where(lane_at > block + 1, sums, 0.0), axis=1, keepdims=True)
                near = dscore[:, pl.ds(pl.multiple_of(block * 128, 128), 384)]
                near = jnp.dot(flip, near, preferred_element_type=F32)
                near = jnp.concatenate([near, jnp.zeros((128, BAND - 384), F32)], axis=1)
                near = pltpu.roll(near, BAND - 127, 1, stride=1, stride_axis=0)
                near = jnp.dot(flip, near.astype(BF), preferred_element_type=F32)
                near = near + jnp.where(band_at == 0, before, 0.0)
                near = (near + jnp.where(band_at == 383, after, 0.0)).astype(BF)
                query_back = wide[:, 0:width] + jnp.dot(
                    near, table_ref[...], preferred_element_type=F32
                )
                dtable_ref[...] += lax.dot_general(
                    near, part, (((0,), (0,)), ((), ())), preferred_element_type=F32
                )
                found = query_back if found is None else jnp.where(mask, query_back, found)
            low[b, 0, block] = (found * 0.125).astype(BF)
            if plan is not None:
                step(b * n + block)
            return carry

        lax.fori_loop(0, n, one_block, 0)
        low[b, 1] = jnp.transpose(dkt[...]).astype(BF).reshape(n, local, width)
        low[b, 2] = jnp.transpose(dvt[...]).astype(BF).reshape(n, local, width)
        place = features_of(out_ref, rep, width)
        target = out_ref.at[rep, :, b] if place is None else out_ref.at[:, b, :, place]
        leaving.append(
            send_all(others, lambda other: low.at[b, :, other], target, tsem.at[b], usem.at[b])
        )
        for part in range(3):
            target[part] = low[b, part, rep]
    for copies in arriving:
        for copy in copies:
            copy.wait_send()
    for copies in leaving:
        for copy in copies:
            copy.wait()
    if plan is not None:

        def rest(i, carry):
            step(i)
            return carry

        lax.fori_loop(batch * n, max(batch * n, units + BESIDE_LAG[-1]), rest, 0)
        finish()


def attention_backward(stacked, heads, table, mixed, logsum, pairs):
    batch, _, n, local, width = heads.shape
    total = n * local
    dma = pltpu.SemaphoreType.DMA
    plan, lefts, rights, outs, buffers = (None, [], [], [], [])
    if pairs:
        lefts, rights, groups, units, outs = reducer_plan(pairs)
        plan = (len(lefts), len(rights), groups, units)
        buffers = reducer_buffers(units)
    found = pl.pallas_call(
        functools.partial(backward_kernel, plan),
        out_shape=[
            jax.ShapeDtypeStruct(sent_shape(3, n, batch, local, width), BF),
            jax.ShapeDtypeStruct(table.shape, F32),
        ]
        + outs,
        in_specs=[VM] * 5 + [ANY] * (len(lefts) + len(rights)),
        out_specs=[VM] * 2 + [ANY] * len(outs),
        scratch_shapes=[
            pltpu.VMEM((batch, n, local, width), BF),
            pltpu.VMEM((batch, 3, n, local, width), BF),
            pltpu.VMEM((128, total + 256), F32),
            pltpu.VMEM((total, width + 128), BF),
            pltpu.VMEM((128, total + 256), BF),
            pltpu.VMEM((128, total), BF),
            pltpu.VMEM((width, total), F32),
            pltpu.VMEM((width, total), F32),
        ]
        + [dma((batch, n - 1))] * 4
        + buffers,
        compiler_params=pltpu.CompilerParams(
            collective_id=3, has_side_effects=True, vmem_limit_bytes=48 << 20
        ),
        name="attention_backward",
    )(stacked, heads, table, mixed, logsum, *lefts, *rights)
    return found[0], found[1], list(found[2:])


def shifted(value, axis, steps):
    count = lax.axis_size(axis)
    leading, last = (max(0, -steps), min(count, count - steps))
    return lax.ppermute(value, axis, [(source, source + steps) for source in range(leading, last)])


def statistics(values):
    centre = jnp.mean(values, axis=-1, keepdims=True)
    centred = values - centre
    spread = jnp.mean(centred * centred, axis=-1, keepdims=True)
    return centre, lax.rsqrt(spread + EPSILON)


def norm(values, gain, shift):
    centre, scale = statistics(values)
    return (values - centre) * scale * gain + shift


def norm_back(values, gain, grad):
    centre, scale = statistics(values)
    hat = (values - centre) * scale
    weighed = grad * gain
    back = (
        weighed
        - jnp.mean(weighed, axis=-1, keepdims=True)
        - hat * jnp.mean(weighed * hat, axis=-1, keepdims=True)
    ) * scale
    return back, jnp.sum(grad * hat, axis=0), jnp.sum(grad, axis=0)


def swish(values):
    return values * jax.nn.sigmoid(values)


def swish_slope(values):
    gate = jax.nn.sigmoid(values)
    return gate * (1.0 + values * (1.0 - gate))


def times(left, right):
    return jnp.dot(left, right, preferred_element_type=F32)


def times_back(left, right):
    return lax.dot_general(left, right, (((1,), (1,)), ((), ())), preferred_element_type=F32)


def column_sum(values):
    return jnp.sum(values.astype(F32), axis=0)


MATRICES = (2, 4, 8, 10, 11, 13, 18, 22, 25, 27)
VECTORS = (0, 1, 5, 6, 7, 9, 12, 14, 16, 17, 20, 21, 23, 24, 28, 29, 30)
OFFSETS = (3, 26)
TABLE_AT = 15
TAPS_AT = 19


SMALLS = VECTORS + OFFSETS + (TAPS_AT, TABLE_AT)


def small_rows(shards):
    width = shards[0].shape[0]
    count = len(VECTORS) + sum(shards[i].shape[0] // width for i in OFFSETS)
    count += shards[TAPS_AT].shape[0] + shards[TABLE_AT].shape[0]
    return -(-count // 16) * 16


def pack_small(shards):
    width = shards[0].shape[0]
    rows = [shards[i].reshape(-1, width) for i in VECTORS + OFFSETS]
    rows.append(shards[TAPS_AT])
    table = shards[TABLE_AT]
    rows.append(jnp.pad(table, ((0, 0), (0, width - table.shape[1]))))
    packed = jnp.concatenate(rows, axis=0)
    return jnp.pad(packed, ((0, small_rows(shards) - packed.shape[0]), (0, 0)))


def unpack_small(gathered, shards):
    n, _, width = gathered.shape
    full = {}
    at = 0
    for i in VECTORS:
        full[i] = gathered[:, at].reshape(n * width).astype(F32)
        at += 1
    for i in OFFSETS:
        count = shards[i].shape[0] // width
        full[i] = gathered[:, at : at + count].reshape(n * width * count).astype(F32)
        at += count
    count = shards[TAPS_AT].shape[0]
    full[TAPS_AT] = jnp.transpose(gathered[:, at : at + count], (1, 0, 2)).reshape(count, -1)
    at += count
    rows, cols = shards[TABLE_AT].shape
    table = gathered[:, at : at + rows, :cols]
    full[TABLE_AT] = jnp.transpose(table, (1, 0, 2)).reshape(rows, n * cols)
    return full


def list_sums(grads, n):
    table = grads[TABLE_AT]
    width = grads[0].shape[0] // n
    parts = jnp.transpose(table.reshape(table.shape[0], n, -1), (1, 0, 2)).reshape(n, -1)
    parts = jnp.pad(parts, ((0, 0), (0, -parts.shape[1] % width))).reshape(n, -1, width)
    parts = jnp.transpose(parts, (1, 0, 2)).reshape(-1, n * width)
    return [grads[i] for i in VECTORS + OFFSETS + (TAPS_AT,)] + [parts]


def pack_sums(smalls, n):
    features = smalls[0].shape[0]
    rows = []
    for a in smalls:
        if a.ndim == 1:
            a = jnp.transpose(a.reshape(n, -1, features // n), (1, 0, 2)).reshape(-1, features)
        rows.append(a)
    return jnp.concatenate(rows, axis=0)


def split_kernel(offset_rows, tap_rows, x_ref, *outs):
    width = x_ref.shape[1]
    at = 0
    for i in range(len(VECTORS)):
        outs[i][...] = x_ref[at, :]
        at += 1
    for i in range(len(OFFSETS)):
        for k in range(offset_rows):
            outs[len(VECTORS) + i][pl.ds(k * width, width)] = x_ref[at, :]
            at += 1
    outs[len(VECTORS) + len(OFFSETS)][...] = x_ref[at : at + tap_rows, :]


def split_sums(summed, shards):
    width = summed.shape[1]
    order = VECTORS + OFFSETS + (TAPS_AT,)
    offset_rows = shards[OFFSETS[0]].shape[0] // width
    tap_rows = shards[TAPS_AT].shape[0]
    if width % 128 == 0:
        parts = pl.pallas_call(
            functools.partial(split_kernel, offset_rows, tap_rows),
            out_shape=[jax.ShapeDtypeStruct(shards[i].shape, F32) for i in order],
            in_specs=[VM],
            out_specs=[VM] * len(order),
            name="split_sums",
        )(summed)
        at = sum(shards[i].size for i in order) // width
    else:
        parts, at = ([], 0)
        for i in order:
            count = shards[i].size // width
            parts.append(summed[at : at + count].reshape(shards[i].shape))
            at += count
    found = dict(zip(order, parts))
    table = shards[TABLE_AT]
    found[TABLE_AT] = summed[at:].reshape(-1)[: table.size].reshape(table.shape)
    return found


def feed_forward(entering, gain, shift, widen, offset, narrow, bias):
    normed = norm(entering, gain, shift).astype(BF)
    act = times(normed, widen) + offset
    hidden = swish(act).astype(BF)
    return entering + 0.5 * (times(hidden, narrow) + bias), (normed, act, hidden)


def feed_backward(entering, gain, widen, narrow, saved, out_grad):
    normed, act, hidden = saved
    out_low = (0.5 * out_grad).astype(BF)
    act_grad = (times_back(out_low, narrow) * swish_slope(act)).astype(BF)
    normed_grad = times_back(act_grad, widen)
    back, grad_gain, grad_shift = norm_back(entering, gain, normed_grad)
    return (
        out_grad + back,
        (grad_gain, grad_shift, column_sum(act_grad), column_sum(out_low)),
        [(hidden, out_low), (normed, act_grad)],
    )


def sigmoid(values):
    return 1.0 / (1.0 + jnp.exp(-values))


def conv_forward_kernel(doubled_ref, rim_ref, taps_ref, gain_ref, shift_ref, depth_ref, acted_ref, padded):
    local, features = (depth_ref.shape[1], depth_ref.shape[2])
    rim = rim_ref.shape[1]
    taps = taps_ref.shape[0]
    padded[32 - rim : 32, :] = rim_ref[0].astype(F32)

    def gate_rows(i, carry):
        rows = pl.ds(pl.multiple_of(i * 32, 32), 32)
        both = doubled_ref[0, rows, :]
        padded[pl.ds(pl.multiple_of(32 + i * 32, 32), 32), :] = both[:, :features] * sigmoid(
            both[:, features:]
        )
        return carry

    lax.fori_loop(0, local // 32, gate_rows, 0)

    def columns(i, carry):
        cols = pl.ds(pl.multiple_of(i * 128, 128), 128)
        first = 32 - (taps - 1)
        total = padded[first : first + local, cols] * taps_ref[0:1, cols]
        for j in range(1, taps):
            total = total + padded[first + j : first + j + local, cols] * taps_ref[j : j + 1, cols]
        depth_ref[0, :, cols] = total
        return carry

    lax.fori_loop(0, features // 128, columns, 0)

    def norm_rows(i, carry):
        rows = pl.ds(pl.multiple_of(i * 32, 32), 32)
        normed = norm(depth_ref[0, rows, :], gain_ref[...], shift_ref[...])
        acted_ref[0, rows, :] = (normed * sigmoid(normed)).astype(BF)
        return carry

    lax.fori_loop(0, local // 32, norm_rows, 0)


def block_spec(shape):
    return pl.BlockSpec((1,) + shape[1:], lambda b: (b,) + (0,) * (len(shape) - 1))


def fixed_spec(shape):
    return pl.BlockSpec(shape, lambda b: (0,) * len(shape))


def conv_forward(doubled, rim_in, taps, gain, shift):
    batch, local, features = (doubled.shape[0], doubled.shape[1], taps.shape[1])
    shape = (batch, local, features)
    return pl.pallas_call(
        conv_forward_kernel,
        out_shape=[jax.ShapeDtypeStruct(shape, F32), jax.ShapeDtypeStruct(shape, BF)],
        grid=(batch,),
        in_specs=[
            block_spec(doubled.shape),
            block_spec(rim_in.shape),
            fixed_spec(taps.shape),
            fixed_spec(gain.shape),
            fixed_spec(shift.shape),
        ],
        out_specs=[block_spec(shape), block_spec(shape)],
        scratch_shapes=[pltpu.VMEM((32 + local, features), F32)],
        compiler_params=pltpu.CompilerParams(vmem_limit_bytes=32 << 20),
        name="conv_forward",
    )(doubled, rim_in, taps, gain, shift)


def depth_backward_kernel(depth_ref, grad_ref, gain_ref, shift_ref, back_ref, sums_ref):
    local = depth_ref.shape[1]

    @pl.when(pl.program_id(0) == 0)
    def _():
        sums_ref[...] = jnp.zeros_like(sums_ref)

    def body(i, carry):
        rows = pl.ds(pl.multiple_of(i * 32, 32), 32)
        values = depth_ref[0, rows, :]
        centre, scale = statistics(values)
        hat = (values - centre) * scale
        gain = gain_ref[...]
        normed = hat * gain + shift_ref[...]
        gate = sigmoid(normed)
        grad = grad_ref[0, rows, :] * gate * (1.0 + normed * (1.0 - gate))
        weighed = grad * gain
        back_ref[0, rows, :] = (
            weighed
            - jnp.mean(weighed, axis=-1, keepdims=True)
            - hat * jnp.mean(weighed * hat, axis=-1, keepdims=True)
        ) * scale
        sums_ref[0:1, :] += jnp.sum(grad * hat, axis=0, keepdims=True)
        sums_ref[1:2, :] += jnp.sum(grad, axis=0, keepdims=True)
        return carry

    lax.fori_loop(0, local // 32, body, 0)


def depth_backward(depth, grad, gain, shift):
    return pl.pallas_call(
        depth_backward_kernel,
        out_shape=[
            jax.ShapeDtypeStruct(depth.shape, F32),
            jax.ShapeDtypeStruct((8, depth.shape[2]), F32),
        ],
        grid=(depth.shape[0],),
        in_specs=[
            block_spec(depth.shape),
            block_spec(grad.shape),
            fixed_spec(gain.shape),
            fixed_spec(shift.shape),
        ],
        out_specs=[block_spec(depth.shape), fixed_spec((8, depth.shape[2]))],
        compiler_params=pltpu.CompilerParams(vmem_limit_bytes=32 << 20),
        name="depth_backward",
    )(depth, grad, gain, shift)


def conv_backward_kernel(
    back_ref, after_ref, doubled_ref, rim_ref, taps_ref, out_ref, dtaps_ref, padded, behind
):
    local, features = (back_ref.shape[1], back_ref.shape[2])
    rim = rim_ref.shape[1]
    taps = taps_ref.shape[0]

    @pl.when(pl.program_id(0) == 0)
    def _():
        dtaps_ref[...] = jnp.zeros_like(dtaps_ref)

    padded[32 - rim : 32, :] = rim_ref[0].astype(F32)
    behind[local : local + rim, :] = after_ref[0].astype(F32)

    def gate_rows(i, carry):
        rows = pl.ds(pl.multiple_of(i * 32, 32), 32)
        both = doubled_ref[0, rows, :]
        padded[pl.ds(pl.multiple_of(32 + i * 32, 32), 32), :] = both[:, :features] * sigmoid(
            both[:, features:]
        )
        behind[rows, :] = back_ref[0, rows, :]
        return carry

    lax.fori_loop(0, local // 32, gate_rows, 0)

    def columns(i, carry):
        cols = pl.ds(pl.multiple_of(i * 128, 128), 128)
        first = 32 - (taps - 1)
        own = back_ref[0, :, cols]
        total = own * taps_ref[taps - 1 : taps, cols]
        dtaps_ref[taps - 1 : taps, cols] += jnp.sum(
            own * padded[first + taps - 1 : first + taps - 1 + local, cols], axis=0, keepdims=True
        )
        for j in range(taps - 1):
            ahead = taps - 1 - j
            total = total + behind[ahead : ahead + local, cols] * taps_ref[j : j + 1, cols]
            dtaps_ref[j : j + 1, cols] += jnp.sum(
                own * padded[first + j : first + j + local, cols], axis=0, keepdims=True
            )
        side = doubled_ref[0, :, cols]
        gate = sigmoid(doubled_ref[0, :, pl.ds(pl.multiple_of(features + i * 128, 128), 128)])
        gated = total * gate
        out_ref[0, :, cols] = gated.astype(BF)
        out_ref[0, :, pl.ds(pl.multiple_of(features + i * 128, 128), 128)] = (
            gated * side * (1.0 - gate)
        ).astype(BF)
        return carry

    lax.fori_loop(0, features // 128, columns, 0)


def conv_backward(back, after, doubled, rim_in, taps):
    batch, local, features = back.shape
    padded_taps = (-(-taps.shape[0] // 8) * 8, features)
    found, dtaps = pl.pallas_call(
        conv_backward_kernel,
        out_shape=[
            jax.ShapeDtypeStruct(doubled.shape, BF),
            jax.ShapeDtypeStruct(padded_taps, F32),
        ],
        grid=(batch,),
        in_specs=[
            block_spec(back.shape),
            block_spec(after.shape),
            block_spec(doubled.shape),
            block_spec(rim_in.shape),
            fixed_spec(taps.shape),
        ],
        out_specs=[block_spec(doubled.shape), fixed_spec(padded_taps)],
        scratch_shapes=[
            pltpu.VMEM((32 + local, features), F32),
            pltpu.VMEM((32 + local, features), F32),
        ],
        compiler_params=pltpu.CompilerParams(vmem_limit_bytes=32 << 20),
        name="conv_backward",
    )(back, after, doubled, rim_in, taps)
    return found, dtaps[: taps.shape[0]]


def on_device(*arguments):
    inputs, shards, cotangent = (arguments[0], arguments[1:32], arguments[32])
    n_rep, n_shard = (lax.axis_size("rep"), lax.axis_size("shard"))
    micro, local, seqs, features = inputs.shape
    batch = micro * seqs
    fast = (
        n_rep == 8
        and n_shard == 4
        and features == 1024
        and batch * local == 256
        and all(shards[i].shape[0] % 256 == 0 for i in MATRICES)
    )

    def rows_of(array):
        return jnp.transpose(array, (0, 2, 1, 3)).reshape(batch * local, features)

    def whole_of(rows):
        return jnp.transpose(rows.reshape(micro, seqs, local, features), (0, 2, 1, 3))

    if fast:
        smalls = [shards[i] for i in SMALLS]
        full, gathered = gather_fast([shards[i] for i in MATRICES], smalls, small_rows(shards))
    else:
        small = pack_small(shards)
        full = [lax.all_gather(shards[i], "shard", axis=0, tiled=True) for i in MATRICES]
        gathered = lax.all_gather(small, "shard", axis=0, tiled=False)
    w = dict(zip(MATRICES, full))
    w.update(unpack_small(gathered, shards))

    level0 = rows_of(inputs).astype(F32)
    level1, early = feed_forward(level0, w[0], w[1], w[2], w[3], w[4], w[5])

    attend_in = norm(level1, w[6], w[7]).astype(BF)
    query = (times(attend_in, w[8]) + w[9]).astype(BF).reshape(batch, local, features)
    keys = times(attend_in, w[10]).astype(BF).reshape(batch, local, features)
    values = (times(attend_in, w[11]) + w[12]).astype(BF).reshape(batch, local, features)
    place = jnp.clip(jnp.arange(BAND) - 64, 0, TABLE - 1)
    place = jnp.where(jnp.arange(BAND) >= 384, 0, place)
    table = w[TABLE_AT]
    spread_table = jnp.tile(jnp.take(table, place, axis=0), (1, features // n_rep // HD))
    heads, mixed_h, logsum, mixed = attention_forward(
        to_heads([query, keys, values], n_rep), spread_table
    )
    mixed = from_heads(mixed)[0]
    level2 = level1 + times(mixed, w[13]) + w[14]

    conv_in = norm(level2, w[16], w[17]).astype(BF)
    doubled = times(conv_in, w[18])
    doubled = doubled.reshape(batch, local, 2 * features)
    taps = w[TAPS_AT].astype(F32)
    rim = taps.shape[0] - 1
    edge = doubled[:, local - rim :]
    edge = (edge[:, :, :features] * jax.nn.sigmoid(edge[:, :, features:])).astype(BF)
    rim_in = shifted(edge, "rep", 1)
    depth, acted = conv_forward(doubled, rim_in, taps, w[20][None], w[21][None])
    acted = acted.reshape(batch * local, features)
    level3 = level2 + times(acted, w[22])

    level4, later = feed_forward(level3, w[23], w[24], w[25], w[26], w[27], w[28])
    output = norm(level4, w[29], w[30]).astype(BF)

    grads = {}
    incoming = rows_of(cotangent).astype(F32)
    back4, grads[29], grads[30] = norm_back(level4, w[29], incoming)
    back3, found, later_pairs = feed_backward(level3, w[23], w[25], w[27], later, back4)
    grads[23], grads[24], grads[26], grads[28] = found

    conv_out = back3.astype(BF)
    acted_grad = times_back(conv_out, w[22]).reshape(batch, local, features)
    depth_back, sums = depth_backward(depth, acted_grad, w[20][None], w[21][None])
    grads[20], grads[21] = (sums[0], sums[1])
    after = shifted(depth_back[:, :rim].astype(BF), "rep", -1)
    doubled_back, grads[TAPS_AT] = conv_backward(depth_back, after, doubled, rim_in, taps)
    doubled_back = doubled_back.reshape(batch * local, 2 * features)
    conv_back = times_back(doubled_back, w[18])
    back, grads[16], grads[17] = norm_back(level2, w[16], conv_back)
    back2 = back3 + back

    mixer_out = back2.astype(BF)
    grads[14] = column_sum(mixer_out)
    mixed_back = times_back(mixer_out, w[13]).astype(BF).reshape(batch, local, features)
    ahead = 2 if fast else 0
    pairs = [
        (27, later_pairs[0]),
        (25, later_pairs[1]),
        (22, (acted, conv_out)),
        (18, (conv_in, doubled_back)),
        (13, (mixed, mixer_out)),
    ]
    found, table_b, before = attention_backward(
        to_heads([mixed_back], n_rep),
        heads,
        spread_table,
        mixed_h,
        logsum,
        [pair for _, pair in pairs[:ahead]],
    )
    query_back, key_back, value_back = from_heads(found)
    folded = table_b.reshape(BAND, -1, HD).sum(axis=1)
    grads[TABLE_AT] = jnp.concatenate(
        [
            (folded[0:65].sum(axis=0) + folded[384:].sum(axis=0))[None],
            folded[65:136],
            folded[136:384].sum(axis=0)[None],
        ]
    )
    grads[9] = column_sum(query_back)
    grads[12] = column_sum(value_back)
    attend_back = (
        times_back(query_back, w[8]) + times_back(key_back, w[10]) + times_back(value_back, w[11])
    )
    back, grads[6], grads[7] = norm_back(level1, w[6], attend_back)
    back1 = back2 + back
    back0, found, early_pairs = feed_backward(level0, w[0], w[2], w[4], early, back1)
    grads[0], grads[1], grads[3], grads[5] = found

    pairs += [
        (8, (attend_in, query_back)),
        (10, (attend_in, key_back)),
        (11, (attend_in, value_back)),
        (4, early_pairs[0]),
        (2, early_pairs[1]),
    ]
    kept, sums = ([pair for _, pair in pairs[ahead:]], list_sums(grads, n_shard))
    if fast:
        matrices, smalls = reduce_fast(kept, sums, before)
    else:
        matrices, smalls = reduce_plain(kept, sums)
    summed = dict(zip([i for i, _ in pairs], matrices))
    summed.update(split_sums(smalls, shards))
    return (whole_of(output), whole_of(back0)) + tuple(summed[i] for i in range(31))


def solution(mesh):
    rows, vector, matrix = (P(None, "rep", "shard", None), P("shard"), P("shard", None))
    columns = P(None, "shard")
    weights = tuple(
        matrix if i in MATRICES else columns if i in (TABLE_AT, TAPS_AT) else vector
        for i in range(31)
    )
    return jax.shard_map(
        on_device,
        mesh=mesh,
        in_specs=(rows,) + weights + (rows,),
        out_specs=(rows, rows) + weights,
        check_vma=False,
    )
```

```python
import functools

import jax
import jax.numpy as jnp
from jax import lax
from jax.experimental import pallas as pl
from jax.experimental.pallas import tpu as pltpu
from jax.sharding import PartitionSpec as P

H = 16
HD = 64
LEFT = 64
RIGHT = 8
TABLE = 73
EPSILON = 1e-05
BAND = 512
MESH = pl.DeviceIdType.MESH
BF = jnp.bfloat16
F32 = jnp.float32
ANY = pl.BlockSpec(memory_space=pltpu.HBM)
VM = pl.BlockSpec(memory_space=pltpu.VMEM)


def here():
    rep = lax.axis_index("rep")
    z = lax.axis_index("shard")
    core = lax.rem(rep, 2)
    x = lax.rem(rep // 2, 2)
    y = rep // 4
    z0 = lax.rem(z, 2)
    z1 = z // 2
    peers = {
        "z1": (rep, lax.rem(z + 2, 4)),
        "z0": (rep, z + 1 - 2 * z0),
        "zz": (rep, 3 - z),
        "x": (rep + 2 - 4 * x, z),
        "y": (rep + 4 - 8 * y, z),
        "c": (rep + 1 - 2 * core, z),
    }
    return z, core, x, y, z0, z1, peers


def meet(peers):
    barrier = pltpu.get_barrier_semaphore()
    for name in peers:
        pl.semaphore_signal(barrier, inc=1, device_id=peers[name], device_id_type=MESH)
    pl.semaphore_wait(barrier, len(peers))


GATHER_LAG = (0, 1, 2, 3, 4)


def fill_rows(packed, smalls):
    width = packed.shape[1]
    packed[...] = jnp.zeros_like(packed)
    at = 0
    for ref in smalls:
        if len(ref.shape) == 1:
            for k in range(ref.shape[0] // width):
                packed[at, :] = ref[pl.ds(k * width, width)].astype(F32)
                at += 1
        else:
            packed[at : at + ref.shape[0], 0 : ref.shape[1]] = ref[...].astype(F32)
            at += ref.shape[0]


def gather_kernel(chunks, n_arr, n_small, *refs):
    ins, smalls = (refs[:n_arr], refs[n_arr : n_arr + n_small])
    refs = refs[n_arr + n_small :]
    outs, small_out = (refs[:n_arr], refs[n_arr])
    ssem, rsem, lsem, lsem2, qsem, psem, packed, small = refs[n_arr + 1 : n_arr + 9]
    bufs = refs[n_arr + 9 :]
    z, core, x, y, z0, z1, peers = here()
    far = ((slice(None), 1 - z0), (1 - z1, z0))
    meet(peers)
    sent = []

    def send(c, slot, src, dst, to):
        copy = pltpu.make_async_remote_copy(
            src_ref=src,
            dst_ref=dst,
            send_sem=ssem.at[c, slot],
            recv_sem=rsem.at[c, slot],
            device_id=peers[to],
            device_id_type=MESH,
        )
        copy.start()
        sent.append(copy)
        return copy

    around = []
    state = {}

    def place(c):
        array, first, count = chunks[c]
        return (ins[array], outs[array], pl.ds(first, count))

    def wait(c, key):
        for copy in state[c, key]:
            copy.wait_recv()

    def stage_z(c):
        src, out, cols = place(c)
        src = src.at[y, x, core, :, :, cols]
        dst = out.at[z1, z0, y, x, core, :, :, cols]
        state[c, "z1"] = [send(c, 0, src, dst, "z1")]
        state[c, "z0"] = [send(c, 1, src, dst, "z0")]

    def stage_zz(c):
        _, out, cols = place(c)
        wait(c, "z1")
        view = out.at[1 - z1, z0, y, x, core, :, :, cols]
        state[c, "z0"].append(send(c, 2, view, view, "z0"))

    def stage_one(c):
        _, out, cols = place(c)
        wait(c, "z0")
        state[c, "one"] = []
        for i, (a, b) in enumerate(far):
            view = out.at[a, b, y, x, core, 0, :, cols]
            state[c, "one"].append(send(c, 3 + i, view, view, "x"))
            view = out.at[a, b, y, x, core, 1, :, cols]
            state[c, "one"].append(send(c, 5 + i, view, view, "y"))

    def stage_two(c):
        _, out, cols = place(c)
        wait(c, "one")
        state[c, "two"] = []
        for i, (a, b) in enumerate(far):
            view = out.at[a, b, y, :, core, 0, :, cols]
            state[c, "two"].append(send(c, 7 + i, view, view, "y"))
            view = out.at[a, b, :, x, core, 1, :, cols]
            state[c, "two"].append(send(c, 9 + i, view, view, "x"))

    def stage_core(c):
        _, out, cols = place(c)
        wait(c, "two")
        state[c, "core"] = []
        for i, (a, b) in enumerate(far):
            view = out.at[a, b, :, :, core, :, :, cols]
            state[c, "core"].append(send(c, 11 + i, view, view, "c"))

    stages = (stage_z, stage_zz, stage_one, stage_two, stage_core)
    local = []
    for step in range(len(chunks) + GATHER_LAG[-1]):
        for stage, lag in zip(stages, GATHER_LAG):
            if 0 <= step - lag < len(chunks):
                stage(step - lag)
        if step == 0:
            for a in range(n_arr):
                copy = pltpu.make_async_copy(ins[a], bufs[a], lsem.at[a])
                copy.start()
                local.append(copy)
            fill_rows(packed, smalls)
            small[...] = packed[...].astype(BF)
            for k, to in enumerate(("z0", "z1", "zz")):
                copy = pltpu.make_async_remote_copy(
                    src_ref=small,
                    dst_ref=small_out.at[z],
                    send_sem=qsem.at[k],
                    recv_sem=psem.at[k],
                    device_id=peers[to],
                    device_id_type=MESH,
                )
                copy.start()
                around.append(copy)
            small_own = pltpu.make_async_copy(small, small_out.at[z], lsem.at[n_arr])
            small_own.start()
        if step == 2:
            for a in range(n_arr):
                local[a].wait()
                copy = pltpu.make_async_copy(bufs[a], outs[a].at[z1, z0], lsem2.at[a])
                copy.start()
                local[a] = copy
    for c in range(len(chunks)):
        wait(c, "core")
    for copy in sent + around:
        copy.wait_send()
    for copy in around:
        copy.wait_recv()
    small_own.wait()
    for copy in local:
        copy.wait()


def gather_chunks(shapes):
    chunks = []
    for i, (rows, cols) in enumerate(shapes):
        for first in range(0, cols, 1024 * 256 // rows):
            chunks.append((i, first, 1024 * 256 // rows))
    return chunks


def gather_fast(shards, smalls, rows):
    count, width = (len(shards), smalls[0].shape[0])
    ins = [w.reshape(2, 2, 2, 2, w.shape[0] // 16, w.shape[1]) for w in shards]
    chunks = gather_chunks([w.shape for w in shards])
    outs = [jax.ShapeDtypeStruct((2, 2) + w.shape, w.dtype) for w in ins]
    outs.append(jax.ShapeDtypeStruct((4, rows, width), BF))
    dma = pltpu.SemaphoreType.DMA
    found = pl.pallas_call(
        functools.partial(gather_kernel, chunks, count, len(smalls)),
        out_shape=outs,
        in_specs=[ANY] * count + [VM] * len(smalls),
        out_specs=[ANY] * (count + 1),
        scratch_shapes=[
            dma((len(chunks), 13)),
            dma((len(chunks), 13)),
            dma((count + 1,)),
            dma((count,)),
            dma((3,)),
            dma((3,)),
            pltpu.VMEM((rows, width), F32),
            pltpu.VMEM((rows, width), BF),
        ]
        + [pltpu.VMEM(w.shape, w.dtype) for w in ins],
        compiler_params=pltpu.CompilerParams(
            collective_id=0, has_side_effects=True, vmem_limit_bytes=58 << 20
        ),
        name="gather_weights",
    )(*ins, *smalls)
    return [w.reshape(-1, w.shape[-1]) for w in found[:count]], found[count]


def fill_sums(total, smalls):
    width = total.shape[1] // 4
    total[...] = jnp.zeros_like(total)
    at = 0
    for ref in smalls:
        if len(ref.shape) > 1:
            total[at : at + ref.shape[0], :] = ref[...]
            at += ref.shape[0]
        elif ref.shape[0] == 4 * width:
            total[at, :] = ref[...]
            at += 1
        else:
            each = ref.shape[0] // (4 * width)
            for k in range(each):
                for z in range(4):
                    total[at, pl.ds(z * width, width)] = ref[pl.ds((z * each + k) * width, width)]
                at += 1


REDUCE_LAG = (0, 1, 2, 3, 4, 5, 6, 7)
BESIDE_LAG = (0, 1, 2, 4, 6, 7, 8, 9)


def reducer(groups, units, lefts, rights, outs, buffers, lags):
    lbuf, rbuf, sbuf, b1, b2, b3, b4, b5, lsem, ssem, rsem, osem = buffers
    z, core, x, y, z0, z1, peers = here()

    def remote(u, slot, src, dst, to):
        return pltpu.make_async_remote_copy(
            src_ref=src,
            dst_ref=dst,
            send_sem=ssem.at[u, slot],
            recv_sem=rsem.at[u, slot],
            device_id=peers[to],
            device_id_type=MESH,
        )

    def copy_core(u):
        return [remote(u, 0, sbuf.at[lax.rem(u, 2)], b1.at[u], "c")]

    def copy_first(u):
        return [
            remote(u, 1, b1.at[u, :, :, 0, 1 - x], b2.at[u, 0], "x"),
            remote(u, 2, b1.at[u, :, :, 1, 1 - y], b2.at[u, 1], "y"),
        ]

    def copy_z0(u):
        return [remote(u, 3, b2.at[u, :, :, 1 - z0], b3.at[u], "z0")]

    def copy_z1(u):
        return [remote(u, 4, b3.at[u, :, 1 - z1], b4.at[u], "z1")]

    def copy_second(u):
        return [
            remote(u, 5, b4.at[u, 0, 1 - y], b5.at[u, 0], "y"),
            remote(u, 6, b4.at[u, 1, 1 - x], b5.at[u, 1], "x"),
        ]

    def block(group, k, *at):
        if groups[group][4]:
            return outs[group].at[(k,) + at]
        at = at + (slice(None),) * (5 - len(at))
        return outs[group].at[at + (pl.ds(pl.multiple_of(k * 1024, 1024), 1024),)]

    def copy_own(u, group=0, k=0):
        return [
            pltpu.make_async_copy(b5.at[u, 0], block(group, k, core, 0, x, y), osem.at[u, 0]),
            pltpu.make_async_copy(b5.at[u, 1], block(group, k, core, 1, y, x), osem.at[u, 1]),
        ]

    def spread_second(u, group=0, k=0):
        return [
            remote(u, 7, b5.at[u, 0], block(group, k, core, 0, x, y), "y"),
            remote(u, 8, b5.at[u, 1], block(group, k, core, 1, y, x), "x"),
        ]

    def spread_first(u, group=0, k=0):
        a, b = (block(group, k, core, 0, x), block(group, k, core, 1, y))
        return [remote(u, 9, a, a, "x"), remote(u, 10, b, b, "y")]

    def spread_core(u, group=0, k=0):
        a = block(group, k, core)
        return [remote(u, 11, a, a, "c")]

    def start_out(u, *makers):
        for group, (_, _, first, count, _) in enumerate(groups):

            @pl.when(jnp.logical_and(u >= first, u < first + count))
            def _():
                for make in makers:
                    start(make(u, group, u - first))

    def start(copies):
        for copy in copies:
            copy.start()

    def arrive(copies):
        for copy in copies:
            copy.wait_recv()

    def load(u):
        slot = lax.rem(u, 3)
        for li, ri, first, count, by_rows in groups:

            @pl.when(jnp.logical_and(u >= first, u < first + count))
            def _():
                k = u - first
                for part in range(4):
                    at = pl.multiple_of(part * 1024 + k * 256, 256) if by_rows else part * 256
                    pltpu.make_async_copy(
                        lefts[li].at[:, pl.ds(at, 256)], lbuf.at[slot, part], lsem.at[slot, part]
                    ).start()
                at = 0 if by_rows else pl.multiple_of(k * 1024, 1024)
                pltpu.make_async_copy(
                    rights[ri].at[:, pl.ds(at, 1024)], rbuf.at[slot], lsem.at[slot, 4]
                ).start()

    def product(u, part, half):
        slot = lax.rem(u, 3)
        left = lbuf[slot, part, :, pl.ds(pl.multiple_of(half * 128, 128), 128)]
        return lax.dot_general(
            left, rbuf[slot], (((0,), (0,)), ((), ())), preferred_element_type=F32
        ).reshape(2, 2, 2, 16, 1024)

    def begin():
        load(0)
        load(1)

    def stage_multiply(u):
        slot = lax.rem(u, 3)
        for part in range(4):
            pltpu.make_async_copy(
                lefts[0].at[:, pl.ds(0, 256)], lbuf.at[slot, part], lsem.at[slot, part]
            ).wait()
        pltpu.make_async_copy(
            rights[0].at[:, pl.ds(0, 1024)], rbuf.at[slot], lsem.at[slot, 4]
        ).wait()

        @pl.when(u >= 2)
        def _():
            for copy in copy_core(u - 2):
                copy.wait_send()

        def body(part, carry):
            sbuf[lax.rem(u, 2), part // 2, lax.rem(part, 2)] = product(u, part, 1 - core).astype(BF)
            return carry

        lax.fori_loop(0, 4, body, 0)
        start(copy_core(u))

    def stage_own(u):
        arrive(copy_core(u))

        def body(part, carry):
            a, b = (part // 2, lax.rem(part, 2))
            b1[u, a, b] = (product(u, part, core) + b1[u, a, b].astype(F32)).astype(BF)
            return carry

        lax.fori_loop(0, 4, body, 0)
        start(copy_first(u))

        @pl.when(u + 2 < units)
        def _():
            load(u + 2)

    def stage_first(u):
        arrive(copy_first(u))

        def body(part, carry):
            a, b = (part // 2, lax.rem(part, 2))
            for half, bit in ((0, x), (1, y)):
                b2[u, half, a, b] = (
                    b2[u, half, a, b].astype(F32) + b1[u, a, b, half, bit].astype(F32)
                ).astype(BF)
            return carry

        lax.fori_loop(0, 4, body, 0)
        start(copy_z0(u))

    def stage_z0(u):
        arrive(copy_z0(u))
        for half in range(2):
            for a in range(2):
                b3[u, half, a] = (
                    b3[u, half, a].astype(F32) + b2[u, half, a, z0].astype(F32)
                ).astype(BF)
        start(copy_z1(u))

    def stage_z1(u):
        arrive(copy_z1(u))
        for half in range(2):
            b4[u, half] = (b4[u, half].astype(F32) + b3[u, half, z1].astype(F32)).astype(BF)
        start(copy_second(u))

    def stage_second(u):
        arrive(copy_second(u))
        for half, bit in ((0, y), (1, x)):
            b5[u, half] = (b5[u, half].astype(F32) + b4[u, half, bit].astype(F32)).astype(BF)
        start_out(u, copy_own, spread_second)

    def stage_spread(u):
        arrive(spread_second(u))
        for copy in copy_own(u):
            copy.wait()
        start_out(u, spread_first)

    def stage_core(u):
        arrive(spread_first(u))
        start_out(u, spread_core)

    stages = (
        stage_multiply,
        stage_own,
        stage_first,
        stage_z0,
        stage_z1,
        stage_second,
        stage_spread,
        stage_core,
    )

    def step(i):
        for stage, lag in zip(stages, lags):
            u = i - lag

            @pl.when(jnp.logical_and(u >= 0, u < units))
            def _():
                stage(u)

    def finish_one(u, carry):
        arrive(spread_core(u))
        for copies in (
            copy_first,
            copy_z0,
            copy_z1,
            copy_second,
            spread_second,
            spread_first,
            spread_core,
        ):
            for copy in copies(u):
                copy.wait_send()

        @pl.when(u >= units - 2)
        def _():
            for copy in copy_core(u):
                copy.wait_send()

        return carry

    def finish():
        lax.fori_loop(0, units, finish_one, 0)

    return begin, step, finish


def reducer_buffers(units):
    dma = pltpu.SemaphoreType.DMA
    return [
        pltpu.VMEM((3, 4, 256, 256), BF),
        pltpu.VMEM((3, 256, 1024), BF),
        pltpu.VMEM((2, 2, 2, 2, 2, 2, 16, 1024), BF),
        pltpu.VMEM((units, 2, 2, 2, 2, 2, 16, 1024), BF),
        pltpu.VMEM((units, 2, 2, 2, 2, 16, 1024), BF),
        pltpu.VMEM((units, 2, 2, 2, 16, 1024), BF),
        pltpu.VMEM((units, 2, 2, 16, 1024), BF),
        pltpu.VMEM((units, 2, 16, 1024), BF),
        dma((3, 5)),
        dma((units, 12)),
        dma((units, 12)),
        dma((units, 2)),
    ]


def reducer_plan(pairs):
    lefts, rights, groups, units = ([], [], [], 0)

    def index_of(arrays, array):
        for i, known in enumerate(arrays):
            if known is array:
                return i
        arrays.append(array)
        return len(arrays) - 1

    for left, right in pairs:
        by_rows = left.shape[1] > 1024
        count = left.shape[1] // 1024 if by_rows else right.shape[1] // 1024
        groups.append((index_of(lefts, left), index_of(rights, right), units, count, by_rows))
        units += count
    outs = []
    for _, _, _, count, by_rows in groups:
        shape = (count, 2, 2, 2, 2, 16, 1024) if by_rows else (2, 2, 2, 2, 16, count * 1024)
        outs.append(jax.ShapeDtypeStruct(shape, BF))
    return lefts, rights, groups, units, outs


def reduce_kernel(groups, units, n_left, n_right, n_small, *refs):
    lefts, rights = (refs[:n_left], refs[n_left : n_left + n_right])
    refs = refs[n_left + n_right :]
    smalls, outs, small_out = (refs[:n_small], refs[n_small:-18], refs[-18])
    hop_out, hop_in, hop_total, hsem, isem = refs[-17:-12]
    z, _, _, _, _, _, peers = here()
    del peers["zz"]
    begin, step, finish = reducer(groups, units, lefts, rights, outs, refs[-12:], REDUCE_LAG)
    begin()
    meet(peers)
    hops = ("c", "x", "y", "z0", "z1")

    def hop(k):
        return pltpu.make_async_remote_copy(
            src_ref=hop_out.at[k],
            dst_ref=hop_in.at[k],
            send_sem=hsem.at[k],
            recv_sem=isem.at[k],
            device_id=peers[hops[k]],
            device_id_type=MESH,
        )

    def stage_hop(k):
        hop(k).wait_recv()
        total = hop_out[k].astype(F32) + hop_in[k].astype(F32)
        if k + 1 < len(hops):
            hop_out[k + 1] = total.astype(BF)
            hop(k + 1).start()
        else:
            width = small_out.shape[1]
            hop_total[...] = total
            small_out[...] = hop_total[:, pl.ds(pl.multiple_of(z * width, width), width)]

    def body(i, carry):
        step(i)

        @pl.when(i == 0)
        def _():
            fill_sums(hop_total, smalls)
            hop_out[0] = hop_total[...].astype(BF)
            hop(0).start()

        for k in range(len(hops)):

            @pl.when(i == 2 * k + 2)
            def _():
                stage_hop(k)

        return carry

    lax.fori_loop(0, units + REDUCE_LAG[-1], body, 0)
    finish()
    for k in range(len(hops)):
        hop(k).wait_send()


def reduce_fast(pairs, smalls, before=()):
    lefts, rights, groups, units, outs = reducer_plan(pairs)
    dma = pltpu.SemaphoreType.DMA
    rows = sum(a.shape[0] if a.ndim > 1 else a.shape[0] // 1024 for a in smalls)
    rows = -(-rows // 16) * 16
    found = pl.pallas_call(
        functools.partial(reduce_kernel, groups, units, len(lefts), len(rights), len(smalls)),
        out_shape=outs + [jax.ShapeDtypeStruct((rows, 256), F32)],
        in_specs=[ANY] * (len(lefts) + len(rights)) + [VM] * len(smalls),
        out_specs=[ANY] * len(outs) + [VM],
        scratch_shapes=[
            pltpu.VMEM((5, rows, 1024), BF),
            pltpu.VMEM((5, rows, 1024), BF),
            pltpu.VMEM((rows, 1024), F32),
            dma((5,)),
            dma((5,)),
        ]
        + reducer_buffers(units),
        compiler_params=pltpu.CompilerParams(
            collective_id=1, has_side_effects=True, vmem_limit_bytes=60 << 20
        ),
        name="reduce_grads",
    )(*lefts, *rights, *smalls)
    found, summed = (list(before) + list(found[:-1]), found[-1])
    return widened([w.reshape(-1, w.shape[-1]) for w in found]), summed


def widen_kernel(*refs):
    count = len(refs) // 2
    for i in range(count):
        refs[count + i][...] = refs[i][...].astype(F32)


def widened(arrays):
    specs = [pl.BlockSpec((a.shape[0] // 8, a.shape[1]), lambda i: (i, 0)) for a in arrays]
    return pl.pallas_call(
        widen_kernel,
        out_shape=[jax.ShapeDtypeStruct(a.shape, F32) for a in arrays],
        grid=(8,),
        in_specs=specs,
        out_specs=specs,
        compiler_params=pltpu.CompilerParams(vmem_limit_bytes=60 << 20),
        name="widen_sums",
    )(*arrays)


def reduce_plain(pairs, small):
    small = pack_sums(small, lax.axis_size("shard"))
    grads = []
    for left, right in pairs:
        full = lax.dot_general(left, right, (((0,), (0,)), ((), ())), preferred_element_type=F32)
        part = lax.psum_scatter(full.astype(BF), "shard", scatter_dimension=0, tiled=True)
        grads.append(lax.psum(part, "rep").astype(F32))
    summed = lax.psum(small.astype(BF), ("rep", "shard")).astype(F32)
    width = small.shape[1] // lax.axis_size("shard")
    return grads, lax.dynamic_slice_in_dim(summed, lax.axis_index("shard") * width, width, 1)


def greet(n, more=()):
    rep = lax.axis_index("rep")
    others = [jnp.bitwise_xor(rep, d) for d in range(1, n)]
    barrier = pltpu.get_barrier_semaphore()
    for other in others:
        pl.semaphore_signal(barrier, inc=1, device_id={"rep": other}, device_id_type=MESH)
    for other in more:
        pl.semaphore_signal(barrier, inc=1, device_id=other, device_id_type=MESH)
    pl.semaphore_wait(barrier, n - 1 + len(more))
    return rep, others


def send_all(others, src_of, dst, ssem, rsem):
    copies = []
    for d, other in enumerate(others):
        copy = pltpu.make_async_remote_copy(
            src_ref=src_of(other),
            dst_ref=dst,
            send_sem=ssem.at[d],
            recv_sem=rsem.at[d],
            device_id={"rep": other},
            device_id_type=MESH,
        )
        copy.start()
        copies.append(copy)
    return copies


def to_heads(arrays, n):
    batch, local, features = arrays[0].shape
    parts = [a.reshape(batch, local, n, features // n) for a in arrays]
    stacked = jnp.stack([jnp.transpose(p, (2, 0, 1, 3)) for p in parts], axis=1)
    return stacked


def from_heads(swapped):
    if swapped.ndim == 4:
        k, batch, local, features = swapped.shape
        return [swapped[i].reshape(batch * local, features) for i in range(k)]
    n, k, batch, local, width = swapped.shape
    return [
        jnp.transpose(swapped[:, i], (1, 2, 0, 3)).reshape(batch * local, n * width)
        for i in range(k)
    ]


def head_mask(shape, head):
    lane = lax.broadcasted_iota(jnp.int32, shape, 1)
    return jnp.logical_and(lane >= head * HD, lane < (head + 1) * HD)


def spread_bias(bias, spread, block):
    wide = bias.shape[1]
    lane = lax.broadcasted_iota(jnp.int32, (128, wide), 1)
    bias[...] = jnp.where(lane < (block + 1) * 128, spread[:, 0:1], spread[:, 383:384])
    rolled = pltpu.roll(spread, 0, 1, stride=1, stride_axis=0)
    bias[:, pl.ds(pl.multiple_of(block * 128, 128), 384)] = rolled[:, 0:384]


def features_of(out_ref, rep, width):
    if width % 128:
        return None
    return pl.ds(pl.multiple_of(rep * width, width), width)


def forward_kernel(
    x_ref, table_ref, heads_ref, mixed_ref, lse_ref, out_ref, bias, low, ssem, rsem, tsem, usem
):
    batch, _, n, local, width = heads_ref.shape
    total = n * local
    rep, others = greet(n)
    arriving, leaving = ([], [])
    for b in range(batch):
        arriving.append(
            send_all(
                others,
                lambda other: x_ref.at[other, :, b],
                heads_ref.at[b, :, rep],
                ssem.at[b],
                rsem.at[b],
            )
        )
    for b in range(batch):
        for part in range(3):
            heads_ref[b, part, rep] = x_ref[rep, part, b]
    for b in range(batch):
        for copy in arriving[b]:
            copy.wait_recv()

        def one_block(block, carry):
            keys = heads_ref[b, 1].reshape(total, width)
            values = heads_ref[b, 2].reshape(total, width)
            query = heads_ref[b, 0, block] * jnp.asarray(0.125, BF)
            mixed, logsum = (None, None)
            for head in range(width // HD):
                mask = head_mask((128, width), head)
                part = jnp.where(mask, query, jnp.zeros_like(query))
                spread = lax.dot_general(
                    part, table_ref[...], (((1,), (1,)), ((), ())), preferred_element_type=F32
                )
                spread_bias(bias, spread.astype(BF).astype(F32), block)
                scores = lax.dot_general(
                    part, keys, (((1,), (1,)), ((), ())), preferred_element_type=F32
                )
                scores = scores + bias[:, 128 : 128 + total]
                top = jnp.max(scores, axis=1, keepdims=True)
                weight = jnp.exp(scores - top)
                summed = jnp.sum(weight, axis=1, keepdims=True)
                one = jnp.dot(weight.astype(BF), values, preferred_element_type=F32) / summed
                own = jnp.broadcast_to(top + jnp.log(summed), (128, width))
                mixed = one if mixed is None else jnp.where(mask, one, mixed)
                logsum = own if logsum is None else jnp.where(mask, own, logsum)
            mixed_ref[b, block] = mixed
            lse_ref[b, block] = logsum
            low[b, block] = mixed.astype(BF)
            return carry

        lax.fori_loop(0, n, one_block, 0)
        place = features_of(out_ref, rep, width)
        target = out_ref.at[rep, 0, b] if place is None else out_ref.at[0, b, :, place]
        leaving.append(
            send_all(others, lambda other: low.at[b, other], target, tsem.at[b], usem.at[b])
        )
        target[...] = low[b, rep]
    for copies in arriving:
        for copy in copies:
            copy.wait_send()
    for copies in leaving:
        for copy in copies:
            copy.wait()


def sent_shape(count, n, batch, local, width):
    if width % 128:
        return (n, count, batch, local, width)
    return (count, batch, local, n * width)


def attention_forward(stacked, table):
    n, _, batch, local, width = stacked.shape
    shape = jax.ShapeDtypeStruct((batch, n, local, width), F32)
    dma = pltpu.SemaphoreType.DMA
    return pl.pallas_call(
        forward_kernel,
        out_shape=[
            jax.ShapeDtypeStruct((batch, 3, n, local, width), BF),
            shape,
            shape,
            jax.ShapeDtypeStruct(sent_shape(1, n, batch, local, width), BF),
        ],
        in_specs=[VM, VM],
        out_specs=[VM] * 4,
        scratch_shapes=[
            pltpu.VMEM((128, n * local + 256), F32),
            pltpu.VMEM((batch, n, local, width), BF),
        ]
        + [dma((batch, n - 1))] * 4,
        compiler_params=pltpu.CompilerParams(
            collective_id=2, has_side_effects=True, vmem_limit_bytes=40 << 20
        ),
        name="attention_forward",
    )(stacked, table)


def backward_kernel(plan, *refs):
    x_ref, heads_ref, table_ref, mixed_ref, lse_ref = refs[:5]
    refs = refs[5:]
    batch, _, n, local, width = heads_ref.shape
    total = n * local
    if plan is None:
        out_ref, dtable_ref = refs[:2]
        refs = refs[2:]
        rep, others = greet(n)
    else:
        n_left, n_right, groups, units = plan
        lefts, rights = (refs[:n_left], refs[n_left : n_left + n_right])
        refs = refs[n_left + n_right :]
        out_ref, dtable_ref = refs[:2]
        outs = refs[2 : 2 + len(groups)]
        refs = refs[2 + len(groups) :]
        begin, step, finish = reducer(
            groups, units, lefts, rights, outs, refs[12:], BESIDE_LAG
        )
        begin()
        peers = here()[-1]
        rep, others = greet(n, (peers["z0"], peers["z1"]))
    grads, low, bias, keyx, dscore, prob, dkt, dvt, ssem, rsem, tsem, usem = refs[:12]
    arriving, leaving = ([], [])
    for b in range(batch):
        arriving.append(
            send_all(
                others,
                lambda other: x_ref.at[other, 0, b],
                grads.at[b, rep],
                ssem.at[b],
                rsem.at[b],
            )
        )
    dtable_ref[...] = jnp.zeros_like(dtable_ref)
    dscore[:, 0:128] = jnp.zeros((128, 128), BF)
    dscore[:, 128 + total : 256 + total] = jnp.zeros((128, 128), BF)
    row = lax.broadcasted_iota(jnp.int32, (total, 128), 0) // 128
    lane = lax.broadcasted_iota(jnp.int32, (total, 128), 1)
    keyx[:, width : width + 128] = (row == lane).astype(BF)
    flip = (
        lax.broadcasted_iota(jnp.int32, (128, 128), 0)
        + lax.broadcasted_iota(jnp.int32, (128, 128), 1)
        == 127
    ).astype(BF)
    lane_at = lax.broadcasted_iota(jnp.int32, (128, 128), 1)
    band_at = lax.broadcasted_iota(jnp.int32, (128, BAND), 1)
    for b in range(batch):
        grads[b, rep] = x_ref[rep, 0, b]
    for b in range(batch):
        dkt[...] = jnp.zeros_like(dkt)
        dvt[...] = jnp.zeros_like(dvt)
        keyx[:, 0:width] = heads_ref[b, 1].reshape(total, width)
        for copy in arriving[b]:
            copy.wait_recv()

        def one_block(block, carry):
            keys = heads_ref[b, 1].reshape(total, width)
            values = heads_ref[b, 2].reshape(total, width)
            query = heads_ref[b, 0, block] * jnp.asarray(0.125, BF)
            grad = grads[b, block]
            weighed = grad.astype(F32) * mixed_ref[b, block]
            logsums = lse_ref[b, block]
            query_t = jnp.transpose(query.astype(F32)).astype(BF)
            grad_t = jnp.transpose(grad.astype(F32)).astype(BF)
            found = None
            for head in range(width // HD):
                mask = head_mask((128, width), head)
                lanes = slice(head * HD, (head + 1) * HD)
                part = jnp.where(mask, query, jnp.zeros_like(query))
                grad_part = jnp.where(mask, grad, jnp.zeros_like(grad))
                balance = jnp.sum(jnp.where(mask, weighed, 0.0), axis=1, keepdims=True)
                logsum = logsums[:, head * HD : head * HD + 1]
                spread = lax.dot_general(
                    part, table_ref[...], (((1,), (1,)), ((), ())), preferred_element_type=F32
                )
                spread_bias(bias, spread.astype(BF).astype(F32), block)
                scores = lax.dot_general(
                    part, keys, (((1,), (1,)), ((), ())), preferred_element_type=F32
                )
                chance = jnp.exp(scores + bias[:, 128 : 128 + total] - logsum)
                back = lax.dot_general(
                    grad_part, values, (((1,), (1,)), ((), ())), preferred_element_type=F32
                )
                prob[...] = chance.astype(BF)
                dscore[:, 128 : 128 + total] = (chance * (back - balance)).astype(BF)
                score_back = dscore[:, 128 : 128 + total]
                dkt[lanes, :] += jnp.dot(
                    query_t[lanes, :], score_back, preferred_element_type=F32
                )
                dvt[lanes, :] += jnp.dot(grad_t[lanes, :], prob[...], preferred_element_type=F32)
                wide = jnp.dot(score_back, keyx[...], preferred_element_type=F32)
                sums = wide[:, width : width + 128]
                before = jnp.sum(jnp.where(lane_at < block - 1, sums, 0.0), axis=1, keepdims=True)
                after = jnp.sum(jnp.where(lane_at > block + 1, sums, 0.0), axis=1, keepdims=True)
                near = dscore[:, pl.ds(pl.multiple_of(block * 128, 128), 384)]
                near = jnp.dot(flip, near, preferred_element_type=F32)
                near = jnp.concatenate([near, jnp.zeros((128, BAND - 384), F32)], axis=1)
                near = pltpu.roll(near, BAND - 127, 1, stride=1, stride_axis=0)
                near = jnp.dot(flip, near.astype(BF), preferred_element_type=F32)
                near = near + jnp.where(band_at == 0, before, 0.0)
                near = (near + jnp.where(band_at == 383, after, 0.0)).astype(BF)
                query_back = wide[:, 0:width] + jnp.dot(
                    near, table_ref[...], preferred_element_type=F32
                )
                dtable_ref[...] += lax.dot_general(
                    near, part, (((0,), (0,)), ((), ())), preferred_element_type=F32
                )
                found = query_back if found is None else jnp.where(mask, query_back, found)
            low[b, 0, block] = (found * 0.125).astype(BF)
            if plan is not None:
                step(b * n + block)
            return carry

        lax.fori_loop(0, n, one_block, 0)
        low[b, 1] = jnp.transpose(dkt[...]).astype(BF).reshape(n, local, width)
        low[b, 2] = jnp.transpose(dvt[...]).astype(BF).reshape(n, local, width)
        place = features_of(out_ref, rep, width)
        target = out_ref.at[rep, :, b] if place is None else out_ref.at[:, b, :, place]
        leaving.append(
            send_all(others, lambda other: low.at[b, :, other], target, tsem.at[b], usem.at[b])
        )
        for part in range(3):
            target[part] = low[b, part, rep]
    for copies in arriving:
        for copy in copies:
            copy.wait_send()
    for copies in leaving:
        for copy in copies:
            copy.wait()
    if plan is not None:

        def rest(i, carry):
            step(i)
            return carry

        lax.fori_loop(batch * n, max(batch * n, units + BESIDE_LAG[-1]), rest, 0)
        finish()


def attention_backward(stacked, heads, table, mixed, logsum, pairs):
    batch, _, n, local, width = heads.shape
    total = n * local
    dma = pltpu.SemaphoreType.DMA
    plan, lefts, rights, outs, buffers = (None, [], [], [], [])
    if pairs:
        lefts, rights, groups, units, outs = reducer_plan(pairs)
        plan = (len(lefts), len(rights), groups, units)
        buffers = reducer_buffers(units)
    found = pl.pallas_call(
        functools.partial(backward_kernel, plan),
        out_shape=[
            jax.ShapeDtypeStruct(sent_shape(3, n, batch, local, width), BF),
            jax.ShapeDtypeStruct(table.shape, F32),
        ]
        + outs,
        in_specs=[VM] * 5 + [ANY] * (len(lefts) + len(rights)),
        out_specs=[VM] * 2 + [ANY] * len(outs),
        scratch_shapes=[
            pltpu.VMEM((batch, n, local, width), BF),
            pltpu.VMEM((batch, 3, n, local, width), BF),
            pltpu.VMEM((128, total + 256), F32),
            pltpu.VMEM((total, width + 128), BF),
            pltpu.VMEM((128, total + 256), BF),
            pltpu.VMEM((128, total), BF),
            pltpu.VMEM((width, total), F32),
            pltpu.VMEM((width, total), F32),
        ]
        + [dma((batch, n - 1))] * 4
        + buffers,
        compiler_params=pltpu.CompilerParams(
            collective_id=3, has_side_effects=True, vmem_limit_bytes=48 << 20
        ),
        name="attention_backward",
    )(stacked, heads, table, mixed, logsum, *lefts, *rights)
    return found[0], found[1], list(found[2:])


def shifted(value, axis, steps):
    count = lax.axis_size(axis)
    leading, last = (max(0, -steps), min(count, count - steps))
    return lax.ppermute(value, axis, [(source, source + steps) for source in range(leading, last)])


def statistics(values):
    centre = jnp.mean(values, axis=-1, keepdims=True)
    centred = values - centre
    spread = jnp.mean(centred * centred, axis=-1, keepdims=True)
    return centre, lax.rsqrt(spread + EPSILON)


def norm(values, gain, shift):
    centre, scale = statistics(values)
    return (values - centre) * scale * gain + shift


def norm_back(values, gain, grad):
    centre, scale = statistics(values)
    hat = (values - centre) * scale
    weighed = grad * gain
    back = (
        weighed
        - jnp.mean(weighed, axis=-1, keepdims=True)
        - hat * jnp.mean(weighed * hat, axis=-1, keepdims=True)
    ) * scale
    return back, jnp.sum(grad * hat, axis=0), jnp.sum(grad, axis=0)


def swish(values):
    return values * jax.nn.sigmoid(values)


def swish_slope(values):
    gate = jax.nn.sigmoid(values)
    return gate * (1.0 + values * (1.0 - gate))


def times(left, right):
    return jnp.dot(left, right, preferred_element_type=F32)


def times_back(left, right):
    return lax.dot_general(left, right, (((1,), (1,)), ((), ())), preferred_element_type=F32)


def column_sum(values):
    return jnp.sum(values.astype(F32), axis=0)


MATRICES = (2, 4, 8, 10, 11, 13, 18, 22, 25, 27)
VECTORS = (0, 1, 5, 6, 7, 9, 12, 14, 16, 17, 20, 21, 23, 24, 28, 29, 30)
OFFSETS = (3, 26)
TABLE_AT = 15
TAPS_AT = 19


SMALLS = VECTORS + OFFSETS + (TAPS_AT, TABLE_AT)


def small_rows(shards):
    width = shards[0].shape[0]
    count = len(VECTORS) + sum(shards[i].shape[0] // width for i in OFFSETS)
    count += shards[TAPS_AT].shape[0] + shards[TABLE_AT].shape[0]
    return -(-count // 16) * 16


def pack_small(shards):
    width = shards[0].shape[0]
    rows = [shards[i].reshape(-1, width) for i in VECTORS + OFFSETS]
    rows.append(shards[TAPS_AT])
    table = shards[TABLE_AT]
    rows.append(jnp.pad(table, ((0, 0), (0, width - table.shape[1]))))
    packed = jnp.concatenate(rows, axis=0)
    return jnp.pad(packed, ((0, small_rows(shards) - packed.shape[0]), (0, 0)))


def unpack_small(gathered, shards):
    n, _, width = gathered.shape
    full = {}
    at = 0
    for i in VECTORS:
        full[i] = gathered[:, at].reshape(n * width).astype(F32)
        at += 1
    for i in OFFSETS:
        count = shards[i].shape[0] // width
        full[i] = gathered[:, at : at + count].reshape(n * width * count).astype(F32)
        at += count
    count = shards[TAPS_AT].shape[0]
    full[TAPS_AT] = jnp.transpose(gathered[:, at : at + count], (1, 0, 2)).reshape(count, -1)
    at += count
    rows, cols = shards[TABLE_AT].shape
    table = gathered[:, at : at + rows, :cols]
    full[TABLE_AT] = jnp.transpose(table, (1, 0, 2)).reshape(rows, n * cols)
    return full


def list_sums(grads, n):
    table = grads[TABLE_AT]
    width = grads[0].shape[0] // n
    parts = jnp.transpose(table.reshape(table.shape[0], n, -1), (1, 0, 2)).reshape(n, -1)
    parts = jnp.pad(parts, ((0, 0), (0, -parts.shape[1] % width))).reshape(n, -1, width)
    parts = jnp.transpose(parts, (1, 0, 2)).reshape(-1, n * width)
    return [grads[i] for i in VECTORS + OFFSETS + (TAPS_AT,)] + [parts]


def pack_sums(smalls, n):
    features = smalls[0].shape[0]
    rows = []
    for a in smalls:
        if a.ndim == 1:
            a = jnp.transpose(a.reshape(n, -1, features // n), (1, 0, 2)).reshape(-1, features)
        rows.append(a)
    return jnp.concatenate(rows, axis=0)


def split_kernel(offset_rows, tap_rows, x_ref, *outs):
    width = x_ref.shape[1]
    at = 0
    for i in range(len(VECTORS)):
        outs[i][...] = x_ref[at, :]
        at += 1
    for i in range(len(OFFSETS)):
        for k in range(offset_rows):
            outs[len(VECTORS) + i][pl.ds(k * width, width)] = x_ref[at, :]
            at += 1
    outs[len(VECTORS) + len(OFFSETS)][...] = x_ref[at : at + tap_rows, :]


def split_sums(summed, shards):
    width = summed.shape[1]
    order = VECTORS + OFFSETS + (TAPS_AT,)
    offset_rows = shards[OFFSETS[0]].shape[0] // width
    tap_rows = shards[TAPS_AT].shape[0]
    if width % 128 == 0:
        parts = pl.pallas_call(
            functools.partial(split_kernel, offset_rows, tap_rows),
            out_shape=[jax.ShapeDtypeStruct(shards[i].shape, F32) for i in order],
            in_specs=[VM],
            out_specs=[VM] * len(order),
            name="split_sums",
        )(summed)
        at = sum(shards[i].size for i in order) // width
    else:
        parts, at = ([], 0)
        for i in order:
            count = shards[i].size // width
            parts.append(summed[at : at + count].reshape(shards[i].shape))
            at += count
    found = dict(zip(order, parts))
    table = shards[TABLE_AT]
    found[TABLE_AT] = summed[at:].reshape(-1)[: table.size].reshape(table.shape)
    return found


def feed_forward(entering, gain, shift, widen, offset, narrow, bias):
    normed = norm(entering, gain, shift).astype(BF)
    act = times(normed, widen) + offset
    hidden = swish(act).astype(BF)
    return entering + 0.5 * (times(hidden, narrow) + bias), (normed, act, hidden)


def feed_backward(entering, gain, widen, narrow, saved, out_grad):
    normed, act, hidden = saved
    out_low = (0.5 * out_grad).astype(BF)
    act_grad = (times_back(out_low, narrow) * swish_slope(act)).astype(BF)
    normed_grad = times_back(act_grad, widen)
    back, grad_gain, grad_shift = norm_back(entering, gain, normed_grad)
    return (
        out_grad + back,
        (grad_gain, grad_shift, column_sum(act_grad), column_sum(out_low)),
        [(hidden, out_low), (normed, act_grad)],
    )


def sigmoid(values):
    return 1.0 / (1.0 + jnp.exp(-values))


def conv_forward_kernel(doubled_ref, rim_ref, taps_ref, gain_ref, shift_ref, depth_ref, acted_ref, padded):
    local, features = (depth_ref.shape[1], depth_ref.shape[2])
    rim = rim_ref.shape[1]
    taps = taps_ref.shape[0]
    padded[32 - rim : 32, :] = rim_ref[0].astype(F32)

    def gate_rows(i, carry):
        rows = pl.ds(pl.multiple_of(i * 32, 32), 32)
        both = doubled_ref[0, rows, :]
        padded[pl.ds(pl.multiple_of(32 + i * 32, 32), 32), :] = both[:, :features] * sigmoid(
            both[:, features:]
        )
        return carry

    lax.fori_loop(0, local // 32, gate_rows, 0)

    def columns(i, carry):
        cols = pl.ds(pl.multiple_of(i * 128, 128), 128)
        first = 32 - (taps - 1)
        total = padded[first : first + local, cols] * taps_ref[0:1, cols]
        for j in range(1, taps):
            total = total + padded[first + j : first + j + local, cols] * taps_ref[j : j + 1, cols]
        depth_ref[0, :, cols] = total
        return carry

    lax.fori_loop(0, features // 128, columns, 0)

    def norm_rows(i, carry):
        rows = pl.ds(pl.multiple_of(i * 32, 32), 32)
        normed = norm(depth_ref[0, rows, :], gain_ref[...], shift_ref[...])
        acted_ref[0, rows, :] = (normed * sigmoid(normed)).astype(BF)
        return carry

    lax.fori_loop(0, local // 32, norm_rows, 0)


def block_spec(shape):
    return pl.BlockSpec((1,) + shape[1:], lambda b: (b,) + (0,) * (len(shape) - 1))


def fixed_spec(shape):
    return pl.BlockSpec(shape, lambda b: (0,) * len(shape))


def conv_forward(doubled, rim_in, taps, gain, shift):
    batch, local, features = (doubled.shape[0], doubled.shape[1], taps.shape[1])
    shape = (batch, local, features)
    return pl.pallas_call(
        conv_forward_kernel,
        out_shape=[jax.ShapeDtypeStruct(shape, F32), jax.ShapeDtypeStruct(shape, BF)],
        grid=(batch,),
        in_specs=[
            block_spec(doubled.shape),
            block_spec(rim_in.shape),
            fixed_spec(taps.shape),
            fixed_spec(gain.shape),
            fixed_spec(shift.shape),
        ],
        out_specs=[block_spec(shape), block_spec(shape)],
        scratch_shapes=[pltpu.VMEM((32 + local, features), F32)],
        compiler_params=pltpu.CompilerParams(vmem_limit_bytes=32 << 20),
        name="conv_forward",
    )(doubled, rim_in, taps, gain, shift)


def depth_backward_kernel(depth_ref, grad_ref, gain_ref, shift_ref, back_ref, sums_ref):
    local = depth_ref.shape[1]

    @pl.when(pl.program_id(0) == 0)
    def _():
        sums_ref[...] = jnp.zeros_like(sums_ref)

    def body(i, carry):
        rows = pl.ds(pl.multiple_of(i * 32, 32), 32)
        values = depth_ref[0, rows, :]
        centre, scale = statistics(values)
        hat = (values - centre) * scale
        gain = gain_ref[...]
        normed = hat * gain + shift_ref[...]
        gate = sigmoid(normed)
        grad = grad_ref[0, rows, :] * gate * (1.0 + normed * (1.0 - gate))
        weighed = grad * gain
        back_ref[0, rows, :] = (
            weighed
            - jnp.mean(weighed, axis=-1, keepdims=True)
            - hat * jnp.mean(weighed * hat, axis=-1, keepdims=True)
        ) * scale
        sums_ref[0:1, :] += jnp.sum(grad * hat, axis=0, keepdims=True)
        sums_ref[1:2, :] += jnp.sum(grad, axis=0, keepdims=True)
        return carry

    lax.fori_loop(0, local // 32, body, 0)


def depth_backward(depth, grad, gain, shift):
    return pl.pallas_call(
        depth_backward_kernel,
        out_shape=[
            jax.ShapeDtypeStruct(depth.shape, F32),
            jax.ShapeDtypeStruct((8, depth.shape[2]), F32),
        ],
        grid=(depth.shape[0],),
        in_specs=[
            block_spec(depth.shape),
            block_spec(grad.shape),
            fixed_spec(gain.shape),
            fixed_spec(shift.shape),
        ],
        out_specs=[block_spec(depth.shape), fixed_spec((8, depth.shape[2]))],
        compiler_params=pltpu.CompilerParams(vmem_limit_bytes=32 << 20),
        name="depth_backward",
    )(depth, grad, gain, shift)


def conv_backward_kernel(
    back_ref, after_ref, doubled_ref, rim_ref, taps_ref, out_ref, dtaps_ref, padded, behind
):
    local, features = (back_ref.shape[1], back_ref.shape[2])
    rim = rim_ref.shape[1]
    taps = taps_ref.shape[0]

    @pl.when(pl.program_id(0) == 0)
    def _():
        dtaps_ref[...] = jnp.zeros_like(dtaps_ref)

    padded[32 - rim : 32, :] = rim_ref[0].astype(F32)
    behind[local : local + rim, :] = after_ref[0].astype(F32)

    def gate_rows(i, carry):
        rows = pl.ds(pl.multiple_of(i * 32, 32), 32)
        both = doubled_ref[0, rows, :]
        padded[pl.ds(pl.multiple_of(32 + i * 32, 32), 32), :] = both[:, :features] * sigmoid(
            both[:, features:]
        )
        behind[rows, :] = back_ref[0, rows, :]
        return carry

    lax.fori_loop(0, local // 32, gate_rows, 0)

    def columns(i, carry):
        cols = pl.ds(pl.multiple_of(i * 128, 128), 128)
        first = 32 - (taps - 1)
        own = back_ref[0, :, cols]
        total = own * taps_ref[taps - 1 : taps, cols]
        dtaps_ref[taps - 1 : taps, cols] += jnp.sum(
            own * padded[first + taps - 1 : first + taps - 1 + local, cols], axis=0, keepdims=True
        )
        for j in range(taps - 1):
            ahead = taps - 1 - j
            total = total + behind[ahead : ahead + local, cols] * taps_ref[j : j + 1, cols]
            dtaps_ref[j : j + 1, cols] += jnp.sum(
                own * padded[first + j : first + j + local, cols], axis=0, keepdims=True
            )
        side = doubled_ref[0, :, cols]
        gate = sigmoid(doubled_ref[0, :, pl.ds(pl.multiple_of(features + i * 128, 128), 128)])
        gated = total * gate
        out_ref[0, :, cols] = gated.astype(BF)
        out_ref[0, :, pl.ds(pl.multiple_of(features + i * 128, 128), 128)] = (
            gated * side * (1.0 - gate)
        ).astype(BF)
        return carry

    lax.fori_loop(0, features // 128, columns, 0)


def conv_backward(back, after, doubled, rim_in, taps):
    batch, local, features = back.shape
    padded_taps = (-(-taps.shape[0] // 8) * 8, features)
    found, dtaps = pl.pallas_call(
        conv_backward_kernel,
        out_shape=[
            jax.ShapeDtypeStruct(doubled.shape, BF),
            jax.ShapeDtypeStruct(padded_taps, F32),
        ],
        grid=(batch,),
        in_specs=[
            block_spec(back.shape),
            block_spec(after.shape),
            block_spec(doubled.shape),
            block_spec(rim_in.shape),
            fixed_spec(taps.shape),
        ],
        out_specs=[block_spec(doubled.shape), fixed_spec(padded_taps)],
        scratch_shapes=[
            pltpu.VMEM((32 + local, features), F32),
            pltpu.VMEM((32 + local, features), F32),
        ],
        compiler_params=pltpu.CompilerParams(vmem_limit_bytes=32 << 20),
        name="conv_backward",
    )(back, after, doubled, rim_in, taps)
    return found, dtaps[: taps.shape[0]]


def on_device(*arguments):
    inputs, shards, cotangent = (arguments[0], arguments[1:32], arguments[32])
    n_rep, n_shard = (lax.axis_size("rep"), lax.axis_size("shard"))
    micro, local, seqs, features = inputs.shape
    batch = micro * seqs
    fast = (
        n_rep == 8
        and n_shard == 4
        and features == 1024
        and batch * local == 256
        and all(shards[i].shape[0] % 256 == 0 for i in MATRICES)
    )

    def rows_of(array):
        return jnp.transpose(array, (0, 2, 1, 3)).reshape(batch * local, features)

    def whole_of(rows):
        return jnp.transpose(rows.reshape(micro, seqs, local, features), (0, 2, 1, 3))

    if fast:
        smalls = [shards[i] for i in SMALLS]
        full, gathered = gather_fast([shards[i] for i in MATRICES], smalls, small_rows(shards))
    else:
        small = pack_small(shards)
        full = [lax.all_gather(shards[i], "shard", axis=0, tiled=True) for i in MATRICES]
        gathered = lax.all_gather(small, "shard", axis=0, tiled=False)
    w = dict(zip(MATRICES, full))
    w.update(unpack_small(gathered, shards))

    level0 = rows_of(inputs).astype(F32)
    level1, early = feed_forward(level0, w[0], w[1], w[2], w[3], w[4], w[5])

    attend_in = norm(level1, w[6], w[7]).astype(BF)
    query = (times(attend_in, w[8]) + w[9]).astype(BF).reshape(batch, local, features)
    keys = times(attend_in, w[10]).astype(BF).reshape(batch, local, features)
    values = (times(attend_in, w[11]) + w[12]).astype(BF).reshape(batch, local, features)
    place = jnp.clip(jnp.arange(BAND) - 64, 0, TABLE - 1)
    place = jnp.where(jnp.arange(BAND) >= 384, 0, place)
    table = w[TABLE_AT]
    spread_table = jnp.tile(jnp.take(table, place, axis=0), (1, features // n_rep // HD))
    heads, mixed_h, logsum, mixed = attention_forward(
        to_heads([query, keys, values], n_rep), spread_table
    )
    mixed = from_heads(mixed)[0]
    level2 = level1 + times(mixed, w[13]) + w[14]

    conv_in = norm(level2, w[16], w[17]).astype(BF)
    doubled = times(conv_in, w[18])
    doubled = doubled.reshape(batch, local, 2 * features)
    taps = w[TAPS_AT].astype(F32)
    rim = taps.shape[0] - 1
    edge = doubled[:, local - rim :]
    edge = (edge[:, :, :features] * jax.nn.sigmoid(edge[:, :, features:])).astype(BF)
    rim_in = shifted(edge, "rep", 1)
    depth, acted = conv_forward(doubled, rim_in, taps, w[20][None], w[21][None])
    acted = acted.reshape(batch * local, features)
    level3 = level2 + times(acted, w[22])

    level4, later = feed_forward(level3, w[23], w[24], w[25], w[26], w[27], w[28])
    output = norm(level4, w[29], w[30]).astype(BF)

    grads = {}
    incoming = rows_of(cotangent).astype(F32)
    back4, grads[29], grads[30] = norm_back(level4, w[29], incoming)
    back3, found, later_pairs = feed_backward(level3, w[23], w[25], w[27], later, back4)
    grads[23], grads[24], grads[26], grads[28] = found

    conv_out = back3.astype(BF)
    acted_grad = times_back(conv_out, w[22]).reshape(batch, local, features)
    depth_back, sums = depth_backward(depth, acted_grad, w[20][None], w[21][None])
    grads[20], grads[21] = (sums[0], sums[1])
    after = shifted(depth_back[:, :rim].astype(BF), "rep", -1)
    doubled_back, grads[TAPS_AT] = conv_backward(depth_back, after, doubled, rim_in, taps)
    doubled_back = doubled_back.reshape(batch * local, 2 * features)
    conv_back = times_back(doubled_back, w[18])
    back, grads[16], grads[17] = norm_back(level2, w[16], conv_back)
    back2 = back3 + back

    mixer_out = back2.astype(BF)
    grads[14] = column_sum(mixer_out)
    mixed_back = times_back(mixer_out, w[13]).astype(BF).reshape(batch, local, features)
    ahead = 2 if fast else 0
    pairs = [
        (27, later_pairs[0]),
        (25, later_pairs[1]),
        (22, (acted, conv_out)),
        (18, (conv_in, doubled_back)),
        (13, (mixed, mixer_out)),
    ]
    found, table_b, before = attention_backward(
        to_heads([mixed_back], n_rep),
        heads,
        spread_table,
        mixed_h,
        logsum,
        [pair for _, pair in pairs[:ahead]],
    )
    query_back, key_back, value_back = from_heads(found)
    folded = table_b.reshape(BAND, -1, HD).sum(axis=1)
    grads[TABLE_AT] = jnp.concatenate(
        [
            (folded[0:65].sum(axis=0) + folded[384:].sum(axis=0))[None],
            folded[65:136],
            folded[136:384].sum(axis=0)[None],
        ]
    )
    grads[9] = column_sum(query_back)
    grads[12] = column_sum(value_back)
    attend_back = (
        times_back(query_back, w[8]) + times_back(key_back, w[10]) + times_back(value_back, w[11])
    )
    back, grads[6], grads[7] = norm_back(level1, w[6], attend_back)
    back1 = back2 + back
    back0, found, early_pairs = feed_backward(level0, w[0], w[2], w[4], early, back1)
    grads[0], grads[1], grads[3], grads[5] = found

    pairs += [
        (8, (attend_in, query_back)),
        (10, (attend_in, key_back)),
        (11, (attend_in, value_back)),
        (4, early_pairs[0]),
        (2, early_pairs[1]),
    ]
    kept, sums = ([pair for _, pair in pairs[ahead:]], list_sums(grads, n_shard))
    if fast:
        matrices, smalls = reduce_fast(kept, sums, before)
    else:
        matrices, smalls = reduce_plain(kept, sums)
    summed = dict(zip([i for i, _ in pairs], matrices))
    summed.update(split_sums(smalls, shards))
    return (whole_of(output), whole_of(back0)) + tuple(summed[i] for i in range(31))


def solution(mesh):
    rows, vector, matrix = (P(None, "rep", "shard", None), P("shard"), P("shard", None))
    columns = P(None, "shard")
    weights = tuple(
        matrix if i in MATRICES else columns if i in (TABLE_AT, TAPS_AT) else vector
        for i in range(31)
    )
    return jax.shard_map(
        on_device,
        mesh=mesh,
        in_specs=(rows,) + weights + (rows,),
        out_specs=(rows, rows) + weights,
        check_vma=False,
    )
```
